32 devices in a mesh: dp: 4 (over y, core), seq: 8 (over z, x).
Axes of the slice: x: 2, y: 2, z: 4, core: 2. Of those that a mesh axis runs over, the one named last changes fastest.
Arguments:
- activations: bfloat16 [16, 2048, 1280], P('dp', 'seq'), may hold values from -6 to 6
- segment_ids: int32 [16, 2048], P('dp'), may hold values from 0 to 3, never falling along the last dimension, each value on 1 to 1024 neighbouring positions
- norm1_gain: bfloat16 [1280], P('dp'), may hold values from 0.25 to 1.75
- w_qkv: bfloat16 [1280, 16, 3, 80], P('dp'), may hold values from -0.15625 to 0.15625
- per_dim_scale: float32 [80], replicated, may hold values from -1 to 1
- w_out: bfloat16 [1280, 1280], P('dp'), may hold values from -0.625 to 0.625
- norm2_gain: bfloat16 [1280], P('dp'), may hold values from 0.25 to 1.75
- w_up: bfloat16 [1280, 1280], P('dp'), may hold values from -0.15625 to 0.15625
- b_up: bfloat16 [1280], P('dp'), may hold values from -3 to 3
- w_down: bfloat16 [1280, 1280], P('dp'), may hold values from -0.15625 to 0.15625
- b_down: bfloat16 [1280], P('dp'), may hold values from -2 to 2
- cotangent: float32 [16, 2048, 1280], P('dp', 'seq'), may hold values from -6 to 6
Outputs:
- layer_out: bfloat16 [16, 2048, 1280], P('dp', 'seq')
- input_grad: float32 [16, 2048, 1280], P('dp', 'seq')
- grad_norm1_gain: float32 [1280], P('dp')
- grad_w_qkv: float32 [1280, 16, 3, 80], P('dp')
- grad_per_dim_scale: float32 [80], replicated
- grad_w_out: float32 [1280, 1280], P('dp')
- grad_norm2_gain: float32 [1280], P('dp')
- grad_w_up: float32 [1280, 1280], P('dp')
- grad_b_up: float32 [1280], P('dp')
- grad_w_down: float32 [1280, 1280], P('dp')
- grad_b_down: float32 [1280], P('dp')
The draws below stay inside these ranges and needn't reach their ends.
Inputs may be any that keep to these rules, and one draw needn't show every extreme that they name: `segment_ids`: ids never fall along a sequence, and every id from 0 to 3 occurs in each sequence.
All inputs are finite; a program needn't handle non-finite values.
Results may differ from the reference program's by a relative error of at most 0.028.
Values may be sent and summed in bfloat16 or wider, within the bound.
No kernel may reach another device: no remote copies, remote signals or barrier semaphores. Data moves between devices by JAX's collectives and lax.ppermute only.
A program may use at most 320 MiB of HBM per device.

```python
import math
import jax
import jax.numpy as jnp
import numpy as np
from jax import lax

D = 1280
HEADS = 16
HEAD = 80
FF = 1280
L = 2048
DOCS = 4
SEQS = 16


def level_of(stream_key, shape, cuts, least, high):
    loudness = 1.0
    for dim, shards_of in cuts:
        steps = jax.random.uniform(jax.random.fold_in(jax.random.fold_in(stream_key, 6), dim), (shards_of,), jnp.float32, least / len(cuts), high / len(cuts))
        loudness = loudness * jnp.repeat(jnp.exp(steps), shape[dim] // shards_of).reshape((-1,) + (1,) * (len(shape) - 1 - dim))
    return loudness


def profile(number_of, total, limit, lean):
    loads = [(1 << 20) // math.isqrt(grade ** lean) + 1 for grade in range(2, number_of + 1)]
    rest, holding = total - limit - (number_of - 1), [1] * (number_of - 1)
    while rest > 0:
        free = [i for i in range(number_of - 1) if holding[i] < limit]
        pool, left = sum([loads[i] for i in free]), rest
        for i in free:
            extra = min(limit - holding[i], max(1, left * loads[i] // pool), rest)
            holding[i] = holding[i] + extra
            rest = rest - extra
    return np.array([limit] + holding)


def ragged_sizes(own_key, amount, total, most, slope):
    if amount == 2:
        one = jax.random.randint(own_key, (), max(1, total - most), min(most, total - 1) + 1)
        return jnp.stack([one, total - one])
    tallies = jnp.asarray(profile(amount, total, most, slope), jnp.int32)
    twos = (amount - 1) // 2
    donor, sink = tallies[1:1 + 2 * twos:2], tallies[2:2 + 2 * twos:2]
    slack = jnp.minimum(donor - 1, most - sink)
    passed = jax.random.randint(jax.random.fold_in(own_key, 1), (twos,), 0, 1 << 20) % (slack + 1)
    tallies = tallies.at[1:1 + 2 * twos:2].set(donor - passed).at[2:2 + 2 * twos:2].set(sink + passed)
    return tallies[jax.random.permutation(jax.random.fold_in(own_key, 2), amount)]


def scatter_about(rng, shape, scale, reach, split=(), kind=jnp.bfloat16):
    level = level_of(rng, shape, split, -0.22, 0.18) if split else 1.0
    values = jax.random.normal(rng, shape, jnp.float32) * scale * level
    return jnp.minimum(jnp.maximum(values, -reach), reach).astype(kind)


def setup_inputs(seed: int = 0) -> dict:
    arg_keys = jax.random.split(jax.random.key(seed), 13)
    activations = scatter_about(arg_keys[0], (SEQS, L, D), 1.0, 6.0, ((0, 4), (1, 8)))
    segment_ids = jax.vmap(lambda own: jnp.searchsorted(jnp.cumsum(ragged_sizes(own, DOCS, L, L // 2, 2)), jnp.arange(L), side="right"))(jax.random.split(arg_keys[1], SEQS)).reshape((SEQS, L)).astype(jnp.int32)
    norm1_gain = jnp.clip(1.0 + 0.15 * jax.random.normal(arg_keys[2], (D,), jnp.float32), 0.25, 1.75).astype(jnp.bfloat16)
    w_qkv = scatter_about(arg_keys[3], (D, HEADS, 3, HEAD), D ** -0.5, 0.15625, ((0, 4),))
    per_dim_scale = jnp.clip(jax.random.uniform(arg_keys[4], (HEAD,), jnp.float32, -1.0, 1.0), -1.0, 1.0)
    w_out = scatter_about(arg_keys[5], (D, D), (D // 16) ** -0.5, 0.625, ((0, 4),))
    norm2_gain = jnp.clip(1.0 + 0.15 * jax.random.normal(arg_keys[6], (D,), jnp.float32), 0.25, 1.75).astype(jnp.bfloat16)
    w_up = scatter_about(arg_keys[7], (D, FF), D ** -0.5, 0.15625, ((0, 4),))
    b_up = scatter_about(arg_keys[8], (FF,), 0.5, 3.0, ((0, 4),))
    w_down = scatter_about(arg_keys[9], (FF, D), FF ** -0.5, 0.15625, ((0, 4),))
    b_down = scatter_about(arg_keys[10], (D,), 0.3, 2.0, ((0, 4),))
    cotangent = scatter_about(arg_keys[11], (SEQS, L, D), 1.0, 6.0, ((0, 4), (1, 8)), jnp.float32)
    return dict(activations=activations, segment_ids=segment_ids, norm1_gain=norm1_gain, w_qkv=w_qkv, per_dim_scale=per_dim_scale, w_out=w_out, norm2_gain=norm2_gain, w_up=w_up, b_up=b_up, w_down=w_down, b_down=b_down, cotangent=cotangent)


epsilon = 1e-06
scale_base = 1.442695041
masked_value = -1e+30
highest = lax.Precision.HIGHEST

@jax.custom_vjp
def low(v):
    return lax.optimization_barrier(v.astype(jnp.bfloat16)).astype(jnp.float32)

@jax.custom_vjp
def low_back(v):
    return v

def low_keep(v):
    return (low(v), None)

def low_pass(kept, grad):
    return (grad,)

def back_keep(v):
    return (v, None)

def back_low(kept, grad):
    return (low(grad),)
low.defvjp(low_keep, low_pass)
low_back.defvjp(back_keep, back_low)

def attend(queries, keys, values_in, segs):
    length = queries.shape[0]
    places = jnp.arange(length)
    visible_mask = (places[None, :] <= places[:, None]) & (segs[None, :] == segs[:, None])
    scores = low_back(jnp.einsum('qhe,khe->hqk', queries, keys, precision=highest))
    scores = jnp.where(visible_mask[None], scores, masked_value)
    attention_weights = jax.nn.softmax(scores, axis=-1)
    return jnp.einsum('hqk,khe->qhe', low(attention_weights), values_in, precision=highest)

def layer(tokens, segs, norm_in, w_qkv, per_dim_scale, w_out, norm_mid, w_up, b_up, w_down, b_down):
    length = tokens.shape[0]
    heads = w_qkv.shape[1]
    head_size = w_qkv.shape[3]
    rms_in = lax.rsqrt(lax.optimization_barrier(jnp.mean(tokens * tokens, axis=-1, keepdims=True)) + epsilon)
    normed_in = low(tokens * rms_in * norm_in)
    projected = low_back(jnp.einsum('td,dhce->thce', normed_in, w_qkv, precision=highest))
    factor = scale_base / math.sqrt(head_size) * jax.nn.softplus(per_dim_scale)
    queries = low_back(low(projected[:, :, 0, :] * factor))
    keys = low_back(low(projected[:, :, 1, :]))
    values_in = low_back(low(projected[:, :, 2, :]))
    attended = jax.checkpoint(attend)(queries, keys, values_in, segs)
    attended = low_back(low(attended)).reshape(length, heads * head_size)
    branch = low_back(jnp.dot(attended, w_out, precision=highest))
    mid = tokens + branch
    rms_mid = lax.rsqrt(lax.optimization_barrier(jnp.mean(mid * mid, axis=-1, keepdims=True)) + epsilon)
    normed_mid = low(mid * rms_mid * norm_mid)
    pre_act = low_back(jnp.dot(normed_mid, w_up, precision=highest) + b_up)
    activated = low(jax.nn.silu(pre_act))
    return mid + low_back(jnp.dot(activated, w_down, precision=highest) + b_down)

def reference(activations, segment_ids, norm1_gain, w_qkv, per_dim_scale, w_out, norm2_gain, w_up, b_up, w_down, b_down, cotangent):
    params = (norm1_gain.astype(jnp.float32), w_qkv.astype(jnp.float32), per_dim_scale.astype(jnp.float32), w_out.astype(jnp.float32), norm2_gain.astype(jnp.float32), w_up.astype(jnp.float32), b_up.astype(jnp.float32), w_down.astype(jnp.float32), b_down.astype(jnp.float32))

    def one_sequence(totals, sequence_item):
        tokens, segs, grad_out = sequence_item

        def run(tokens_in, *weights):
            return layer(tokens_in, segs, *weights)
        result, pull = jax.vjp(run, tokens.astype(jnp.float32), *params)
        grads = pull(grad_out.astype(jnp.float32))
        totals = tuple((total + piece for total, piece in zip(totals, grads[1:])))
        return (totals, (result.astype(jnp.bfloat16), grads[0]))
    zeros = tuple((jnp.zeros_like(weight) for weight in params))
    totals, (outputs, input_grads) = lax.scan(one_sequence, zeros, (activations, segment_ids, cotangent))
    return (outputs, input_grads, totals[0], totals[1], totals[2], totals[3], totals[4], totals[5], totals[6], totals[7], totals[8])
```

```python
import functools
import math

import jax
import jax.numpy as jnp
from jax import lax
from jax.experimental import pallas as pl
from jax.experimental.pallas import tpu as pltpu
from jax.sharding import PartitionSpec as P

epsilon = 1e-06
scale_base = 1.442695041
log2e = 1.4426950408889634
masked_value = -1e30
score_limit = 100.0
bf16 = jnp.bfloat16
f32 = jnp.float32
axes = ("dp", "seq")
nt = (((1,), (1,)), ((), ()))
nn = (((1,), (0,)), ((), ()))


def mm(a, b, dims=nn):
    return lax.dot_general(a, b, dims, preferred_element_type=f32)


class Team:
    def __init__(self, dp, seq, seqs):
        self.dp, self.seq, self.seqs = dp, seq, seqs
        self.size = seq // seqs
        assert seq % seqs == 0 and self.size % 2 == 0 and dp % 2 == 0
        self.half = self.size // 2
        self.rows = dp // 2

    def places(self):
        for row in range(self.rows):
            for core in range(2):
                for place in range(self.seq):
                    yield row, core, place

    def rank(self, row, core, place):
        return (row * 2 + core) * self.seq + place

    def here(self):
        d = lax.axis_index("dp")
        p = lax.axis_index("seq")
        row, core = d // 2, d % 2
        group = p // self.size
        side = (p % self.size) // self.half
        member = (p % self.half) * 2 + core
        return row, core, group, side, member

    def spread(self, step):
        pairs = []
        for row, core, place in self.places():
            z, u = place // self.size, place % self.size
            s = (z + step) % self.seqs
            pairs.append(
                (
                    self.rank(row, core, place),
                    self.rank(row, u % 2, s * self.size + core * self.half + u // 2),
                )
            )
        return pairs

    def back(self, step):
        return [(b, a) for a, b in self.spread(step)]

    def rotate(self, step):
        pairs = []
        for row, core, place in self.places():
            base = place - place % self.half
            m = (place % self.half) * 2 + core
            to = (m + step) % self.size
            pairs.append((self.rank(row, core, place), self.rank(row, to % 2, base + to // 2)))
        return pairs

    def swap_core(self):
        return [(d, d ^ 1) for d in range(self.dp)]

    def turn_rows(self, step):
        return [(d, (d + 2 * step) % self.dp) for d in range(self.dp)]


def place_in(pieces, count):
    first = pieces[0][0]
    out = jnp.zeros((count,) + first.shape, first.dtype)
    for piece, index in pieces:
        out = lax.dynamic_update_index_in_dim(out, piece, index, 0)
    return out


def gather_dp(team, shard, row, core):
    mine = [(shard, row)]
    for step in range(1, team.rows):
        got = lax.ppermute(shard, "dp", team.turn_rows(step))
        mine.append((got, (row - step) % team.rows))
    mine = place_in(mine, team.rows)
    theirs = lax.ppermute(mine, "dp", team.swap_core())
    first = jnp.where(core == 0, mine, theirs)
    second = jnp.where(core == 0, theirs, mine)
    return jnp.stack([first, second], axis=1).reshape((team.dp,) + shard.shape)


def qkv_kernel(head_size, x_ref, gain_ref, w_ref, factor_ref, out_ref, normed_ref):
    x = x_ref[...].astype(f32)
    rms = lax.rsqrt(jnp.mean(x * x, axis=-1, keepdims=True) + epsilon)
    normed = (x * rms * gain_ref[...]).astype(bf16)
    normed_ref[...] = normed
    packed = (mm(normed, w_ref[...]) * factor_ref[...]).astype(bf16)
    for i in range(packed.shape[1] // head_size):
        out_ref[i // 3, i % 3] = packed[:, i * head_size : (i + 1) * head_size]


def project_qkv(x, gain, w, factor_row, heads, head_size, block):
    tokens, width = x.shape
    wide = w.shape[1]
    return pl.pallas_call(
        functools.partial(qkv_kernel, head_size),
        grid=(tokens // block,),
        in_specs=[
            pl.BlockSpec((block, width), lambda i: (i, 0)),
            pl.BlockSpec((1, width), lambda i: (0, 0)),
            pl.BlockSpec((width, wide), lambda i: (0, 0)),
            pl.BlockSpec((1, wide), lambda i: (0, 0)),
        ],
        out_specs=[
            pl.BlockSpec((heads, 3, block, head_size), lambda i: (0, 0, i, 0)),
            pl.BlockSpec((block, width), lambda i: (i, 0)),
        ],
        out_shape=[
            jax.ShapeDtypeStruct((heads, 3, tokens, head_size), bf16),
            jax.ShapeDtypeStruct((tokens, width), bf16),
        ],
        compiler_params=pltpu.CompilerParams(vmem_limit_bytes=56 << 20),
        cost_estimate=pl.CostEstimate(
            flops=2 * tokens * width * wide,
            bytes_accessed=tokens * width * 4 + width * wide * 2 + tokens * wide * 4,
            transcendentals=0,
        ),
        name="qkv",
    )(x, gain, w, factor_row)


def eye_rows(rows, columns):
    a = lax.broadcasted_iota(jnp.int32, (rows, columns), 0)
    b = lax.broadcasted_iota(jnp.int32, (rows, columns), 1)
    return (a == b).astype(bf16)


def attend_kernel(count, block, pair, table, qkv_ref, start_ref, att_ref, lse_ref, vt_ref, acc_ref):
    size = qkv_ref.shape[3]
    rows = vt_ref.shape[1]
    unit = eye_rows(rows, size)
    one_row = (lax.broadcasted_iota(jnp.int32, (rows, block), 0) == size).astype(f32)
    for h in range(pair):
        for b in range(count):
            here = slice(b * block, (b + 1) * block)
            vt_ref[h, :, here] = (mm(unit, qkv_ref[h, 2, here, :], nt) + one_row).astype(bf16)
    key_index = lax.broadcasted_iota(jnp.int32, (block, block), 0)
    lane_index = lax.broadcasted_iota(jnp.int32, (1, block), 1)
    ones = jnp.ones((8, size), bf16)

    def longest(part):
        best = jnp.zeros((8, block), f32)
        for h in range(pair):
            for b in range(count):
                x = qkv_ref[h, part, b * block : (b + 1) * block, :]
                best = jnp.maximum(best, mm(ones, x * x, nt))
        return jnp.max(best)

    small = longest(0) * longest(1) * 1.1 < score_limit * score_limit

    def query_block(raised, i, carry):
        at = pl.multiple_of(table[0, i] * block, block)
        starts = start_ref[pl.ds(i, 1), :]
        places = lane_index + i * block
        queries = [qkv_ref[h, 0, pl.ds(at, block), :] for h in range(pair)]
        acc_ref[...] = jnp.zeros_like(acc_ref)

        def step(masked, j, peaks):
            key_at = pl.multiple_of(table[0, j] * block, block)
            if masked:
                keys_here = key_index + j * block
                seen = (keys_here >= starts) & (keys_here <= places)
            out = []
            for h in range(pair):
                s = mm(qkv_ref[h, 1, pl.ds(key_at, block), :], queries[h], nt)
                if masked:
                    s = jnp.where(seen, s, masked_value)
                values = vt_ref[h, :, pl.ds(key_at, block)]
                if raised:
                    peak = jnp.maximum(peaks[h], jnp.max(s, axis=0, keepdims=True))
                    p = jnp.exp2(s - peak).astype(bf16)
                    acc_ref[h] = acc_ref[h] * jnp.exp2(peaks[h] - peak) + mm(values, p)
                    out.append(peak)
                else:
                    acc_ref[h] += mm(values, jnp.exp2(s).astype(bf16))
            return tuple(out)

        peaks = ()
        if raised:
            peaks = tuple(jnp.full((1, block), masked_value, f32) for _ in range(pair))
        peaks = lax.fori_loop(table[1, i], table[2, i], functools.partial(step, True), peaks)
        peaks = lax.fori_loop(table[2, i], i, functools.partial(step, False), peaks)
        peaks = step(True, i, peaks)
        for h in range(pair):
            total = acc_ref[h, size : size + 1, :]
            att_ref[h * size : (h + 1) * size, pl.ds(at, block)] = (
                acc_ref[h, :size, :] / total
            ).astype(bf16)
            low = jnp.log2(total)
            lse_ref[h, :, pl.ds(at, block)] = peaks[h] + low if raised else low
        return carry

    @pl.when(small)
    def plain():
        lax.fori_loop(0, count, functools.partial(query_block, False), 0)

    @pl.when(jnp.logical_not(small))
    def careful():
        lax.fori_loop(0, count, functools.partial(query_block, True), 0)


def attend(table, qkv, starts, pair=2):
    heads, _, length, size = qkv.shape
    count, block = starts.shape
    rows = (size // 16 + 1) * 16
    return pl.pallas_call(
        functools.partial(attend_kernel, count, block, pair),
        grid_spec=pltpu.PrefetchScalarGridSpec(
            num_scalar_prefetch=1,
            grid=(heads // pair,),
            in_specs=[
                pl.BlockSpec((pair, 3, length, size), lambda g, t: (g, 0, 0, 0)),
                pl.BlockSpec((count, block), lambda g, t: (0, 0)),
            ],
            out_specs=[
                pl.BlockSpec((pair * size, length), lambda g, t: (g, 0)),
                pl.BlockSpec((pair, 1, length), lambda g, t: (g, 0, 0)),
            ],
            scratch_shapes=[
                pltpu.VMEM((pair, rows, length), bf16),
                pltpu.VMEM((pair, rows, block), f32),
            ],
        ),
        out_shape=[
            jax.ShapeDtypeStruct((heads * size, length), bf16),
            jax.ShapeDtypeStruct((heads, 1, length), f32),
        ],
        compiler_params=pltpu.CompilerParams(vmem_limit_bytes=56 << 20),
        cost_estimate=pl.CostEstimate(
            flops=heads * length * length * size * 2,
            bytes_accessed=heads * length * size * 10,
            transcendentals=heads * length * length // 4,
        ),
        name="attend",
    )(table, qkv, starts)


def attend_back_kernel(
    count,
    block,
    pair,
    table,
    qkv_ref,
    att_ref,
    grad_ref,
    lse_ref,
    start_ref,
    factor_ref,
    out_ref,
    dots_ref,
    qt_ref,
    kt_ref,
    delta_ref,
    dq_ref,
    dk_ref,
    dv_ref,
):
    size = qkv_ref.shape[3]
    unit = eye_rows(size, size)
    for h in range(pair):
        for b in range(count):
            here = slice(b * block, (b + 1) * block)
            qt_ref[h, :, here] = mm(unit, qkv_ref[h, 0, here, :], nt).astype(bf16)
            kt_ref[h, :, here] = mm(unit, qkv_ref[h, 1, here, :], nt).astype(bf16)
        rows = slice(h * size, (h + 1) * size)
        delta_ref[h] = jnp.sum(
            att_ref[rows, :].astype(f32) * grad_ref[rows, :].astype(f32), axis=0, keepdims=True
        )
    dq_ref[...] = jnp.zeros_like(dq_ref)
    key_index = lax.broadcasted_iota(jnp.int32, (block, block), 0)
    lane_index = lax.broadcasted_iota(jnp.int32, (1, block), 1)

    def key_block(j, carry):
        key_at = pl.multiple_of(table[0, j] * block, block)
        keys_here = key_index + j * block
        dk_ref[...] = jnp.zeros_like(dk_ref)
        dv_ref[...] = jnp.zeros_like(dv_ref)

        def step(masked, i, inner):
            at = pl.multiple_of(table[0, i] * block, block)
            if masked:
                seen = (keys_here >= start_ref[pl.ds(i, 1), :]) & (
                    keys_here <= lane_index + i * block
                )
            for h in range(pair):
                grads = grad_ref[h * size : (h + 1) * size, pl.ds(at, block)]
                s = mm(qkv_ref[h, 1, pl.ds(key_at, block), :], qt_ref[h, :, pl.ds(at, block)])
                p = jnp.exp2(s - lse_ref[h, :, pl.ds(at, block)])
                if masked:
                    p = jnp.where(seen, p, 0.0)
                dp = mm(qkv_ref[h, 2, pl.ds(key_at, block), :], grads)
                ds = (p * (dp - delta_ref[h, :, pl.ds(at, block)])).astype(bf16)
                dv_ref[h] += mm(grads, p.astype(bf16), nt)
                dk_ref[h] += mm(qt_ref[h, :, pl.ds(at, block)], ds, nt)
                dq_ref[h, :, pl.ds(at, block)] += mm(kt_ref[h, :, pl.ds(key_at, block)], ds)
            return inner

        step(True, j, 0)
        lax.fori_loop(j + 1, table[3, j], functools.partial(step, False), 0)
        lax.fori_loop(table[3, j], table[4, j], functools.partial(step, True), 0)
        for h in range(pair):
            base = h * 3 * size
            out_ref[base + size : base + 2 * size, pl.ds(key_at, block)] = (
                dk_ref[h] * (1.0 / log2e)
            ).astype(bf16)
            out_ref[base + 2 * size : base + 3 * size, pl.ds(key_at, block)] = dv_ref[h].astype(bf16)
        return carry

    lax.fori_loop(0, count, key_block, 0)

    @pl.when(pl.program_id(0) == 0)
    def clear():
        dots_ref[...] = jnp.zeros_like(dots_ref)

    for h in range(pair):
        base = h * 3 * size
        rounded = dq_ref[h].astype(bf16).astype(f32)
        dots_ref[...] += jnp.sum(qt_ref[h].astype(f32) * rounded, axis=1, keepdims=True)
        out_ref[base : base + size, :] = (rounded * factor_ref[...]).astype(bf16)


def attend_back(chunk, table, qkv, att, grad, lse, starts, factor, pair=2):
    heads, _, length, size = qkv.shape
    count, block = starts.shape
    return pl.pallas_call(
        functools.partial(attend_back_kernel, count, block, pair),
        grid_spec=pltpu.PrefetchScalarGridSpec(
            num_scalar_prefetch=1,
            grid=(1,),
            in_specs=[
                pl.BlockSpec((pair, 3, length, size), lambda g, t: (chunk, 0, 0, 0)),
                pl.BlockSpec((pair * size, length), lambda g, t: (chunk, 0)),
                pl.BlockSpec((pair * size, length), lambda g, t: (chunk, 0)),
                pl.BlockSpec((pair, 1, length), lambda g, t: (chunk, 0, 0)),
                pl.BlockSpec((count, block), lambda g, t: (0, 0)),
                pl.BlockSpec((size, 1), lambda g, t: (0, 0)),
            ],
            out_specs=[
                pl.BlockSpec((pair * 3 * size, length), lambda g, t: (0, 0)),
                pl.BlockSpec((size, 1), lambda g, t: (0, 0)),
            ],
            scratch_shapes=[
                pltpu.VMEM((pair, size, length), bf16),
                pltpu.VMEM((pair, size, length), bf16),
                pltpu.VMEM((pair, 1, length), f32),
                pltpu.VMEM((pair, size, length), f32),
                pltpu.VMEM((pair, size, block), f32),
                pltpu.VMEM((pair, size, block), f32),
            ],
        ),
        out_shape=[
            jax.ShapeDtypeStruct((pair * 3 * size, length), bf16),
            jax.ShapeDtypeStruct((size, 1), f32),
        ],
        compiler_params=pltpu.CompilerParams(vmem_limit_bytes=56 << 20),
        cost_estimate=pl.CostEstimate(
            flops=pair * length * length * size * 5,
            bytes_accessed=pair * length * size * 20,
            transcendentals=pair * length * length // 4,
        ),
        name="attend_back",
    )(table, qkv, att, grad, lse, starts, factor)


def input_side_kernel(count, *refs):
    w_ref, out_ref = refs[count], refs[count + 1]
    grads = jnp.concatenate([ref[...] for ref in refs[:count]], axis=0)
    out_ref[...] = mm(grads.T, w_ref[...], nt).astype(bf16)


def input_side(grads, w, block):
    width, wide = w.shape
    rows, tokens = grads[0].shape
    return pl.pallas_call(
        functools.partial(input_side_kernel, len(grads)),
        grid=(tokens // block,),
        in_specs=[pl.BlockSpec((rows, block), lambda i: (0, i)) for _ in grads]
        + [pl.BlockSpec((width, wide), lambda i: (0, 0))],
        out_specs=pl.BlockSpec((block, width), lambda i: (i, 0)),
        out_shape=jax.ShapeDtypeStruct((tokens, width), bf16),
        compiler_params=pltpu.CompilerParams(vmem_limit_bytes=56 << 20),
        cost_estimate=pl.CostEstimate(
            flops=2 * tokens * width * wide,
            bytes_accessed=tokens * width * 2 + width * wide * 2 + tokens * wide * 2,
            transcendentals=0,
        ),
        name="input_side",
    )(*grads, w)


def reduce_places(buf, places):
    place = lax.axis_index("seq")
    rows = buf.shape[0]
    bits = places.bit_length() - 1
    assert places == 1 << bits and rows % places == 0
    for b in range(bits):
        bit = (place >> b) & 1
        halves = buf.reshape((2, -1) + buf.shape[1:])
        keep = lax.dynamic_index_in_dim(halves, bit, 0, keepdims=False)
        send = lax.dynamic_index_in_dim(halves, 1 - bit, 0, keepdims=False)
        got = lax.ppermute(send, "seq", [(i, i ^ (1 << b)) for i in range(places)])
        buf = (keep.astype(f32) + got.astype(f32)).astype(bf16)
    for b in reversed(range(bits)):
        bit = (place >> b) & 1
        got = lax.ppermute(buf, "seq", [(i, i ^ (1 << b)) for i in range(places)])
        buf = jnp.where(
            bit == 0, jnp.concatenate([buf, got], axis=0), jnp.concatenate([got, buf], axis=0)
        )
    return buf


def sum_everywhere(team, vector):
    vector = vector + lax.ppermute(vector, "dp", team.swap_core())
    total = vector
    for step in range(1, team.rows):
        total = total + lax.ppermute(vector, "dp", team.turn_rows(step))
    for b in range(team.seq.bit_length() - 1):
        total = total + lax.ppermute(
            total, "seq", [(i, i ^ (1 << b)) for i in range(team.seq)]
        )
    return total


def on_device(
    activations,
    segment_ids,
    norm1_gain,
    w_qkv,
    per_dim_scale,
    w_out,
    norm2_gain,
    w_up,
    b_up,
    w_down,
    b_down,
    cotangent,
):
    seqs, span, width = activations.shape
    rows_here, heads, _, head_size = w_qkv.shape
    length = segment_ids.shape[1]
    team = Team(lax.axis_size("dp"), lax.axis_size("seq"), seqs)
    size = team.size
    row, core, group, side, member = team.here()
    local_heads = heads // size
    wide = local_heads * 3 * head_size
    own = seqs * span

    def spread(array):
        out = []
        for step in range(seqs):
            block = lax.dynamic_index_in_dim(array, (group + step) % seqs, 0, keepdims=False)
            out.append(lax.ppermute(block, axes, team.spread(step)))
        return jnp.concatenate(out, axis=0)

    def unspread(array):
        out = []
        for step in range(seqs):
            got = lax.ppermute(array[step * span : (step + 1) * span], axes, team.back(step))
            out.append((got, (group + step) % seqs))
        return place_in(out, seqs)

    other_ids = lax.ppermute(segment_ids, "dp", team.swap_core())
    x_own = spread(activations)
    w_local = w_qkv.reshape(rows_here, heads * 3 * head_size)
    small = jnp.concatenate([norm1_gain, norm2_gain, b_up, b_down])
    small = jnp.pad(small, (0, wide * 16 - small.shape[0])).reshape(16, wide)

    def columns(first):
        part = lax.dynamic_slice_in_dim(w_local, first * wide, wide, 1)
        return jnp.concatenate([part, small], axis=0)

    mine = columns(member)
    got = lax.ppermute(columns(member + 1 - 2 * core), "dp", team.swap_core())
    both = jnp.stack([jnp.where(core == 0, mine, got), jnp.where(core == 0, got, mine)])
    pieces = [(both, row)]
    for step in range(1, team.rows):
        pieces.append(
            (lax.ppermute(both, "dp", team.turn_rows(step)), (row - step) % team.rows)
        )
    w_parts = place_in(pieces, team.rows).reshape(team.dp, rows_here + 16, wide)
    w_half = w_parts[:, :rows_here].reshape(width, wide)
    small = w_parts[:, rows_here:].reshape(team.dp, -1)[:, : 4 * rows_here]
    small = small.reshape(team.dp, 4, rows_here).transpose(1, 0, 2).reshape(4, width).astype(f32)
    gain_in, gain_mid, bias_up, bias_down = (small[i : i + 1] for i in range(4))
    three = jnp.stack([w_out, w_up, w_down])
    three, _ = lax.optimization_barrier((three, w_parts))
    three = gather_dp(team, three, row, core)
    w_out_all, w_up_all, w_down_all = (three[:, i].reshape(-1, width) for i in range(3))
    x_all = jnp.concatenate(
        [x_own] + [lax.ppermute(x_own, axes, team.rotate(-j)) for j in range(1, size)], axis=0
    )
    cot_in, _ = lax.optimization_barrier((cotangent, x_own))
    cot_own = spread(cot_in.astype(bf16))

    ids = lax.dynamic_index_in_dim(
        jnp.where(side == core, segment_ids, other_ids), group, 0, keepdims=False
    )
    starts = jnp.sum((ids[None, :] < ids[:, None]).astype(jnp.int32), axis=1)
    ends = jnp.sum((ids[None, :] <= ids[:, None]).astype(jnp.int32), axis=1) - 1
    count = length // span
    starts = starts.reshape(count, span)
    ends = ends.reshape(count, span)
    index = jnp.arange(count)
    z_of, u_of = index // size, index % size
    at = ((u_of - member) % size) * seqs + (group - z_of) % seqs
    first = starts[:, 0] // span
    last_start = starts[:, -1]
    open_from = jnp.minimum((last_start + span - 1) // span, index)
    open_to = jnp.sum((last_start[None, :] <= index[:, None] * span).astype(jnp.int32), axis=1)
    open_to = jnp.maximum(open_to, index + 1)
    stop = ends[:, -1] // span + 1
    table = jnp.stack([at, first, open_from, open_to, stop]).astype(jnp.int32)

    factor = scale_base / math.sqrt(head_size) * jax.nn.softplus(per_dim_scale)
    unit = jnp.ones((head_size,), f32)
    factor_row = jnp.tile(jnp.concatenate([factor * log2e, unit, unit]), local_heads)[None, :]

    qkv, normed_in = project_qkv(
        x_all, gain_in, w_half, factor_row, local_heads, head_size, span
    )
    att, lse = attend(table, qkv, starts)

    pieces = [(att[:, :own], member)]
    for j in range(1, size):
        got = lax.ppermute(att[:, j * own : (j + 1) * own], axes, team.rotate(j))
        pieces.append((got, (member - j) % size))
    att_own = place_in(pieces, size).reshape(heads * head_size, own)

    x_float = x_own.astype(f32)
    mid = x_float + lax.dot_general(
        att_own, w_out_all, (((0,), (0,)), ((), ())), preferred_element_type=f32
    )
    rms_mid = lax.rsqrt(jnp.mean(mid * mid, axis=-1, keepdims=True) + epsilon)
    normed_mid = (mid * rms_mid * gain_mid).astype(bf16)
    pre_act = mm(normed_mid, w_up_all) + bias_up
    activated = jax.nn.silu(pre_act).astype(bf16)
    result_own = (mid + mm(activated, w_down_all) + bias_down).astype(bf16)

    grad_bias_down = jnp.sum(cot_own.astype(f32), axis=0)
    tn = (((0,), (0,)), ((), ()))
    grad_act = mm(cot_own, w_down_all, nt)
    sig = jax.nn.sigmoid(pre_act)
    grad_pre = (grad_act * sig * (1.0 + pre_act * (1.0 - sig))).astype(bf16)
    grad_bias_up = jnp.sum(grad_pre.astype(f32), axis=0)
    grad_normed_mid = mm(grad_pre, w_up_all, nt)
    grad_gain_mid = jnp.sum(grad_normed_mid * mid * rms_mid, axis=0)
    scaled_mid = grad_normed_mid * gain_mid
    grad_mid = cot_own.astype(f32) + rms_mid * (
        scaled_mid - mid * rms_mid * rms_mid * jnp.mean(scaled_mid * mid, axis=-1, keepdims=True)
    )
    grad_attn = grad_mid.astype(bf16)
    grad_att = mm(w_out_all, grad_attn, nt).astype(bf16).reshape(size, -1, own)
    pieces = [(lax.dynamic_index_in_dim(grad_att, member, 0, keepdims=False), 0)]
    for j in range(1, size):
        out = lax.dynamic_index_in_dim(grad_att, (member + j) % size, 0, keepdims=False)
        pieces.append((lax.ppermute(out, axes, team.rotate(j)), (-j) % size))
    pieces.sort(key=lambda item: item[1])
    grad_heads = jnp.concatenate([piece for piece, _ in pieces], axis=1)

    grad_down = mm(activated, cot_own, tn)
    grad_up = mm(normed_mid, grad_pre, tn)
    grad_out = mm(att_own, grad_attn)

    chunks = [
        attend_back(c, table, qkv, att, grad_heads, lse, starts, factor[:, None])
        for c in range(local_heads // 2)
    ]
    dots = sum(d for _, d in chunks)
    chunks = [g for g, _ in chunks]
    partial = input_side(chunks, w_half, span)
    grad_normed_in = partial[:own].astype(f32)
    for j in range(1, size):
        grad_normed_in = grad_normed_in + lax.ppermute(
            partial[j * own : (j + 1) * own], axes, team.rotate(j)
        ).astype(f32)
    rms_in = lax.rsqrt(jnp.mean(x_float * x_float, axis=-1, keepdims=True) + epsilon)
    grad_gain_in = jnp.sum(grad_normed_in * x_float * rms_in, axis=0)
    scaled_in = grad_normed_in * gain_in
    input_grad_own = grad_mid + rms_in * (
        scaled_in
        - x_float * rms_in * rms_in * jnp.mean(scaled_in * x_float, axis=-1, keepdims=True)
    )
    input_grad = unspread(input_grad_own.astype(bf16)).astype(f32)
    result = unspread(result_own)

    def shared(parts):
        parts = parts.reshape((team.rows, 2) + parts.shape[1:])
        keep = lax.dynamic_index_in_dim(parts, core, 1, keepdims=False)
        send = lax.dynamic_index_in_dim(parts, 1 - core, 1, keepdims=False)
        got = lax.ppermute(send, "dp", team.swap_core())
        both = (keep.astype(f32) + got.astype(f32)).astype(bf16)
        return over_rows(both)

    def over_rows(both):
        total = lax.dynamic_index_in_dim(both, row, 0, keepdims=False).astype(f32)
        for step in range(1, team.rows):
            out = lax.dynamic_index_in_dim(both, (row + step) % team.rows, 0, keepdims=False)
            total = total + lax.ppermute(out, "dp", team.turn_rows(step)).astype(f32)
        return total.astype(bf16)

    vectors = jnp.stack([grad_gain_mid, grad_bias_up, grad_bias_down]).reshape(3, team.dp, -1)
    vectors = vectors.transpose(1, 0, 2).reshape(team.dp, 1, -1).astype(bf16)
    lines = -(-(3 * rows_here + 1) // (16 * team.seq)) * 16 * team.seq
    vectors = jnp.pad(
        vectors, ((0, 0), (0, lines - 3 * rows_here - 1), (0, width - vectors.shape[2]))
    )
    three = jnp.concatenate(
        [g.astype(bf16).reshape(team.dp, rows_here, width) for g in (grad_out, grad_up, grad_down)]
        + [vectors],
        axis=1,
    )
    three = reduce_places(shared(three), team.seq)
    part_out, part_up, part_down = (
        three[i * rows_here : (i + 1) * rows_here].astype(f32) for i in range(3)
    )
    part_gain_mid, part_bias_up, part_bias_down = (
        three[3 * rows_here, i * rows_here : (i + 1) * rows_here].astype(f32) for i in range(3)
    )
    heads_of = []
    for grads in chunks:
        part = mm(grads, normed_in).astype(bf16)
        part = part.reshape(-1, team.rows, 2, rows_here).transpose(1, 2, 0, 3)
        keep = lax.dynamic_index_in_dim(part, core, 1, keepdims=False)
        send = lax.dynamic_index_in_dim(part, 1 - core, 1, keepdims=False)
        got = lax.ppermute(send, "dp", team.swap_core())
        both = jnp.stack(
            [jnp.where(core == 0, keep, got), jnp.where(core == 0, got, keep)], axis=1
        )
        total = over_rows(both)
        total = place_in([(total, member // 2)], team.half)
        lines = total.size // rows_here
        total = reduce_places(total.reshape(lines, rows_here), team.seq)
        heads_of.append(total.reshape(size, -1, rows_here))
    full = jnp.stack(heads_of, axis=1).reshape(heads, 3, head_size, rows_here)
    vectors = sum_everywhere(team, jnp.concatenate([grad_gain_in, dots[:, 0]]))
    d = lax.axis_index("dp")

    def slice_of(i):
        return lax.dynamic_slice_in_dim(vectors, i * width + d * rows_here, rows_here, 0)

    grad_scale = vectors[width:] / (factor * log2e) * (
        scale_base / math.sqrt(head_size)
    ) * jax.nn.sigmoid(per_dim_scale)
    return (
        result,
        input_grad,
        slice_of(0),
        full.astype(f32).transpose(3, 0, 1, 2),
        grad_scale,
        part_out,
        part_gain_mid,
        part_up,
        part_bias_up,
        part_down,
        part_bias_down,
    )


def solution(mesh):
    in_specs = (
        P("dp", "seq", None),
        P("dp", None),
        P("dp"),
        P("dp", None, None, None),
        P(),
        P("dp", None),
        P("dp"),
        P("dp", None),
        P("dp"),
        P("dp", None),
        P("dp"),
        P("dp", "seq", None),
    )
    out_specs = (
        P("dp", "seq", None),
        P("dp", "seq", None),
        P("dp"),
        P("dp", None, None, None),
        P(),
        P("dp", None),
        P("dp"),
        P("dp", None),
        P("dp"),
        P("dp", None),
        P("dp"),
    )
    return jax.shard_map(
        on_device, mesh=mesh, in_specs=in_specs, out_specs=out_specs, check_vma=False
    )
```

```python
import functools
import math

import jax
import jax.numpy as jnp
from jax import lax
from jax.experimental import pallas as pl
from jax.experimental.pallas import tpu as pltpu
from jax.sharding import PartitionSpec as P

epsilon = 1e-06
scale_base = 1.442695041
log2e = 1.4426950408889634
masked_value = -1e30
score_limit = 100.0
bf16 = jnp.bfloat16
f32 = jnp.float32
axes = ("dp", "seq")
brief = pl.CostEstimate(flops=1, bytes_accessed=1, transcendentals=0)
nt = (((1,), (1,)), ((), ()))
nn = (((1,), (0,)), ((), ()))


def mm(a, b, dims=nn):
    return lax.dot_general(a, b, dims, preferred_element_type=f32)


class Team:
    def __init__(self, dp, seq, seqs):
        self.dp, self.seq, self.seqs = dp, seq, seqs
        self.size = seq // seqs
        assert seq % seqs == 0 and self.size % 2 == 0 and dp % 2 == 0
        self.half = self.size // 2
        self.rows = dp // 2

    def places(self):
        for row in range(self.rows):
            for core in range(2):
                for place in range(self.seq):
                    yield row, core, place

    def rank(self, row, core, place):
        return (row * 2 + core) * self.seq + place

    def here(self):
        d = lax.axis_index("dp")
        p = lax.axis_index("seq")
        row, core = d // 2, d % 2
        group = p // self.size
        side = (p % self.size) // self.half
        member = (p % self.half) * 2 + core
        return row, core, group, side, member

    def spread(self, step):
        pairs = []
        for row, core, place in self.places():
            z, u = place // self.size, place % self.size
            s = (z + step) % self.seqs
            pairs.append(
                (
                    self.rank(row, core, place),
                    self.rank(row, u % 2, s * self.size + core * self.half + u // 2),
                )
            )
        return pairs

    def back(self, step):
        return [(b, a) for a, b in self.spread(step)]

    def rotate(self, step):
        pairs = []
        for row, core, place in self.places():
            base = place - place % self.half
            m = (place % self.half) * 2 + core
            to = (m + step) % self.size
            pairs.append((self.rank(row, core, place), self.rank(row, to % 2, base + to // 2)))
        return pairs

    def swap_core(self):
        return [(d, d ^ 1) for d in range(self.dp)]

    def turn_rows(self, step, flip=0):
        return [(d, ((d + 2 * step) % self.dp) ^ flip) for d in range(self.dp)]


def after(value, *first):
    return lax.optimization_barrier((value, first))[0]


def place_in(pieces, count):
    first = pieces[0][0]
    out = jnp.zeros((count,) + first.shape, first.dtype)
    for piece, index in pieces:
        out = lax.dynamic_update_index_in_dim(out, piece, index, 0)
    return out


def join_kernel(count, ends, slots_ref, *refs):
    outs = refs[count:]
    for k in range(count):
        start = 0
        for out_ref, end in zip(outs, ends):
            out_ref[slots_ref[k]] = refs[k][start:end, :].astype(out_ref.dtype)
            start = end


def join(pieces, slots, ends=None, dtype=None):
    count = len(pieces)
    rows, columns = pieces[0].shape
    dtype = dtype or pieces[0].dtype
    ends = ends or (rows,)
    heights = [b - a for a, b in zip((0,) + tuple(ends[:-1]), ends)]
    wide = columns
    if columns % 128 == 0:
        wide = max(b for b in range(128, min(columns, 640) + 1, 128) if columns % b == 0)
    outs = pl.pallas_call(
        functools.partial(join_kernel, count, ends),
        grid_spec=pltpu.PrefetchScalarGridSpec(
            num_scalar_prefetch=1,
            grid=(columns // wide,),
            in_specs=[pl.BlockSpec((rows, wide), lambda i, s: (0, i)) for _ in pieces],
            out_specs=[pl.BlockSpec((count, h, wide), lambda i, s: (0, 0, i)) for h in heights],
        ),
        out_shape=[jax.ShapeDtypeStruct((count, h, columns), dtype) for h in heights],
        compiler_params=pltpu.CompilerParams(vmem_limit_bytes=56 << 20),
        cost_estimate=brief,
        name="join",
    )(jnp.stack(slots).astype(jnp.int32), *pieces)
    return outs if len(ends) > 1 else outs[0]


def qkv_kernel(count, blocks, parts, head_size, *refs):
    x_refs = refs[:count]
    gain_ref, w_ref, factor_ref, out_ref, normed_ref = refs[count:]
    i = pl.program_id(0)
    x = x_refs[0][...]
    for j in range(1, count):
        x = jnp.where(i >= j * blocks, x_refs[j][...], x)
    x = x.astype(f32)
    rms = lax.rsqrt(jnp.mean(x * x, axis=-1, keepdims=True) + epsilon)
    normed = (x * rms * gain_ref[...]).astype(bf16)
    part = x.shape[1] // parts
    for d in range(parts):
        normed_ref[d % 2, :, d // 2 * part : (d // 2 + 1) * part] = normed[
            :, d * part : (d + 1) * part
        ]
    packed = (mm(normed, w_ref[...]) * factor_ref[...]).astype(bf16)
    for h in range(packed.shape[1] // head_size):
        out_ref[h // 3, h % 3] = packed[:, h * head_size : (h + 1) * head_size]


def project_qkv(xs, gain, w, factor_row, heads, head_size, parts, block):
    own, width = xs[0].shape
    count, blocks = len(xs), own // block
    tokens = own * count
    wide = w.shape[1]

    def x_spec(j):
        return pl.BlockSpec(
            (block, width), lambda i: (jnp.clip(i - j * blocks, 0, blocks - 1), 0)
        )

    return pl.pallas_call(
        functools.partial(qkv_kernel, count, blocks, parts, head_size),
        grid=(tokens // block,),
        in_specs=[x_spec(j) for j in range(count)]
        + [
            pl.BlockSpec((1, width), lambda i: (0, 0)),
            pl.BlockSpec((width, wide), lambda i: (0, 0)),
            pl.BlockSpec((1, wide), lambda i: (0, 0)),
        ],
        out_specs=[
            pl.BlockSpec((heads, 3, block, head_size), lambda i: (0, 0, i, 0)),
            pl.BlockSpec((2, block, width // 2), lambda i: (0, i, 0)),
        ],
        out_shape=[
            jax.ShapeDtypeStruct((heads, 3, tokens, head_size), bf16),
            jax.ShapeDtypeStruct((2, tokens, width // 2), bf16),
        ],
        compiler_params=pltpu.CompilerParams(vmem_limit_bytes=56 << 20),
        cost_estimate=brief,
        name="qkv",
    )(*xs, gain, w, factor_row)


def head_grad_kernel(rows, fold, place_ref, grads_ref, normed_ref, *out_refs):
    result = mm(grads_ref[...], normed_ref[0]).astype(bf16)
    part = result.shape[1] // rows
    lines = result.shape[0] // fold
    for side in range(2):
        for row in range(rows):

            @pl.when((pl.program_id(0) == side) & (place_ref[2] == row))
            def store(side=side, row=row):
                for step in range(rows):
                    at = (row + step) % rows * part
                    for k in range(fold):
                        out_refs[side * rows + step][:, k * part : (k + 1) * part] = result[
                            k * lines : (k + 1) * lines, at : at + part
                        ]


def head_grad(grads, normed, rows, row, core):
    _, tokens, width = normed.shape
    lines = grads.shape[0]
    part = width // rows
    fold = 128 // math.gcd(part, 128)
    shape = (lines // fold, fold * part)
    outs = pl.pallas_call(
        functools.partial(head_grad_kernel, rows, fold),
        grid_spec=pltpu.PrefetchScalarGridSpec(
            num_scalar_prefetch=1,
            grid=(2,),
            in_specs=[
                pl.BlockSpec((lines, tokens), lambda i, o: (0, 0)),
                pl.BlockSpec((1, tokens, width), lambda i, o: (o[i], 0, 0)),
            ],
            out_specs=[pl.BlockSpec(shape, lambda i, o: (0, 0)) for _ in range(2 * rows)],
        ),
        out_shape=[jax.ShapeDtypeStruct(shape, bf16) for _ in range(2 * rows)],
        compiler_params=pltpu.CompilerParams(vmem_limit_bytes=56 << 20),
        cost_estimate=brief,
        name="head_grad",
    )(jnp.stack([1 - core, core, row]).astype(jnp.int32), grads, normed)
    return outs[:rows], outs[rows:]


def unfold_kernel(count, fold, core_ref, *refs):
    out_ref = refs[count]
    part = out_ref.shape[1]
    lines = out_ref.shape[0] // fold
    for c in range(count):

        @pl.when(pl.program_id(0) % count == c)
        def store(c=c):
            for k in range(fold):
                out_ref[k * lines : (k + 1) * lines, :] = refs[c][
                    :, k * part : (k + 1) * part
                ].astype(f32)


def unfold(chunks, groups, part, core):
    count = len(chunks)
    lines = chunks[0].shape[0] // (2 * groups)
    wide = chunks[0].shape[1]
    fold = wide // part

    def source(i, o):
        g = i // count
        return (g // 2 * 2 + (g % 2 + o[0]) % 2, 0)

    return pl.pallas_call(
        functools.partial(unfold_kernel, count, fold),
        grid_spec=pltpu.PrefetchScalarGridSpec(
            num_scalar_prefetch=1,
            grid=(2 * groups * count,),
            in_specs=[pl.BlockSpec((lines, wide), source) for _ in chunks],
            out_specs=pl.BlockSpec((lines * fold, part), lambda i, o: (i, 0)),
        ),
        out_shape=jax.ShapeDtypeStruct((2 * groups * count * lines * fold, part), f32),
        compiler_params=pltpu.CompilerParams(vmem_limit_bytes=56 << 20),
        cost_estimate=brief,
        name="unfold",
    )(core.reshape(1).astype(jnp.int32), *chunks)


def eye_rows(rows, columns):
    a = lax.broadcasted_iota(jnp.int32, (rows, columns), 0)
    b = lax.broadcasted_iota(jnp.int32, (rows, columns), 1)
    return (a == b).astype(bf16)


def attend_kernel(count, block, pair, table, qkv_ref, start_ref, att_ref, lse_ref, vt_ref, acc_ref):
    size = qkv_ref.shape[3]
    rows = vt_ref.shape[1]
    unit = eye_rows(rows, size)
    one_row = (lax.broadcasted_iota(jnp.int32, (rows, block), 0) == size).astype(f32)
    for h in range(pair):
        for b in range(count):
            here = slice(b * block, (b + 1) * block)
            vt_ref[h, :, here] = (mm(unit, qkv_ref[h, 2, here, :], nt) + one_row).astype(bf16)
    key_index = lax.broadcasted_iota(jnp.int32, (block, block), 0)
    lane_index = lax.broadcasted_iota(jnp.int32, (1, block), 1)
    ones = jnp.ones((8, size), bf16)

    def longest(part):
        best = jnp.zeros((8, block), f32)
        for h in range(pair):
            for b in range(count):
                x = qkv_ref[h, part, b * block : (b + 1) * block, :]
                best = jnp.maximum(best, mm(ones, x * x, nt))
        return jnp.max(best)

    small = longest(0) * longest(1) * 1.1 < score_limit * score_limit

    def query_block(raised, i, carry):
        at = pl.multiple_of(table[0, i] * block, block)
        starts = start_ref[pl.ds(i, 1), :]
        places = lane_index + i * block
        queries = [qkv_ref[h, 0, pl.ds(at, block), :] for h in range(pair)]
        acc_ref[...] = jnp.zeros_like(acc_ref)

        def step(masked, j, peaks):
            key_at = pl.multiple_of(table[0, j] * block, block)
            if masked:
                keys_here = key_index + j * block
                seen = (keys_here >= starts) & (keys_here <= places)
            scores = [
                mm(qkv_ref[h, 1, pl.ds(key_at, block), :], queries[h], nt) for h in range(pair)
            ]
            if masked:
                scores = [jnp.where(seen, s, masked_value) for s in scores]
            values = [vt_ref[h, :, pl.ds(key_at, block)] for h in range(pair)]
            if not raised:
                probs = [jnp.exp2(s).astype(bf16) for s in scores]
                sums = [mm(values[h], probs[h]) for h in range(pair)]
                for h in range(pair):
                    acc_ref[h] += sums[h]
                return ()
            out = []
            for h in range(pair):
                peak = jnp.maximum(peaks[h], jnp.max(scores[h], axis=0, keepdims=True))
                p = jnp.exp2(scores[h] - peak).astype(bf16)
                acc_ref[h] = acc_ref[h] * jnp.exp2(peaks[h] - peak) + mm(values[h], p)
                out.append(peak)
            return tuple(out)

        peaks = ()
        if raised:
            peaks = tuple(jnp.full((1, block), masked_value, f32) for _ in range(pair))
        peaks = lax.fori_loop(table[1, i], table[2, i], functools.partial(step, True), peaks)
        peaks = lax.fori_loop(table[2, i], i, functools.partial(step, False), peaks)
        peaks = step(True, i, peaks)
        for h in range(pair):
            total = acc_ref[h, size : size + 1, :]
            att_ref[h * size : (h + 1) * size, pl.ds(at, block)] = (
                acc_ref[h, :size, :] / total
            ).astype(bf16)
            low = jnp.log2(total)
            lse_ref[h, :, pl.ds(at, block)] = peaks[h] + low if raised else low
        return carry

    @pl.when(small)
    def plain():
        lax.fori_loop(0, count, functools.partial(query_block, False), 0)

    @pl.when(jnp.logical_not(small))
    def careful():
        lax.fori_loop(0, count, functools.partial(query_block, True), 0)


def attend(table, qkv, starts):
    heads, _, length, size = qkv.shape
    pair = math.gcd(heads, 8)
    count, block = starts.shape
    rows = (size // 16 + 1) * 16
    return pl.pallas_call(
        functools.partial(attend_kernel, count, block, pair),
        grid_spec=pltpu.PrefetchScalarGridSpec(
            num_scalar_prefetch=1,
            grid=(heads // pair,),
            in_specs=[
                pl.BlockSpec((pair, 3, length, size), lambda g, t: (g, 0, 0, 0)),
                pl.BlockSpec((count, block), lambda g, t: (0, 0)),
            ],
            out_specs=[
                pl.BlockSpec((pair * size, length), lambda g, t: (g, 0)),
                pl.BlockSpec((pair, 1, length), lambda g, t: (g, 0, 0)),
            ],
            scratch_shapes=[
                pltpu.VMEM((pair, rows, length), bf16),
                pltpu.VMEM((pair, rows, block), f32),
            ],
        ),
        out_shape=[
            jax.ShapeDtypeStruct((heads * size, length), bf16),
            jax.ShapeDtypeStruct((heads, 1, length), f32),
        ],
        compiler_params=pltpu.CompilerParams(vmem_limit_bytes=56 << 20),
        cost_estimate=brief,
        name="attend",
    )(table, qkv, starts)


def attend_back_kernel(
    count,
    block,
    pair,
    table,
    qkv_ref,
    att_ref,
    grad_ref,
    lse_ref,
    start_ref,
    factor_ref,
    out_ref,
    dots_ref,
    qt_ref,
    kt_ref,
    delta_ref,
    dq_ref,
    dk_ref,
    dv_ref,
):
    size = qkv_ref.shape[3]
    unit = eye_rows(size, size)
    for h in range(pair):
        for b in range(count):
            here = slice(b * block, (b + 1) * block)
            qt_ref[h, :, here] = mm(unit, qkv_ref[h, 0, here, :], nt).astype(bf16)
            kt_ref[h, :, here] = mm(unit, qkv_ref[h, 1, here, :], nt).astype(bf16)
        rows = slice(h * size, (h + 1) * size)
        delta_ref[h] = jnp.sum(
            att_ref[rows, :].astype(f32) * grad_ref[rows, :].astype(f32), axis=0, keepdims=True
        )
    dq_ref[...] = jnp.zeros_like(dq_ref)
    key_index = lax.broadcasted_iota(jnp.int32, (block, block), 0)
    lane_index = lax.broadcasted_iota(jnp.int32, (1, block), 1)

    def key_block(j, carry):
        key_at = pl.multiple_of(table[0, j] * block, block)
        keys_here = key_index + j * block
        dk_ref[...] = jnp.zeros_like(dk_ref)
        dv_ref[...] = jnp.zeros_like(dv_ref)

        def step(masked, i, inner):
            at = pl.multiple_of(table[0, i] * block, block)
            if masked:
                seen = (keys_here >= start_ref[pl.ds(i, 1), :]) & (
                    keys_here <= lane_index + i * block
                )
            both = range(pair)
            grads = [grad_ref[h * size : (h + 1) * size, pl.ds(at, block)] for h in both]
            queries = [qt_ref[h, :, pl.ds(at, block)] for h in both]
            s = [mm(qkv_ref[h, 1, pl.ds(key_at, block), :], queries[h]) for h in both]
            dp = [mm(qkv_ref[h, 2, pl.ds(key_at, block), :], grads[h]) for h in both]
            p = [jnp.exp2(s[h] - lse_ref[h, :, pl.ds(at, block)]) for h in both]
            if masked:
                p = [jnp.where(seen, x, 0.0) for x in p]
            ds = [
                (p[h] * (dp[h] - delta_ref[h, :, pl.ds(at, block)])).astype(bf16) for h in both
            ]
            dv = [mm(grads[h], p[h].astype(bf16), nt) for h in both]
            dk = [mm(queries[h], ds[h], nt) for h in both]
            dq = [mm(kt_ref[h, :, pl.ds(key_at, block)], ds[h]) for h in both]
            for h in both:
                dv_ref[h] += dv[h]
                dk_ref[h] += dk[h]
                dq_ref[h, :, pl.ds(at, block)] += dq[h]
            return inner

        step(True, j, 0)
        lax.fori_loop(j + 1, table[3, j], functools.partial(step, False), 0)
        lax.fori_loop(table[3, j], table[4, j], functools.partial(step, True), 0)
        for h in range(pair):
            base = h * 3 * size
            out_ref[base + size : base + 2 * size, pl.ds(key_at, block)] = (
                dk_ref[h] * (1.0 / log2e)
            ).astype(bf16)
            out_ref[base + 2 * size : base + 3 * size, pl.ds(key_at, block)] = dv_ref[h].astype(bf16)
        return carry

    lax.fori_loop(0, count, key_block, 0)

    @pl.when(pl.program_id(0) == 0)
    def clear():
        dots_ref[...] = jnp.zeros_like(dots_ref)

    for h in range(pair):
        base = h * 3 * size
        rounded = dq_ref[h].astype(bf16).astype(f32)
        dots_ref[...] += jnp.sum(qt_ref[h].astype(f32) * rounded, axis=1, keepdims=True)
        out_ref[base : base + size, :] = (rounded * factor_ref[...]).astype(bf16)


def attend_back(chunk, pair, table, qkv, att, grad, lse, starts, factor):
    heads, _, length, size = qkv.shape
    count, block = starts.shape
    return pl.pallas_call(
        functools.partial(attend_back_kernel, count, block, pair),
        grid_spec=pltpu.PrefetchScalarGridSpec(
            num_scalar_prefetch=1,
            grid=(1,),
            in_specs=[
                pl.BlockSpec((pair, 3, length, size), lambda g, t: (chunk, 0, 0, 0)),
                pl.BlockSpec((pair * size, length), lambda g, t: (chunk, 0)),
                pl.BlockSpec((pair * size, length), lambda g, t: (chunk, 0)),
                pl.BlockSpec((pair, 1, length), lambda g, t: (chunk, 0, 0)),
                pl.BlockSpec((count, block), lambda g, t: (0, 0)),
                pl.BlockSpec((size, 1), lambda g, t: (0, 0)),
            ],
            out_specs=[
                pl.BlockSpec((pair * 3 * size, length), lambda g, t: (0, 0)),
                pl.BlockSpec((size, 1), lambda g, t: (0, 0)),
            ],
            scratch_shapes=[
                pltpu.VMEM((pair, size, length), bf16),
                pltpu.VMEM((pair, size, length), bf16),
                pltpu.VMEM((pair, 1, length), f32),
                pltpu.VMEM((pair, size, length), f32),
                pltpu.VMEM((pair, size, block), f32),
                pltpu.VMEM((pair, size, block), f32),
            ],
        ),
        out_shape=[
            jax.ShapeDtypeStruct((pair * 3 * size, length), bf16),
            jax.ShapeDtypeStruct((size, 1), f32),
        ],
        compiler_params=pltpu.CompilerParams(vmem_limit_bytes=56 << 20),
        cost_estimate=brief,
        name="attend_back",
    )(table, qkv, att, grad, lse, starts, factor)


def input_side_kernel(count, *refs):
    w_ref, out_ref = refs[count], refs[count + 1]
    grads = jnp.concatenate([ref[...] for ref in refs[:count]], axis=0)
    out_ref[...] = mm(grads.T, w_ref[...], nt).astype(bf16)


def input_side(grads, w, block, first, blocks):
    width, wide = w.shape
    rows = grads[0].shape[0]
    tokens = blocks * block
    return pl.pallas_call(
        functools.partial(input_side_kernel, len(grads)),
        grid=(blocks,),
        in_specs=[pl.BlockSpec((rows, block), lambda i: (0, i + first)) for _ in grads]
        + [pl.BlockSpec((width, wide), lambda i: (0, 0))],
        out_specs=pl.BlockSpec((block, width), lambda i: (i, 0)),
        out_shape=jax.ShapeDtypeStruct((tokens, width), bf16),
        compiler_params=pltpu.CompilerParams(vmem_limit_bytes=56 << 20),
        cost_estimate=brief,
        name="input_side",
    )(*grads, w)


def reduce_places(buf, places):
    place = lax.axis_index("seq")
    lines, wide = buf.shape
    bits = places.bit_length() - 1
    assert places == 1 << bits and lines % places == 0
    for b in range(bits):
        bit = (place >> b) & 1
        halves = buf.reshape(2, -1, wide)
        keep = lax.dynamic_index_in_dim(halves, bit, 0, keepdims=False)
        send = lax.dynamic_index_in_dim(halves, 1 - bit, 0, keepdims=False)
        yield send
        got = lax.ppermute(send, "seq", [(i, i ^ (1 << b)) for i in range(places)])
        buf = (keep.astype(f32) + got.astype(f32)).astype(bf16)
    for b in reversed(range(bits)):
        bit = (place >> b) & 1
        yield buf
        got = lax.ppermute(buf, "seq", [(i, i ^ (1 << b)) for i in range(places)])
        buf = jnp.where(
            bit == 0, jnp.concatenate([buf, got], axis=0), jnp.concatenate([got, buf], axis=0)
        )
    yield buf


def last(steps):
    for value in steps:
        pass
    return value


def sum_everywhere(team, vector):
    vector = vector + lax.ppermute(vector, "dp", team.swap_core())
    total = vector
    for step in range(1, team.rows):
        total = total + lax.ppermute(vector, "dp", team.turn_rows(step))
    for b in range(team.seq.bit_length() - 1):
        total = total + lax.ppermute(
            total, "seq", [(i, i ^ (1 << b)) for i in range(team.seq)]
        )
    return total


def on_device(
    activations,
    segment_ids,
    norm1_gain,
    w_qkv,
    per_dim_scale,
    w_out,
    norm2_gain,
    w_up,
    b_up,
    w_down,
    b_down,
    cotangent,
):
    seqs, span, width = activations.shape
    rows_here, heads, _, head_size = w_qkv.shape
    length = segment_ids.shape[1]
    team = Team(lax.axis_size("dp"), lax.axis_size("seq"), seqs)
    size = team.size
    row, core, group, side, member = team.here()
    local_heads = heads // size
    wide = local_heads * 3 * head_size
    own = seqs * span

    def spread(array):
        out = []
        for step in range(seqs):
            block = lax.dynamic_index_in_dim(array, (group + step) % seqs, 0, keepdims=False)
            out.append(lax.ppermute(block, axes, team.spread(step)))
        return join(out, [jnp.int32(k) for k in range(seqs)]).reshape(own, width)

    def unspread(array):
        return [
            lax.ppermute(array[step * span : (step + 1) * span], axes, team.back(step))
            for step in range(seqs)
        ]

    def unspread_done(pieces, dtype):
        return join(pieces, [(group + step) % seqs for step in range(seqs)], dtype=dtype)

    def shard_of(step, flip):
        return (row - step) % team.rows * 2 + (core ^ flip)

    shifts = [(step, flip) for step in range(team.rows) for flip in range(2)]

    w_local = w_qkv.reshape(rows_here, heads * 3 * head_size)
    small = jnp.concatenate([norm1_gain, norm2_gain, b_up, b_down])
    small = jnp.pad(small, (0, wide * 16 - small.shape[0])).reshape(16, wide)

    def columns(first):
        part = lax.dynamic_slice_in_dim(w_local, first * wide, wide, 1)
        return jnp.concatenate([part, small], axis=0)

    parts = [columns(member), columns(member + 1 - 2 * core)]
    far = [
        lax.ppermute(parts[flip], "dp", team.turn_rows(step, flip)) for step, flip in shifts[2:]
    ]
    near = lax.ppermute(parts[1], "dp", team.swap_core())
    x_own = spread(after(activations, *parts))
    other_ids = lax.ppermute(segment_ids, "dp", team.swap_core())
    w_half, small = join(
        [parts[0], near] + far,
        [shard_of(*s) for s in shifts],
        ends=(rows_here, rows_here + 16),
    )
    w_half = w_half.reshape(width, wide)
    small = small.reshape(team.dp, -1)[:, : 4 * rows_here]
    small = small.reshape(team.dp, 4, rows_here).transpose(1, 0, 2).reshape(4, width).astype(f32)
    gain_in, gain_mid, bias_up, bias_down = (small[i : i + 1] for i in range(4))
    xs = [x_own] + [lax.ppermute(x_own, axes, team.rotate(-j)) for j in range(1, size)]
    three = after(jnp.concatenate([w_out, w_up, w_down]), *far)
    three = [three] + [
        lax.ppermute(three, "dp", team.turn_rows(step)) for step in range(1, team.rows)
    ]
    cot_own = spread(after(cotangent, x_own).astype(bf16))

    ids = lax.dynamic_index_in_dim(
        jnp.where(side == core, segment_ids, other_ids), group, 0, keepdims=False
    )
    starts = jnp.sum((ids[None, :] < ids[:, None]).astype(jnp.int32), axis=1)
    ends = jnp.sum((ids[None, :] <= ids[:, None]).astype(jnp.int32), axis=1) - 1
    count = length // span
    starts = starts.reshape(count, span)
    ends = ends.reshape(count, span)
    index = jnp.arange(count)
    z_of, u_of = index // size, index % size
    at = ((u_of - member) % size) * seqs + (group - z_of) % seqs
    first = starts[:, 0] // span
    last_start = starts[:, -1]
    open_from = jnp.minimum((last_start + span - 1) // span, index)
    open_to = jnp.sum((last_start[None, :] <= index[:, None] * span).astype(jnp.int32), axis=1)
    open_to = jnp.maximum(open_to, index + 1)
    stop = ends[:, -1] // span + 1
    table = jnp.stack([at, first, open_from, open_to, stop]).astype(jnp.int32)

    factor = scale_base / math.sqrt(head_size) * jax.nn.softplus(per_dim_scale)
    unit = jnp.ones((head_size,), f32)
    factor_row = jnp.tile(jnp.concatenate([factor * log2e, unit, unit]), local_heads)[None, :]

    qkv, normed_in = project_qkv(
        xs, gain_in, w_half, factor_row, local_heads, head_size, team.dp, span
    )
    att, lse = attend(table, qkv, starts)
    three = after(three, att)
    swapped = [lax.ppermute(piece, "dp", team.swap_core()) for piece in three]
    w_out_all, w_up_all, w_down_all = (
        w.reshape(-1, width)
        for w in join(
            three + swapped,
            [shard_of(step, 0) for step in range(team.rows)]
            + [shard_of(step, 1) for step in range(team.rows)],
            ends=(rows_here, 2 * rows_here, 3 * rows_here),
        )
    )

    pieces = [(att[:, :own], member)]
    for j in range(1, size):
        got = lax.ppermute(att[:, j * own : (j + 1) * own], axes, team.rotate(j))
        pieces.append((got, (member - j) % size))
    att_own = join([p for p, _ in pieces], [s for _, s in pieces])
    att_own = att_own.reshape(heads * head_size, own)

    x_float = x_own.astype(f32)
    mid = x_float + lax.dot_general(
        att_own, w_out_all, (((0,), (0,)), ((), ())), preferred_element_type=f32
    )
    rms_mid = lax.rsqrt(jnp.mean(mid * mid, axis=-1, keepdims=True) + epsilon)
    normed_mid = (mid * rms_mid * gain_mid).astype(bf16)
    pre_act = mm(normed_mid, w_up_all) + bias_up
    activated = jax.nn.silu(pre_act).astype(bf16)
    result_own = (mid + mm(activated, w_down_all) + bias_down).astype(bf16)
    result = unspread(result_own)
    cot_own = after(cot_own, result_own)

    grad_bias_down = jnp.sum(cot_own.astype(f32), axis=0)
    tn = (((0,), (0,)), ((), ()))
    grad_act = mm(cot_own, w_down_all, nt)
    sig = jax.nn.sigmoid(pre_act)
    grad_pre = (grad_act * sig * (1.0 + pre_act * (1.0 - sig))).astype(bf16)
    grad_bias_up = jnp.sum(grad_pre.astype(f32), axis=0)
    grad_normed_mid = mm(grad_pre, w_up_all, nt)
    grad_gain_mid = jnp.sum(grad_normed_mid * mid * rms_mid, axis=0)
    scaled_mid = grad_normed_mid * gain_mid
    grad_mid = cot_own.astype(f32) + rms_mid * (
        scaled_mid - mid * rms_mid * rms_mid * jnp.mean(scaled_mid * mid, axis=-1, keepdims=True)
    )
    grad_attn = grad_mid.astype(bf16)
    grad_att = mm(w_out_all, grad_attn, nt).astype(bf16).reshape(size, -1, own)
    pieces = [(lax.dynamic_index_in_dim(grad_att, member, 0, keepdims=False), 0)]
    for j in range(1, size):
        out = lax.dynamic_index_in_dim(grad_att, (member + j) % size, 0, keepdims=False)
        pieces.append((lax.ppermute(out, axes, team.rotate(j)), (-j) % size))
    pieces.sort(key=lambda item: item[1])
    grad_heads = jnp.concatenate([piece for piece, _ in pieces], axis=1)

    def by_core(grad):
        parts = grad.astype(bf16).reshape(team.rows, 2, rows_here, width)
        keep = lax.dynamic_index_in_dim(parts, core, 1, keepdims=False)
        send = lax.dynamic_index_in_dim(parts, 1 - core, 1, keepdims=False)
        return keep, lax.ppermute(send, "dp", team.swap_core())

    three = [
        by_core(grad)
        for grad in (mm(activated, cot_own, tn), mm(normed_mid, grad_pre, tn), mm(att_own, grad_attn))
    ]

    def both_cores(step):
        at = (row + step) % team.rows
        return jnp.concatenate(
            [
                lax.dynamic_index_in_dim(keep, at, 0, keepdims=False).astype(f32)
                + lax.dynamic_index_in_dim(got, at, 0, keepdims=False).astype(f32)
                for keep, got in three
            ]
        ).astype(bf16)

    three_rows = [both_cores(step) for step in range(team.rows)]
    three_far = [
        lax.ppermute(three_rows[step], "dp", team.turn_rows(step)) for step in range(1, team.rows)
    ]

    def add(first, *more):
        total = first.astype(f32)
        for piece in more:
            total = total + piece.astype(f32)
        return total.astype(bf16)

    pair = math.gcd(local_heads, 4)
    grad_in = after(grad_heads, *three_rows)
    chunks, dots, heads_of = [], 0.0, []
    steps = None
    for c in range(local_heads // pair):
        grads, dot = attend_back(
            c, pair, table, qkv, att, grad_in, lse, starts, factor[:, None]
        )
        chunks.append(grads)
        dots = dots + dot
        if c == 0:
            result = after(result, grads)
            grads = after(grads, *result)
        else:
            if steps is None:
                three_far = after(three_far, grads)
                steps = reduce_places(add(three_rows[0], *three_far), team.seq)
            grads = after(grads, next(steps))
        send, keep = head_grad(grads, normed_in, team.rows, row, core)
        near = [lax.ppermute(piece, "dp", team.swap_core()) for piece in send]
        far = [
            [
                lax.ppermute(source, "dp", team.turn_rows(step))
                for source in (keep[step], near[step])
            ]
            for step in range(1, team.rows)
        ]
        heads_of.append((keep[0], near[0], far))
        grad_in = after(grad_in, *send, *keep)
    steps = steps or reduce_places(add(three_rows[0], *three_far), team.seq)
    blocks = own // span
    chunks = after(chunks, *send, *keep)
    partial = [
        input_side(chunks, w_half, span, j * blocks, blocks) for j in range(1, size)
    ]
    chunks = after(chunks, *partial)
    grad_normed_in = sum(
        [
            lax.ppermute(p, axes, team.rotate(j + 1)).astype(f32)
            for j, p in enumerate(partial)
        ],
        input_side(chunks, w_half, span, 0, blocks).astype(f32),
    )
    rms_in = lax.rsqrt(jnp.mean(x_float * x_float, axis=-1, keepdims=True) + epsilon)
    grad_gain_in = jnp.sum(grad_normed_in * x_float * rms_in, axis=0)
    scaled_in = grad_normed_in * gain_in
    input_grad_own = grad_mid + rms_in * (
        scaled_in
        - x_float * rms_in * rms_in * jnp.mean(scaled_in * x_float, axis=-1, keepdims=True)
    )
    input_grad = unspread_done(unspread(input_grad_own.astype(bf16)), f32)
    result = unspread_done(result, bf16)

    three = last(steps).astype(f32)
    part_out, part_up, part_down = (
        three[i * rows_here : (i + 1) * rows_here] for i in (2, 1, 0)
    )
    full = []
    for mine, theirs, far in heads_of:
        total = jnp.concatenate(
            [add(mine, *[f[0] for f in far]), add(theirs, *[f[1] for f in far])]
        )
        total = place_in([(total, member // 2)], team.half) if team.half > 1 else total
        full.append(last(reduce_places(total.reshape(-1, total.shape[-1]), team.seq)))
    full = unfold(full, team.half, rows_here, core).reshape(heads, 3, head_size, rows_here)
    vectors = sum_everywhere(
        team,
        jnp.concatenate([grad_gain_in, grad_gain_mid, grad_bias_up, grad_bias_down, dots[:, 0]]),
    )
    d = lax.axis_index("dp")

    def slice_of(i):
        return lax.dynamic_slice_in_dim(vectors, i * width + d * rows_here, rows_here, 0)

    grad_scale = vectors[4 * width :] / (factor * log2e) * (
        scale_base / math.sqrt(head_size)
    ) * jax.nn.sigmoid(per_dim_scale)
    return (
        result,
        input_grad,
        slice_of(0),
        full.transpose(3, 0, 1, 2),
        grad_scale,
        part_out,
        slice_of(1),
        part_up,
        slice_of(2),
        part_down,
        slice_of(3),
    )


def solution(mesh):
    in_specs = (
        P("dp", "seq", None),
        P("dp", None),
        P("dp"),
        P("dp", None, None, None),
        P(),
        P("dp", None),
        P("dp"),
        P("dp", None),
        P("dp"),
        P("dp", None),
        P("dp"),
        P("dp", "seq", None),
    )
    out_specs = (
        P("dp", "seq", None),
        P("dp", "seq", None),
        P("dp"),
        P("dp", None, None, None),
        P(),
        P("dp", None),
        P("dp"),
        P("dp", None),
        P("dp"),
        P("dp", None),
        P("dp"),
    )
    return jax.shard_map(
        on_device, mesh=mesh, in_specs=in_specs, out_specs=out_specs, check_vma=False
    )
```

```python
import functools
import math

import jax
import jax.numpy as jnp
from jax import lax
from jax.experimental import pallas as pl
from jax.experimental.pallas import tpu as pltpu
from jax.sharding import PartitionSpec as P

epsilon = 1e-06
scale_base = 1.442695041
log2e = 1.4426950408889634
masked_value = -1e30
score_limit = 100.0
bf16 = jnp.bfloat16
f32 = jnp.float32
axes = ("dp", "seq")
brief = pl.CostEstimate(flops=1, bytes_accessed=1, transcendentals=0)
nt = (((1,), (1,)), ((), ()))
nn = (((1,), (0,)), ((), ()))


def mm(a, b, dims=nn):
    return lax.dot_general(a, b, dims, preferred_element_type=f32)


class Team:
    def __init__(self, dp, seq, seqs):
        self.dp, self.seq, self.seqs = dp, seq, seqs
        self.size = seq // seqs
        assert seq % seqs == 0 and self.size % 2 == 0 and dp % 2 == 0
        self.half = self.size // 2
        self.rows = dp // 2

    def places(self):
        for row in range(self.rows):
            for core in range(2):
                for place in range(self.seq):
                    yield row, core, place

    def rank(self, row, core, place):
        return (row * 2 + core) * self.seq + place

    def here(self):
        d = lax.axis_index("dp")
        p = lax.axis_index("seq")
        row, core = d // 2, d % 2
        group = p // self.size
        side = (p % self.size) // self.half
        member = (p % self.half) * 2 + core
        return row, core, group, side, member

    def spread(self, step):
        pairs = []
        for row, core, place in self.places():
            z, u = place // self.size, place % self.size
            s = (z + step) % self.seqs
            pairs.append(
                (
                    self.rank(row, core, place),
                    self.rank(row, u % 2, s * self.size + core * self.half + u // 2),
                )
            )
        return pairs

    def back(self, step):
        return [(b, a) for a, b in self.spread(step)]

    def rotate(self, step):
        pairs = []
        for row, core, place in self.places():
            base = place - place % self.half
            m = (place % self.half) * 2 + core
            to = (m + step) % self.size
            pairs.append((self.rank(row, core, place), self.rank(row, to % 2, base + to // 2)))
        return pairs

    def swap_core(self):
        return [(d, d ^ 1) for d in range(self.dp)]

    def turn_rows(self, step, flip=0):
        return [(d, ((d + 2 * step) % self.dp) ^ flip) for d in range(self.dp)]


def after(value, *first):
    return lax.optimization_barrier((value, first))[0]


def place_in(pieces, count):
    first = pieces[0][0]
    out = jnp.zeros((count,) + first.shape, first.dtype)
    for piece, index in pieces:
        out = lax.dynamic_update_index_in_dim(out, piece, index, 0)
    return out


def join_kernel(count, ends, slots_ref, *refs):
    outs = refs[count:]
    for k in range(count):
        start = 0
        for out_ref, end in zip(outs, ends):
            out_ref[slots_ref[k]] = refs[k][start:end, :].astype(out_ref.dtype)
            start = end


def join(pieces, slots, ends=None, dtype=None):
    count = len(pieces)
    rows, columns = pieces[0].shape
    dtype = dtype or pieces[0].dtype
    ends = ends or (rows,)
    heights = [b - a for a, b in zip((0,) + tuple(ends[:-1]), ends)]
    wide = columns
    if columns % 128 == 0:
        wide = max(b for b in range(128, min(columns, 640) + 1, 128) if columns % b == 0)
    outs = pl.pallas_call(
        functools.partial(join_kernel, count, ends),
        grid_spec=pltpu.PrefetchScalarGridSpec(
            num_scalar_prefetch=1,
            grid=(columns // wide,),
            in_specs=[pl.BlockSpec((rows, wide), lambda i, s: (0, i)) for _ in pieces],
            out_specs=[pl.BlockSpec((count, h, wide), lambda i, s: (0, 0, i)) for h in heights],
        ),
        out_shape=[jax.ShapeDtypeStruct((count, h, columns), dtype) for h in heights],
        compiler_params=pltpu.CompilerParams(vmem_limit_bytes=56 << 20),
        cost_estimate=brief,
        name="join",
    )(jnp.stack(slots).astype(jnp.int32), *pieces)
    return outs if len(ends) > 1 else outs[0]


def qkv_kernel(count, blocks, parts, head_size, *refs):
    x_refs = refs[:count]
    gain_ref, w_ref, factor_ref, out_ref, normed_ref = refs[count:]
    i = pl.program_id(0)
    x = x_refs[0][...]
    for j in range(1, count):
        x = jnp.where(i >= j * blocks, x_refs[j][...], x)
    x = x.astype(f32)
    rms = lax.rsqrt(jnp.mean(x * x, axis=-1, keepdims=True) + epsilon)
    normed = (x * rms * gain_ref[...]).astype(bf16)
    part = x.shape[1] // parts
    for d in range(parts):
        normed_ref[d % 2, :, d // 2 * part : (d // 2 + 1) * part] = normed[
            :, d * part : (d + 1) * part
        ]
    packed = (mm(normed, w_ref[...]) * factor_ref[...]).astype(bf16)
    for h in range(packed.shape[1] // head_size):
        out_ref[h // 3, h % 3] = packed[:, h * head_size : (h + 1) * head_size]


def project_qkv(xs, gain, w, factor_row, heads, head_size, parts, block):
    own, width = xs[0].shape
    count, blocks = len(xs), own // block
    tokens = own * count
    wide = w.shape[1]

    def x_spec(j):
        return pl.BlockSpec(
            (block, width), lambda i: (jnp.clip(i - j * blocks, 0, blocks - 1), 0)
        )

    return pl.pallas_call(
        functools.partial(qkv_kernel, count, blocks, parts, head_size),
        grid=(tokens // block,),
        in_specs=[x_spec(j) for j in range(count)]
        + [
            pl.BlockSpec((1, width), lambda i: (0, 0)),
            pl.BlockSpec((width, wide), lambda i: (0, 0)),
            pl.BlockSpec((1, wide), lambda i: (0, 0)),
        ],
        out_specs=[
            pl.BlockSpec((heads, 3, block, head_size), lambda i: (0, 0, i, 0)),
            pl.BlockSpec((2, block, width // 2), lambda i: (0, i, 0)),
        ],
        out_shape=[
            jax.ShapeDtypeStruct((heads, 3, tokens, head_size), bf16),
            jax.ShapeDtypeStruct((2, tokens, width // 2), bf16),
        ],
        compiler_params=pltpu.CompilerParams(vmem_limit_bytes=56 << 20),
        cost_estimate=brief,
        name="qkv",
    )(*xs, gain, w, factor_row)


def head_grad_kernel(rows, fold, place_ref, grads_ref, normed_ref, *out_refs):
    result = mm(grads_ref[...], normed_ref[0]).astype(bf16)
    part = result.shape[1] // rows
    lines = result.shape[0] // fold
    for side in range(2):
        for row in range(rows):

            @pl.when((pl.program_id(0) == side) & (place_ref[2] == row))
            def store(side=side, row=row):
                for step in range(rows):
                    at = (row + step) % rows * part
                    for k in range(fold):
                        out_refs[side * rows + step][:, k * part : (k + 1) * part] = result[
                            k * lines : (k + 1) * lines, at : at + part
                        ]


def head_grad(grads, normed, rows, row, core):
    _, tokens, width = normed.shape
    lines = grads.shape[0]
    part = width // rows
    fold = 128 // math.gcd(part, 128)
    shape = (lines // fold, fold * part)
    outs = pl.pallas_call(
        functools.partial(head_grad_kernel, rows, fold),
        grid_spec=pltpu.PrefetchScalarGridSpec(
            num_scalar_prefetch=1,
            grid=(2,),
            in_specs=[
                pl.BlockSpec((lines, tokens), lambda i, o: (0, 0)),
                pl.BlockSpec((1, tokens, width), lambda i, o: (o[i], 0, 0)),
            ],
            out_specs=[pl.BlockSpec(shape, lambda i, o: (0, 0)) for _ in range(2 * rows)],
        ),
        out_shape=[jax.ShapeDtypeStruct(shape, bf16) for _ in range(2 * rows)],
        compiler_params=pltpu.CompilerParams(vmem_limit_bytes=56 << 20),
        cost_estimate=brief,
        name="head_grad",
    )(jnp.stack([1 - core, core, row]).astype(jnp.int32), grads, normed)
    return outs[:rows], outs[rows:]


def unfold_kernel(count, fold, core_ref, *refs):
    out_ref = refs[count]
    part = out_ref.shape[1]
    lines = out_ref.shape[0] // fold
    for c in range(count):

        @pl.when(pl.program_id(0) % count == c)
        def store(c=c):
            for k in range(fold):
                out_ref[k * lines : (k + 1) * lines, :] = refs[c][
                    :, k * part : (k + 1) * part
                ].astype(f32)


def unfold(chunks, groups, part, core):
    count = len(chunks)
    lines = chunks[0].shape[0] // (2 * groups)
    wide = chunks[0].shape[1]
    fold = wide // part

    def source(i, o):
        g = i // count
        return (g // 2 * 2 + (g % 2 + o[0]) % 2, 0)

    return pl.pallas_call(
        functools.partial(unfold_kernel, count, fold),
        grid_spec=pltpu.PrefetchScalarGridSpec(
            num_scalar_prefetch=1,
            grid=(2 * groups * count,),
            in_specs=[pl.BlockSpec((lines, wide), source) for _ in chunks],
            out_specs=pl.BlockSpec((lines * fold, part), lambda i, o: (i, 0)),
        ),
        out_shape=jax.ShapeDtypeStruct((2 * groups * count * lines * fold, part), f32),
        compiler_params=pltpu.CompilerParams(vmem_limit_bytes=56 << 20),
        cost_estimate=brief,
        name="unfold",
    )(core.reshape(1).astype(jnp.int32), *chunks)


def eye_rows(rows, columns):
    a = lax.broadcasted_iota(jnp.int32, (rows, columns), 0)
    b = lax.broadcasted_iota(jnp.int32, (rows, columns), 1)
    return (a == b).astype(bf16)


def attend_kernel(count, block, pair, table, qkv_ref, start_ref, att_ref, lse_ref, vt_ref, acc_ref):
    size = qkv_ref.shape[3]
    rows = vt_ref.shape[1]
    unit = eye_rows(rows, size)
    one_row = (lax.broadcasted_iota(jnp.int32, (rows, block), 0) == size).astype(f32)
    for h in range(pair):
        for b in range(count):
            here = slice(b * block, (b + 1) * block)
            vt_ref[h, :, here] = (mm(unit, qkv_ref[h, 2, here, :], nt) + one_row).astype(bf16)
    key_index = lax.broadcasted_iota(jnp.int32, (block, block), 0)
    lane_index = lax.broadcasted_iota(jnp.int32, (1, block), 1)
    ones = jnp.ones((8, size), bf16)

    def longest(part):
        best = jnp.zeros((8, block), f32)
        for h in range(pair):
            for b in range(count):
                x = qkv_ref[h, part, b * block : (b + 1) * block, :]
                best = jnp.maximum(best, mm(ones, x * x, nt))
        return jnp.max(best)

    small = longest(0) * longest(1) * 1.1 < score_limit * score_limit

    def query_block(raised, i, carry):
        at = pl.multiple_of(table[0, i] * block, block)
        starts = start_ref[pl.ds(i, 1), :]
        places = lane_index + i * block
        queries = [qkv_ref[h, 0, pl.ds(at, block), :] for h in range(pair)]
        acc_ref[...] = jnp.zeros_like(acc_ref)

        def step(masked, j, peaks):
            key_at = pl.multiple_of(table[0, j] * block, block)
            if masked:
                keys_here = key_index + j * block
                seen = (keys_here >= starts) & (keys_here <= places)
            scores = [
                mm(qkv_ref[h, 1, pl.ds(key_at, block), :], queries[h], nt) for h in range(pair)
            ]
            if masked:
                scores = [jnp.where(seen, s, masked_value) for s in scores]
            values = [vt_ref[h, :, pl.ds(key_at, block)] for h in range(pair)]
            if not raised:
                probs = [jnp.exp2(s).astype(bf16) for s in scores]
                sums = [mm(values[h], probs[h]) for h in range(pair)]
                for h in range(pair):
                    acc_ref[h] += sums[h]
                return ()
            out = []
            for h in range(pair):
                peak = jnp.maximum(peaks[h], jnp.max(scores[h], axis=0, keepdims=True))
                p = jnp.exp2(scores[h] - peak).astype(bf16)
                acc_ref[h] = acc_ref[h] * jnp.exp2(peaks[h] - peak) + mm(values[h], p)
                out.append(peak)
            return tuple(out)

        peaks = ()
        if raised:
            peaks = tuple(jnp.full((1, block), masked_value, f32) for _ in range(pair))
        peaks = lax.fori_loop(table[1, i], table[2, i], functools.partial(step, True), peaks)
        peaks = lax.fori_loop(table[2, i], i, functools.partial(step, False), peaks)
        peaks = step(True, i, peaks)
        for h in range(pair):
            total = acc_ref[h, size : size + 1, :]
            att_ref[h * size : (h + 1) * size, pl.ds(at, block)] = (
                acc_ref[h, :size, :] / total
            ).astype(bf16)
            low = jnp.log2(total)
            lse_ref[h, :, pl.ds(at, block)] = peaks[h] + low if raised else low
        return carry

    @pl.when(small)
    def plain():
        lax.fori_loop(0, count, functools.partial(query_block, False), 0)

    @pl.when(jnp.logical_not(small))
    def careful():
        lax.fori_loop(0, count, functools.partial(query_block, True), 0)


def attend(table, qkv, starts):
    heads, _, length, size = qkv.shape
    pair = math.gcd(heads, 8)
    count, block = starts.shape
    rows = (size // 16 + 1) * 16
    return pl.pallas_call(
        functools.partial(attend_kernel, count, block, pair),
        grid_spec=pltpu.PrefetchScalarGridSpec(
            num_scalar_prefetch=1,
            grid=(heads // pair,),
            in_specs=[
                pl.BlockSpec((pair, 3, length, size), lambda g, t: (g, 0, 0, 0)),
                pl.BlockSpec((count, block), lambda g, t: (0, 0)),
            ],
            out_specs=[
                pl.BlockSpec((pair * size, length), lambda g, t: (g, 0)),
                pl.BlockSpec((pair, 1, length), lambda g, t: (g, 0, 0)),
            ],
            scratch_shapes=[
                pltpu.VMEM((pair, rows, length), bf16),
                pltpu.VMEM((pair, rows, block), f32),
            ],
        ),
        out_shape=[
            jax.ShapeDtypeStruct((heads * size, length), bf16),
            jax.ShapeDtypeStruct((heads, 1, length), f32),
        ],
        compiler_params=pltpu.CompilerParams(vmem_limit_bytes=56 << 20),
        cost_estimate=brief,
        name="attend",
    )(table, qkv, starts)


def attend_back_kernel(
    count,
    block,
    pair,
    table,
    qkv_ref,
    att_ref,
    grad_ref,
    lse_ref,
    start_ref,
    factor_ref,
    out_ref,
    dots_ref,
    qt_ref,
    kt_ref,
    delta_ref,
    dq_ref,
    dk_ref,
    dv_ref,
):
    size = qkv_ref.shape[3]
    unit = eye_rows(size, size)
    for h in range(pair):
        for b in range(count):
            here = slice(b * block, (b + 1) * block)
            qt_ref[h, :, here] = mm(unit, qkv_ref[h, 0, here, :], nt).astype(bf16)
            kt_ref[h, :, here] = mm(unit, qkv_ref[h, 1, here, :], nt).astype(bf16)
        rows = slice(h * size, (h + 1) * size)
        delta_ref[h] = jnp.sum(
            att_ref[rows, :].astype(f32) * grad_ref[rows, :].astype(f32), axis=0, keepdims=True
        )
    dq_ref[...] = jnp.zeros_like(dq_ref)
    key_index = lax.broadcasted_iota(jnp.int32, (block, block), 0)
    lane_index = lax.broadcasted_iota(jnp.int32, (1, block), 1)

    def key_block(j, carry):
        key_at = pl.multiple_of(table[0, j] * block, block)
        keys_here = key_index + j * block
        dk_ref[...] = jnp.zeros_like(dk_ref)
        dv_ref[...] = jnp.zeros_like(dv_ref)

        def step(masked, i, inner):
            at = pl.multiple_of(table[0, i] * block, block)
            if masked:
                seen = (keys_here >= start_ref[pl.ds(i, 1), :]) & (
                    keys_here <= lane_index + i * block
                )
            both = range(pair)
            grads = [grad_ref[h * size : (h + 1) * size, pl.ds(at, block)] for h in both]
            queries = [qt_ref[h, :, pl.ds(at, block)] for h in both]
            s = [mm(qkv_ref[h, 1, pl.ds(key_at, block), :], queries[h]) for h in both]
            dp = [mm(qkv_ref[h, 2, pl.ds(key_at, block), :], grads[h]) for h in both]
            p = [jnp.exp2(s[h] - lse_ref[h, :, pl.ds(at, block)]) for h in both]
            if masked:
                p = [jnp.where(seen, x, 0.0) for x in p]
            ds = [
                (p[h] * (dp[h] - delta_ref[h, :, pl.ds(at, block)])).astype(bf16) for h in both
            ]
            dv = [mm(grads[h], p[h].astype(bf16), nt) for h in both]
            dk = [mm(queries[h], ds[h], nt) for h in both]
            dq = [mm(kt_ref[h, :, pl.ds(key_at, block)], ds[h]) for h in both]
            for h in both:
                dv_ref[h] += dv[h]
                dk_ref[h] += dk[h]
                dq_ref[h, :, pl.ds(at, block)] += dq[h]
            return inner

        step(True, j, 0)
        lax.fori_loop(j + 1, table[3, j], functools.partial(step, False), 0)
        lax.fori_loop(table[3, j], table[4, j], functools.partial(step, True), 0)
        for h in range(pair):
            base = h * 3 * size
            out_ref[base + size : base + 2 * size, pl.ds(key_at, block)] = (
                dk_ref[h] * (1.0 / log2e)
            ).astype(bf16)
            out_ref[base + 2 * size : base + 3 * size, pl.ds(key_at, block)] = dv_ref[h].astype(bf16)
        return carry

    lax.fori_loop(0, count, key_block, 0)

    @pl.when(pl.program_id(0) == 0)
    def clear():
        dots_ref[...] = jnp.zeros_like(dots_ref)

    for h in range(pair):
        base = h * 3 * size
        rounded = dq_ref[h].astype(bf16).astype(f32)
        dots_ref[...] += jnp.sum(qt_ref[h].astype(f32) * rounded, axis=1, keepdims=True)
        out_ref[base : base + size, :] = (rounded * factor_ref[...]).astype(bf16)


def attend_back(chunk, pair, table, qkv, att, grad, lse, starts, factor):
    heads, _, length, size = qkv.shape
    count, block = starts.shape
    return pl.pallas_call(
        functools.partial(attend_back_kernel, count, block, pair),
        grid_spec=pltpu.PrefetchScalarGridSpec(
            num_scalar_prefetch=1,
            grid=(1,),
            in_specs=[
                pl.BlockSpec((pair, 3, length, size), lambda g, t: (chunk, 0, 0, 0)),
                pl.BlockSpec((pair * size, length), lambda g, t: (chunk, 0)),
                pl.BlockSpec((pair * size, length), lambda g, t: (chunk, 0)),
                pl.BlockSpec((pair, 1, length), lambda g, t: (chunk, 0, 0)),
                pl.BlockSpec((count, block), lambda g, t: (0, 0)),
                pl.BlockSpec((size, 1), lambda g, t: (0, 0)),
            ],
            out_specs=[
                pl.BlockSpec((pair * 3 * size, length), lambda g, t: (0, 0)),
                pl.BlockSpec((size, 1), lambda g, t: (0, 0)),
            ],
            scratch_shapes=[
                pltpu.VMEM((pair, size, length), bf16),
                pltpu.VMEM((pair, size, length), bf16),
                pltpu.VMEM((pair, 1, length), f32),
                pltpu.VMEM((pair, size, length), f32),
                pltpu.VMEM((pair, size, block), f32),
                pltpu.VMEM((pair, size, block), f32),
            ],
        ),
        out_shape=[
            jax.ShapeDtypeStruct((pair * 3 * size, length), bf16),
            jax.ShapeDtypeStruct((size, 1), f32),
        ],
        compiler_params=pltpu.CompilerParams(vmem_limit_bytes=56 << 20),
        cost_estimate=brief,
        name="attend_back",
    )(table, qkv, att, grad, lse, starts, factor)


def input_side_kernel(count, *refs):
    w_ref, out_ref = refs[count], refs[count + 1]
    grads = jnp.concatenate([ref[...] for ref in refs[:count]], axis=0)
    out_ref[...] = mm(grads.T, w_ref[...], nt).astype(bf16)


def input_side(grads, w, block, first, blocks):
    width, wide = w.shape
    rows = grads[0].shape[0]
    tokens = blocks * block
    return pl.pallas_call(
        functools.partial(input_side_kernel, len(grads)),
        grid=(blocks,),
        in_specs=[pl.BlockSpec((rows, block), lambda i: (0, i + first)) for _ in grads]
        + [pl.BlockSpec((width, wide), lambda i: (0, 0))],
        out_specs=pl.BlockSpec((block, width), lambda i: (i, 0)),
        out_shape=jax.ShapeDtypeStruct((tokens, width), bf16),
        compiler_params=pltpu.CompilerParams(vmem_limit_bytes=56 << 20),
        cost_estimate=pl.CostEstimate(
            flops=4 * tokens * width * wide, bytes_accessed=1, transcendentals=0
        ),
        name="input_side",
    )(*grads, w)


def reduce_places(buf, places):
    place = lax.axis_index("seq")
    lines, wide = buf.shape
    bits = places.bit_length() - 1
    assert places == 1 << bits and lines % places == 0
    for b in range(bits):
        bit = (place >> b) & 1
        halves = buf.reshape(2, -1, wide)
        keep = lax.dynamic_index_in_dim(halves, bit, 0, keepdims=False)
        send = lax.dynamic_index_in_dim(halves, 1 - bit, 0, keepdims=False)
        yield send
        got = lax.ppermute(send, "seq", [(i, i ^ (1 << b)) for i in range(places)])
        buf = (keep.astype(f32) + got.astype(f32)).astype(bf16)
    for b in reversed(range(bits)):
        bit = (place >> b) & 1
        yield buf
        got = lax.ppermute(buf, "seq", [(i, i ^ (1 << b)) for i in range(places)])
        buf = jnp.where(
            bit == 0, jnp.concatenate([buf, got], axis=0), jnp.concatenate([got, buf], axis=0)
        )
    yield buf


def last(steps):
    for value in steps:
        pass
    return value


def sum_everywhere(team, vector):
    vector = vector + lax.ppermute(vector, "dp", team.swap_core())
    total = vector
    for step in range(1, team.rows):
        total = total + lax.ppermute(vector, "dp", team.turn_rows(step))
    for b in range(team.seq.bit_length() - 1):
        total = total + lax.ppermute(
            total, "seq", [(i, i ^ (1 << b)) for i in range(team.seq)]
        )
    return total


def on_device(
    activations,
    segment_ids,
    norm1_gain,
    w_qkv,
    per_dim_scale,
    w_out,
    norm2_gain,
    w_up,
    b_up,
    w_down,
    b_down,
    cotangent,
):
    seqs, span, width = activations.shape
    rows_here, heads, _, head_size = w_qkv.shape
    length = segment_ids.shape[1]
    team = Team(lax.axis_size("dp"), lax.axis_size("seq"), seqs)
    size = team.size
    row, core, group, side, member = team.here()
    local_heads = heads // size
    wide = local_heads * 3 * head_size
    own = seqs * span

    def spread(array, *near):
        out = []
        for step in range(seqs):
            source = after(array, *near) if near and step < seqs // 2 else array
            block = lax.dynamic_index_in_dim(source, (group + step) % seqs, 0, keepdims=False)
            out.append(lax.ppermute(block, axes, team.spread(step)))
        return out

    def spread_done(pieces):
        return join(pieces, [jnp.int32(k) for k in range(seqs)]).reshape(own, width)

    def unspread(array):
        return [
            lax.ppermute(array[step * span : (step + 1) * span], axes, team.back(step))
            for step in range(seqs)
        ]

    def unspread_done(pieces, dtype):
        return join(pieces, [(group + step) % seqs for step in range(seqs)], dtype=dtype)

    def shard_of(step, flip):
        return (row - step) % team.rows * 2 + (core ^ flip)

    shifts = [(step, flip) for step in range(team.rows) for flip in range(2)]

    w_local = w_qkv.reshape(rows_here, heads * 3 * head_size)
    small = jnp.concatenate([norm1_gain, norm2_gain, b_up, b_down])
    small = jnp.pad(small, (0, wide * 16 - small.shape[0])).reshape(16, wide)

    def columns(first):
        part = lax.dynamic_slice_in_dim(w_local, first * wide, wide, 1)
        return jnp.concatenate([part, small], axis=0)

    parts = [columns(member), columns(member + 1 - 2 * core)]
    far = [
        lax.ppermute(parts[flip], "dp", team.turn_rows(step, flip)) for step, flip in shifts[2:]
    ]
    near = lax.ppermute(parts[1], "dp", team.swap_core())
    x_own = spread_done(spread(after(activations, *parts), near))
    other_ids = lax.ppermute(segment_ids, "dp", team.swap_core())
    w_half, small = join(
        [parts[0], near] + far,
        [shard_of(*s) for s in shifts],
        ends=(rows_here, rows_here + 16),
    )
    w_half = w_half.reshape(width, wide)
    small = small.reshape(team.dp, -1)[:, : 4 * rows_here]
    small = small.reshape(team.dp, 4, rows_here).transpose(1, 0, 2).reshape(4, width).astype(f32)
    gain_in, gain_mid, bias_up, bias_down = (small[i : i + 1] for i in range(4))
    xs = [x_own] + [lax.ppermute(x_own, axes, team.rotate(-j)) for j in range(1, size)]
    three = after(jnp.concatenate([w_out, w_up, w_down]), *far)
    three = [three] + [
        lax.ppermute(three, "dp", team.turn_rows(step)) for step in range(1, team.rows)
    ]
    cot_own = spread(after(cotangent, x_own).astype(bf16))

    ids = lax.dynamic_index_in_dim(
        jnp.where(side == core, segment_ids, other_ids), group, 0, keepdims=False
    )
    starts = jnp.sum((ids[None, :] < ids[:, None]).astype(jnp.int32), axis=1)
    ends = jnp.sum((ids[None, :] <= ids[:, None]).astype(jnp.int32), axis=1) - 1
    count = length // span
    starts = starts.reshape(count, span)
    ends = ends.reshape(count, span)
    index = jnp.arange(count)
    z_of, u_of = index // size, index % size
    at = ((u_of - member) % size) * seqs + (group - z_of) % seqs
    first = starts[:, 0] // span
    last_start = starts[:, -1]
    open_from = jnp.minimum((last_start + span - 1) // span, index)
    open_to = jnp.sum((last_start[None, :] <= index[:, None] * span).astype(jnp.int32), axis=1)
    open_to = jnp.maximum(open_to, index + 1)
    stop = ends[:, -1] // span + 1
    table = jnp.stack([at, first, open_from, open_to, stop]).astype(jnp.int32)

    factor = scale_base / math.sqrt(head_size) * jax.nn.softplus(per_dim_scale)
    unit = jnp.ones((head_size,), f32)
    factor_row = jnp.tile(jnp.concatenate([factor * log2e, unit, unit]), local_heads)[None, :]

    qkv, normed_in = project_qkv(
        xs, gain_in, w_half, factor_row, local_heads, head_size, team.dp, span
    )
    early = seqs // 2
    qkv, cot_own[early:] = after((qkv, cot_own[early:]), *cot_own[early:])
    att, lse = attend(table, qkv, starts)
    three = after(three, att)
    swapped = [lax.ppermute(piece, "dp", team.swap_core()) for piece in three]
    w_out_all, w_up_all, w_down_all = (
        w.reshape(-1, width)
        for w in join(
            three + swapped,
            [shard_of(step, 0) for step in range(team.rows)]
            + [shard_of(step, 1) for step in range(team.rows)],
            ends=(rows_here, 2 * rows_here, 3 * rows_here),
        )
    )

    pieces = [(att[:, :own], member)]
    for j in range(1, size):
        got = lax.ppermute(att[:, j * own : (j + 1) * own], axes, team.rotate(j))
        pieces.append((got, (member - j) % size))
    att_own = join([p for p, _ in pieces], [s for _, s in pieces])
    att_own = att_own.reshape(heads * head_size, own)

    x_float = x_own.astype(f32)
    mid = x_float + lax.dot_general(
        att_own, w_out_all, (((0,), (0,)), ((), ())), preferred_element_type=f32
    )
    rms_mid = lax.rsqrt(jnp.mean(mid * mid, axis=-1, keepdims=True) + epsilon)
    normed_mid = (mid * rms_mid * gain_mid).astype(bf16)
    pre_act = mm(normed_mid, w_up_all) + bias_up
    activated = jax.nn.silu(pre_act).astype(bf16)
    result_own = (mid + mm(activated, w_down_all) + bias_down).astype(bf16)
    result = unspread(result_own)
    cot_own = spread_done(after(cot_own, result_own))

    grad_bias_down = jnp.sum(cot_own.astype(f32), axis=0)
    tn = (((0,), (0,)), ((), ()))
    grad_act = mm(cot_own, w_down_all, nt)
    sig = jax.nn.sigmoid(pre_act)
    grad_pre = (grad_act * sig * (1.0 + pre_act * (1.0 - sig))).astype(bf16)
    grad_bias_up = jnp.sum(grad_pre.astype(f32), axis=0)
    grad_normed_mid = mm(grad_pre, w_up_all, nt)
    grad_gain_mid = jnp.sum(grad_normed_mid * mid * rms_mid, axis=0)
    scaled_mid = grad_normed_mid * gain_mid
    grad_mid = cot_own.astype(f32) + rms_mid * (
        scaled_mid - mid * rms_mid * rms_mid * jnp.mean(scaled_mid * mid, axis=-1, keepdims=True)
    )
    grad_attn = grad_mid.astype(bf16)
    grad_att = mm(w_out_all, grad_attn, nt).astype(bf16).reshape(size, -1, own)
    pieces = [(lax.dynamic_index_in_dim(grad_att, member, 0, keepdims=False), 0)]
    for j in range(1, size):
        out = lax.dynamic_index_in_dim(grad_att, (member + j) % size, 0, keepdims=False)
        pieces.append((lax.ppermute(out, axes, team.rotate(j)), (-j) % size))
    pieces.sort(key=lambda item: item[1])
    grad_heads = jnp.concatenate([piece for piece, _ in pieces], axis=1)

    def by_core(grad):
        parts = grad.astype(bf16).reshape(team.rows, 2, rows_here, width)
        keep = lax.dynamic_index_in_dim(parts, core, 1, keepdims=False)
        send = lax.dynamic_index_in_dim(parts, 1 - core, 1, keepdims=False)
        return keep, lax.ppermute(send, "dp", team.swap_core())

    three = [
        by_core(grad)
        for grad in (mm(activated, cot_own, tn), mm(normed_mid, grad_pre, tn), mm(att_own, grad_attn))
    ]

    def both_cores(step):
        at = (row + step) % team.rows
        return jnp.concatenate(
            [
                lax.dynamic_index_in_dim(keep, at, 0, keepdims=False).astype(f32)
                + lax.dynamic_index_in_dim(got, at, 0, keepdims=False).astype(f32)
                for keep, got in three
            ]
        ).astype(bf16)

    three_rows = [both_cores(step) for step in range(team.rows)]
    three_far = [
        lax.ppermute(three_rows[step], "dp", team.turn_rows(step)) for step in range(1, team.rows)
    ]

    def add(first, *more):
        total = first.astype(f32)
        for piece in more:
            total = total + piece.astype(f32)
        return total.astype(bf16)

    pair = math.gcd(local_heads, 4)
    grad_in = after(grad_heads, *three_rows)
    chunks, dots, heads_of = [], 0.0, []
    steps = None
    for c in range(local_heads // pair):
        grads, dot = attend_back(
            c, pair, table, qkv, att, grad_in, lse, starts, factor[:, None]
        )
        chunks.append(grads)
        dots = dots + dot
        if c == 0:
            result = after(result, grads)
            grads = after(grads, *result)
        else:
            if steps is None:
                three_far = after(three_far, grads)
                steps = reduce_places(add(three_rows[0], *three_far), team.seq)
            grads = after(grads, next(steps))
        send, keep = head_grad(grads, normed_in, team.rows, row, core)
        near = [lax.ppermute(piece, "dp", team.swap_core()) for piece in send]
        far = [
            [
                lax.ppermute(source, "dp", team.turn_rows(step))
                for source in (keep[step], near[step])
            ]
            for step in range(1, team.rows)
        ]
        heads_of.append((keep[0], near[0], far))
        grad_in = after(grad_in, *send, *keep)
    steps = steps or reduce_places(add(three_rows[0], *three_far), team.seq)
    blocks = own // span
    chunks = after(chunks, *send, *keep)
    partial = [
        input_side(chunks, w_half, span, j * blocks, blocks) for j in range(1, size)
    ]
    chunks = after(chunks, *partial)
    heads_of = after(heads_of, *partial)
    grad_normed_in = sum(
        [
            lax.ppermute(p, axes, team.rotate(j + 1)).astype(f32)
            for j, p in enumerate(partial)
        ],
        input_side(chunks, w_half, span, 0, blocks).astype(f32),
    )
    rms_in = lax.rsqrt(jnp.mean(x_float * x_float, axis=-1, keepdims=True) + epsilon)
    grad_gain_in = jnp.sum(grad_normed_in * x_float * rms_in, axis=0)
    scaled_in = grad_normed_in * gain_in
    input_grad_own = grad_mid + rms_in * (
        scaled_in
        - x_float * rms_in * rms_in * jnp.mean(scaled_in * x_float, axis=-1, keepdims=True)
    )
    input_grad = unspread_done(unspread(input_grad_own.astype(bf16)), f32)
    result = unspread_done(result, bf16)

    three = last(steps).astype(f32)
    part_out, part_up, part_down = (
        three[i * rows_here : (i + 1) * rows_here] for i in (2, 1, 0)
    )
    full = []
    for mine, theirs, far in heads_of:
        total = jnp.concatenate(
            [add(mine, *[f[0] for f in far]), add(theirs, *[f[1] for f in far])]
        )
        total = place_in([(total, member // 2)], team.half) if team.half > 1 else total
        full.append(last(reduce_places(total.reshape(-1, total.shape[-1]), team.seq)))
    full = unfold(full, team.half, rows_here, core).reshape(heads, 3, head_size, rows_here)
    vectors = sum_everywhere(
        team,
        jnp.concatenate([grad_gain_in, grad_gain_mid, grad_bias_up, grad_bias_down, dots[:, 0]]),
    )
    d = lax.axis_index("dp")

    def slice_of(i):
        return lax.dynamic_slice_in_dim(vectors, i * width + d * rows_here, rows_here, 0)

    grad_scale = vectors[4 * width :] / (factor * log2e) * (
        scale_base / math.sqrt(head_size)
    ) * jax.nn.sigmoid(per_dim_scale)
    return (
        result,
        input_grad,
        slice_of(0),
        full.transpose(3, 0, 1, 2),
        grad_scale,
        part_out,
        slice_of(1),
        part_up,
        slice_of(2),
        part_down,
        slice_of(3),
    )


def solution(mesh):
    in_specs = (
        P("dp", "seq", None),
        P("dp", None),
        P("dp"),
        P("dp", None, None, None),
        P(),
        P("dp", None),
        P("dp"),
        P("dp", None),
        P("dp"),
        P("dp", None),
        P("dp"),
        P("dp", "seq", None),
    )
    out_specs = (
        P("dp", "seq", None),
        P("dp", "seq", None),
        P("dp"),
        P("dp", None, None, None),
        P(),
        P("dp", None),
        P("dp"),
        P("dp", None),
        P("dp"),
        P("dp", None),
        P("dp"),
    )
    return jax.shard_map(
        on_device, mesh=mesh, in_specs=in_specs, out_specs=out_specs, check_vma=False
    )
```

```python
import functools
import math

import jax
import jax.numpy as jnp
from jax import lax
from jax.experimental import pallas as pl
from jax.experimental.pallas import tpu as pltpu
from jax.sharding import PartitionSpec as P

epsilon = 1e-06
scale_base = 1.442695041
log2e = 1.4426950408889634
masked_value = -1e30
score_limit = 100.0
bf16 = jnp.bfloat16
f32 = jnp.float32
axes = ("dp", "seq")
brief = pl.CostEstimate(flops=1, bytes_accessed=1, transcendentals=0)
nt = (((1,), (1,)), ((), ()))
nn = (((1,), (0,)), ((), ()))


def mm(a, b, dims=nn):
    return lax.dot_general(a, b, dims, preferred_element_type=f32)


class Team:
    def __init__(self, dp, seq, seqs):
        self.dp, self.seq, self.seqs = dp, seq, seqs
        self.size = seq // seqs
        assert seq % seqs == 0 and self.size % 2 == 0 and dp % 2 == 0
        self.half = self.size // 2
        self.rows = dp // 2

    def places(self):
        for row in range(self.rows):
            for core in range(2):
                for place in range(self.seq):
                    yield row, core, place

    def rank(self, row, core, place):
        return (row * 2 + core) * self.seq + place

    def here(self):
        d = lax.axis_index("dp")
        p = lax.axis_index("seq")
        row, core = d // 2, d % 2
        group = p // self.size
        side = (p % self.size) // self.half
        member = (p % self.half) * 2 + core
        return row, core, group, side, member

    def spread(self, step):
        pairs = []
        for row, core, place in self.places():
            z, u = place // self.size, place % self.size
            s = (z + step) % self.seqs
            pairs.append(
                (
                    self.rank(row, core, place),
                    self.rank(row, u % 2, s * self.size + core * self.half + u // 2),
                )
            )
        return pairs

    def back(self, step):
        return [(b, a) for a, b in self.spread(step)]

    def rotate(self, step):
        pairs = []
        for row, core, place in self.places():
            base = place - place % self.half
            m = (place % self.half) * 2 + core
            to = (m + step) % self.size
            pairs.append((self.rank(row, core, place), self.rank(row, to % 2, base + to // 2)))
        return pairs

    def swap_core(self):
        return [(d, d ^ 1) for d in range(self.dp)]

    def turn_rows(self, step, flip=0):
        return [(d, ((d + 2 * step) % self.dp) ^ flip) for d in range(self.dp)]


def after(value, *first):
    return lax.optimization_barrier((value, first))[0]


def place_in(pieces, count):
    first = pieces[0][0]
    out = jnp.zeros((count,) + first.shape, first.dtype)
    for piece, index in pieces:
        out = lax.dynamic_update_index_in_dim(out, piece, index, 0)
    return out


def join_kernel(count, ends, slots_ref, *refs):
    outs = refs[count:]
    for k in range(count):
        start = 0
        for out_ref, end in zip(outs, ends):
            out_ref[slots_ref[k]] = refs[k][start:end, :].astype(out_ref.dtype)
            start = end


def join(pieces, slots, ends=None, dtype=None):
    count = len(pieces)
    rows, columns = pieces[0].shape
    dtype = dtype or pieces[0].dtype
    ends = ends or (rows,)
    heights = [b - a for a, b in zip((0,) + tuple(ends[:-1]), ends)]
    wide = columns
    if columns % 128 == 0:
        wide = max(b for b in range(128, min(columns, 640) + 1, 128) if columns % b == 0)
    outs = pl.pallas_call(
        functools.partial(join_kernel, count, ends),
        grid_spec=pltpu.PrefetchScalarGridSpec(
            num_scalar_prefetch=1,
            grid=(columns // wide,),
            in_specs=[pl.BlockSpec((rows, wide), lambda i, s: (0, i)) for _ in pieces],
            out_specs=[pl.BlockSpec((count, h, wide), lambda i, s: (0, 0, i)) for h in heights],
        ),
        out_shape=[jax.ShapeDtypeStruct((count, h, columns), dtype) for h in heights],
        compiler_params=pltpu.CompilerParams(vmem_limit_bytes=56 << 20),
        cost_estimate=brief,
        name="join",
    )(jnp.stack(slots).astype(jnp.int32), *pieces)
    return outs if len(ends) > 1 else outs[0]


def qkv_kernel(count, blocks, parts, head_size, *refs):
    x_refs = refs[:count]
    gain_ref, w_ref, factor_ref, out_ref, normed_ref = refs[count:]
    i = pl.program_id(0)
    x = x_refs[0][...]
    for j in range(1, count):
        x = jnp.where(i >= j * blocks, x_refs[j][...], x)
    x = x.astype(f32)
    rms = lax.rsqrt(jnp.mean(x * x, axis=-1, keepdims=True) + epsilon)
    normed = (x * rms * gain_ref[...]).astype(bf16)
    part = x.shape[1] // parts
    for d in range(parts):
        normed_ref[d % 2, :, d // 2 * part : (d // 2 + 1) * part] = normed[
            :, d * part : (d + 1) * part
        ]
    packed = (mm(normed, w_ref[...]) * factor_ref[...]).astype(bf16)
    for h in range(packed.shape[1] // head_size):
        out_ref[h // 3, h % 3] = packed[:, h * head_size : (h + 1) * head_size]


def project_qkv(xs, gain, w, factor_row, heads, head_size, parts, block):
    own, width = xs[0].shape
    count, blocks = len(xs), own // block
    tokens = own * count
    wide = w.shape[1]

    def x_spec(j):
        return pl.BlockSpec(
            (block, width), lambda i: (jnp.clip(i - j * blocks, 0, blocks - 1), 0)
        )

    return pl.pallas_call(
        functools.partial(qkv_kernel, count, blocks, parts, head_size),
        grid=(tokens // block,),
        in_specs=[x_spec(j) for j in range(count)]
        + [
            pl.BlockSpec((1, width), lambda i: (0, 0)),
            pl.BlockSpec((width, wide), lambda i: (0, 0)),
            pl.BlockSpec((1, wide), lambda i: (0, 0)),
        ],
        out_specs=[
            pl.BlockSpec((heads, 3, block, head_size), lambda i: (0, 0, i, 0)),
            pl.BlockSpec((2, block, width // 2), lambda i: (0, i, 0)),
        ],
        out_shape=[
            jax.ShapeDtypeStruct((heads, 3, tokens, head_size), bf16),
            jax.ShapeDtypeStruct((2, tokens, width // 2), bf16),
        ],
        compiler_params=pltpu.CompilerParams(vmem_limit_bytes=56 << 20),
        cost_estimate=brief,
        name="qkv",
    )(*xs, gain, w, factor_row)


def head_grad_kernel(rows, fold, place_ref, grads_ref, normed_ref, *out_refs):
    result = mm(grads_ref[...], normed_ref[0]).astype(bf16)
    part = result.shape[1] // rows
    lines = result.shape[0] // fold
    for side in range(2):
        for row in range(rows):

            @pl.when((pl.program_id(0) == side) & (place_ref[2] == row))
            def store(side=side, row=row):
                for step in range(rows):
                    at = (row + step) % rows * part
                    for k in range(fold):
                        out_refs[side * rows + step][:, k * part : (k + 1) * part] = result[
                            k * lines : (k + 1) * lines, at : at + part
                        ]


def head_grad(grads, normed, rows, row, core):
    _, tokens, width = normed.shape
    lines = grads.shape[0]
    part = width // rows
    fold = 128 // math.gcd(part, 128)
    shape = (lines // fold, fold * part)
    outs = pl.pallas_call(
        functools.partial(head_grad_kernel, rows, fold),
        grid_spec=pltpu.PrefetchScalarGridSpec(
            num_scalar_prefetch=1,
            grid=(2,),
            in_specs=[
                pl.BlockSpec((lines, tokens), lambda i, o: (0, 0)),
                pl.BlockSpec((1, tokens, width), lambda i, o: (o[i], 0, 0)),
            ],
            out_specs=[pl.BlockSpec(shape, lambda i, o: (0, 0)) for _ in range(2 * rows)],
        ),
        out_shape=[jax.ShapeDtypeStruct(shape, bf16) for _ in range(2 * rows)],
        compiler_params=pltpu.CompilerParams(vmem_limit_bytes=56 << 20),
        cost_estimate=brief,
        name="head_grad",
    )(jnp.stack([1 - core, core, row]).astype(jnp.int32), grads, normed)
    return outs[:rows], outs[rows:]


def unfold_kernel(count, fold, core_ref, *refs):
    out_ref = refs[count]
    part = out_ref.shape[1]
    lines = out_ref.shape[0] // fold
    for c in range(count):

        @pl.when(pl.program_id(0) % count == c)
        def store(c=c):
            for k in range(fold):
                out_ref[k * lines : (k + 1) * lines, :] = refs[c][
                    :, k * part : (k + 1) * part
                ].astype(f32)


def unfold(chunks, groups, part, core):
    count = len(chunks)
    lines = chunks[0].shape[0] // (2 * groups)
    wide = chunks[0].shape[1]
    fold = wide // part

    def source(i, o):
        g = i // count
        return (g // 2 * 2 + (g % 2 + o[0]) % 2, 0)

    return pl.pallas_call(
        functools.partial(unfold_kernel, count, fold),
        grid_spec=pltpu.PrefetchScalarGridSpec(
            num_scalar_prefetch=1,
            grid=(2 * groups * count,),
            in_specs=[pl.BlockSpec((lines, wide), source) for _ in chunks],
            out_specs=pl.BlockSpec((lines * fold, part), lambda i, o: (i, 0)),
        ),
        out_shape=jax.ShapeDtypeStruct((2 * groups * count * lines * fold, part), f32),
        compiler_params=pltpu.CompilerParams(vmem_limit_bytes=56 << 20),
        cost_estimate=brief,
        name="unfold",
    )(core.reshape(1).astype(jnp.int32), *chunks)


def eye_rows(rows, columns):
    a = lax.broadcasted_iota(jnp.int32, (rows, columns), 0)
    b = lax.broadcasted_iota(jnp.int32, (rows, columns), 1)
    return (a == b).astype(bf16)


def attend_kernel(count, block, pair, table, qkv_ref, start_ref, att_ref, lse_ref, vt_ref, acc_ref):
    size = qkv_ref.shape[3]
    rows = vt_ref.shape[1]
    unit = eye_rows(rows, size)
    one_row = (lax.broadcasted_iota(jnp.int32, (rows, block), 0) == size).astype(f32)
    for h in range(pair):
        for b in range(count):
            here = slice(b * block, (b + 1) * block)
            vt_ref[h, :, here] = (mm(unit, qkv_ref[h, 2, here, :], nt) + one_row).astype(bf16)
    key_index = lax.broadcasted_iota(jnp.int32, (block, block), 0)
    lane_index = lax.broadcasted_iota(jnp.int32, (1, block), 1)
    ones = jnp.ones((8, size), bf16)

    def longest(part):
        best = jnp.zeros((8, block), f32)
        for h in range(pair):
            for b in range(count):
                x = qkv_ref[h, part, b * block : (b + 1) * block, :]
                best = jnp.maximum(best, mm(ones, x * x, nt))
        return jnp.max(best)

    small = longest(0) * longest(1) * 1.1 < score_limit * score_limit

    def query_block(raised, i, carry):
        at = pl.multiple_of(table[0, i] * block, block)
        starts = start_ref[pl.ds(i, 1), :]
        places = lane_index + i * block
        queries = [qkv_ref[h, 0, pl.ds(at, block), :] for h in range(pair)]
        acc_ref[...] = jnp.zeros_like(acc_ref)

        def step(masked, j, peaks):
            key_at = pl.multiple_of(table[0, j] * block, block)
            if masked:
                keys_here = key_index + j * block
                seen = (keys_here >= starts) & (keys_here <= places)
            scores = [
                mm(qkv_ref[h, 1, pl.ds(key_at, block), :], queries[h], nt) for h in range(pair)
            ]
            if masked:
                scores = [jnp.where(seen, s, masked_value) for s in scores]
            values = [vt_ref[h, :, pl.ds(key_at, block)] for h in range(pair)]
            if not raised:
                probs = [jnp.exp2(s).astype(bf16) for s in scores]
                sums = [mm(values[h], probs[h]) for h in range(pair)]
                for h in range(pair):
                    acc_ref[h] += sums[h]
                return ()
            out = []
            for h in range(pair):
                peak = jnp.maximum(peaks[h], jnp.max(scores[h], axis=0, keepdims=True))
                p = jnp.exp2(scores[h] - peak).astype(bf16)
                acc_ref[h] = acc_ref[h] * jnp.exp2(peaks[h] - peak) + mm(values[h], p)
                out.append(peak)
            return tuple(out)

        peaks = ()
        if raised:
            peaks = tuple(jnp.full((1, block), masked_value, f32) for _ in range(pair))
        peaks = lax.fori_loop(table[1, i], table[2, i], functools.partial(step, True), peaks)
        peaks = lax.fori_loop(table[2, i], i, functools.partial(step, False), peaks)
        peaks = step(True, i, peaks)
        for h in range(pair):
            total = acc_ref[h, size : size + 1, :]
            att_ref[h * size : (h + 1) * size, pl.ds(at, block)] = (
                acc_ref[h, :size, :] / total
            ).astype(bf16)
            low = jnp.log2(total)
            lse_ref[h, :, pl.ds(at, block)] = peaks[h] + low if raised else low
        return carry

    @pl.when(small)
    def plain():
        lax.fori_loop(0, count, functools.partial(query_block, False), 0)

    @pl.when(jnp.logical_not(small))
    def careful():
        lax.fori_loop(0, count, functools.partial(query_block, True), 0)


def attend(table, qkv, starts):
    heads, _, length, size = qkv.shape
    pair = math.gcd(heads, 8)
    count, block = starts.shape
    rows = (size // 16 + 1) * 16
    return pl.pallas_call(
        functools.partial(attend_kernel, count, block, pair),
        grid_spec=pltpu.PrefetchScalarGridSpec(
            num_scalar_prefetch=1,
            grid=(heads // pair,),
            in_specs=[
                pl.BlockSpec((pair, 3, length, size), lambda g, t: (g, 0, 0, 0)),
                pl.BlockSpec((count, block), lambda g, t: (0, 0)),
            ],
            out_specs=[
                pl.BlockSpec((pair * size, length), lambda g, t: (g, 0)),
                pl.BlockSpec((pair, 1, length), lambda g, t: (g, 0, 0)),
            ],
            scratch_shapes=[
                pltpu.VMEM((pair, rows, length), bf16),
                pltpu.VMEM((pair, rows, block), f32),
            ],
        ),
        out_shape=[
            jax.ShapeDtypeStruct((heads * size, length), bf16),
            jax.ShapeDtypeStruct((heads, 1, length), f32),
        ],
        compiler_params=pltpu.CompilerParams(vmem_limit_bytes=56 << 20),
        cost_estimate=brief,
        name="attend",
    )(table, qkv, starts)


def attend_back_kernel(
    count,
    block,
    pair,
    table,
    qkv_ref,
    att_ref,
    grad_ref,
    lse_ref,
    start_ref,
    factor_ref,
    out_ref,
    dots_ref,
    qt_ref,
    kt_ref,
    delta_ref,
    dq_ref,
    dk_ref,
    dv_ref,
):
    size = qkv_ref.shape[3]
    unit = eye_rows(size, size)
    for h in range(pair):
        for b in range(count):
            here = slice(b * block, (b + 1) * block)
            qt_ref[h, :, here] = mm(unit, qkv_ref[h, 0, here, :], nt).astype(bf16)
            kt_ref[h, :, here] = mm(unit, qkv_ref[h, 1, here, :], nt).astype(bf16)
        rows = slice(h * size, (h + 1) * size)
        delta_ref[h] = jnp.sum(
            att_ref[rows, :].astype(f32) * grad_ref[rows, :].astype(f32), axis=0, keepdims=True
        )
    dq_ref[...] = jnp.zeros_like(dq_ref)
    key_index = lax.broadcasted_iota(jnp.int32, (block, block), 0)
    lane_index = lax.broadcasted_iota(jnp.int32, (1, block), 1)

    def key_block(j, carry):
        key_at = pl.multiple_of(table[0, j] * block, block)
        keys_here = key_index + j * block
        dk_ref[...] = jnp.zeros_like(dk_ref)
        dv_ref[...] = jnp.zeros_like(dv_ref)

        def step(masked, i, inner):
            at = pl.multiple_of(table[0, i] * block, block)
            if masked:
                seen = (keys_here >= start_ref[pl.ds(i, 1), :]) & (
                    keys_here <= lane_index + i * block
                )
            both = range(pair)
            grads = [grad_ref[h * size : (h + 1) * size, pl.ds(at, block)] for h in both]
            queries = [qt_ref[h, :, pl.ds(at, block)] for h in both]
            s = [mm(qkv_ref[h, 1, pl.ds(key_at, block), :], queries[h]) for h in both]
            dp = [mm(qkv_ref[h, 2, pl.ds(key_at, block), :], grads[h]) for h in both]
            p = [jnp.exp2(s[h] - lse_ref[h, :, pl.ds(at, block)]) for h in both]
            if masked:
                p = [jnp.where(seen, x, 0.0) for x in p]
            ds = [
                (p[h] * (dp[h] - delta_ref[h, :, pl.ds(at, block)])).astype(bf16) for h in both
            ]
            dv = [mm(grads[h], p[h].astype(bf16), nt) for h in both]
            dk = [mm(queries[h], ds[h], nt) for h in both]
            dq = [mm(kt_ref[h, :, pl.ds(key_at, block)], ds[h]) for h in both]
            for h in both:
                dv_ref[h] += dv[h]
                dk_ref[h] += dk[h]
                dq_ref[h, :, pl.ds(at, block)] += dq[h]
            return inner

        step(True, j, 0)
        lax.fori_loop(j + 1, table[3, j], functools.partial(step, False), 0)
        lax.fori_loop(table[3, j], table[4, j], functools.partial(step, True), 0)
        for h in range(pair):
            base = h * 3 * size
            out_ref[base + size : base + 2 * size, pl.ds(key_at, block)] = (
                dk_ref[h] * (1.0 / log2e)
            ).astype(bf16)
            out_ref[base + 2 * size : base + 3 * size, pl.ds(key_at, block)] = dv_ref[h].astype(bf16)
        return carry

    lax.fori_loop(0, count, key_block, 0)

    @pl.when(pl.program_id(0) == 0)
    def clear():
        dots_ref[...] = jnp.zeros_like(dots_ref)

    for h in range(pair):
        base = h * 3 * size
        rounded = dq_ref[h].astype(bf16).astype(f32)
        dots_ref[...] += jnp.sum(qt_ref[h].astype(f32) * rounded, axis=1, keepdims=True)
        out_ref[base : base + size, :] = (rounded * factor_ref[...]).astype(bf16)


def attend_back(chunk, pair, table, qkv, att, grad, lse, starts, factor):
    heads, _, length, size = qkv.shape
    count, block = starts.shape
    return pl.pallas_call(
        functools.partial(attend_back_kernel, count, block, pair),
        grid_spec=pltpu.PrefetchScalarGridSpec(
            num_scalar_prefetch=1,
            grid=(1,),
            in_specs=[
                pl.BlockSpec((pair, 3, length, size), lambda g, t: (chunk, 0, 0, 0)),
                pl.BlockSpec((pair * size, length), lambda g, t: (chunk, 0)),
                pl.BlockSpec((pair * size, length), lambda g, t: (chunk, 0)),
                pl.BlockSpec((pair, 1, length), lambda g, t: (chunk, 0, 0)),
                pl.BlockSpec((count, block), lambda g, t: (0, 0)),
                pl.BlockSpec((size, 1), lambda g, t: (0, 0)),
            ],
            out_specs=[
                pl.BlockSpec((pair * 3 * size, length), lambda g, t: (0, 0)),
                pl.BlockSpec((size, 1), lambda g, t: (0, 0)),
            ],
            scratch_shapes=[
                pltpu.VMEM((pair, size, length), bf16),
                pltpu.VMEM((pair, size, length), bf16),
                pltpu.VMEM((pair, 1, length), f32),
                pltpu.VMEM((pair, size, length), f32),
                pltpu.VMEM((pair, size, block), f32),
                pltpu.VMEM((pair, size, block), f32),
            ],
        ),
        out_shape=[
            jax.ShapeDtypeStruct((pair * 3 * size, length), bf16),
            jax.ShapeDtypeStruct((size, 1), f32),
        ],
        compiler_params=pltpu.CompilerParams(vmem_limit_bytes=56 << 20),
        cost_estimate=brief,
        name="attend_back",
    )(table, qkv, att, grad, lse, starts, factor)


def input_side_kernel(count, *refs):
    w_ref, out_ref = refs[count], refs[count + 1]
    grads = jnp.concatenate([ref[...] for ref in refs[:count]], axis=0)
    out_ref[...] = mm(grads.T, w_ref[...], nt).astype(bf16)


def input_side(grads, w, block, first, blocks):
    width, wide = w.shape
    rows = grads[0].shape[0]
    tokens = blocks * block
    return pl.pallas_call(
        functools.partial(input_side_kernel, len(grads)),
        grid=(blocks,),
        in_specs=[pl.BlockSpec((rows, block), lambda i: (0, i + first)) for _ in grads]
        + [pl.BlockSpec((width, wide), lambda i: (0, 0))],
        out_specs=pl.BlockSpec((block, width), lambda i: (i, 0)),
        out_shape=jax.ShapeDtypeStruct((tokens, width), bf16),
        compiler_params=pltpu.CompilerParams(vmem_limit_bytes=56 << 20),
        cost_estimate=pl.CostEstimate(
            flops=4 * tokens * width * wide, bytes_accessed=1, transcendentals=0
        ),
        name="input_side",
    )(*grads, w)


def reduce_places(buf, places, late=(), hold=()):
    place = lax.axis_index("seq")
    lines, wide = buf.shape
    bits = places.bit_length() - 1
    assert places == 1 << bits and lines % places == 0
    for b in range(bits):
        bit = (place >> b) & 1
        halves = buf.reshape(2, -1, wide)
        keep = lax.dynamic_index_in_dim(halves, bit, 0, keepdims=False)
        send = lax.dynamic_index_in_dim(halves, 1 - bit, 0, keepdims=False)
        if hold and b == 2:
            send = after(send, *hold)
        yield send
        got = lax.ppermute(send, "seq", [(i, i ^ (1 << b)) for i in range(places)])
        buf = (keep.astype(f32) + got.astype(f32)).astype(bf16)
    for b in reversed(range(bits)):
        bit = (place >> b) & 1
        if late and b == 0:
            buf = after(buf, *late)
        yield buf
        got = lax.ppermute(buf, "seq", [(i, i ^ (1 << b)) for i in range(places)])
        buf = jnp.where(
            bit == 0, jnp.concatenate([buf, got], axis=0), jnp.concatenate([got, buf], axis=0)
        )
    yield buf


def last(steps):
    for value in steps:
        pass
    return value


def sum_everywhere(team, vector):
    vector = vector + lax.ppermute(vector, "dp", team.swap_core())
    total = vector
    for step in range(1, team.rows):
        total = total + lax.ppermute(vector, "dp", team.turn_rows(step))
    for b in range(team.seq.bit_length() - 1):
        total = total + lax.ppermute(
            total, "seq", [(i, i ^ (1 << b)) for i in range(team.seq)]
        )
    return total


def on_device(
    activations,
    segment_ids,
    norm1_gain,
    w_qkv,
    per_dim_scale,
    w_out,
    norm2_gain,
    w_up,
    b_up,
    w_down,
    b_down,
    cotangent,
):
    seqs, span, width = activations.shape
    rows_here, heads, _, head_size = w_qkv.shape
    length = segment_ids.shape[1]
    team = Team(lax.axis_size("dp"), lax.axis_size("seq"), seqs)
    size = team.size
    row, core, group, side, member = team.here()
    local_heads = heads // size
    wide = local_heads * 3 * head_size
    own = seqs * span

    def spread(array, *near):
        out = []
        for step in range(seqs):
            source = after(array, *near) if near and step < seqs // 2 else array
            block = lax.dynamic_index_in_dim(source, (group + step) % seqs, 0, keepdims=False)
            out.append(lax.ppermute(block, axes, team.spread(step)))
        return out

    def spread_done(pieces):
        return join(pieces, [jnp.int32(k) for k in range(seqs)]).reshape(own, width)

    def unspread(array):
        return [
            lax.ppermute(array[step * span : (step + 1) * span], axes, team.back(step))
            for step in range(seqs)
        ]

    def unspread_done(pieces, dtype):
        return join(pieces, [(group + step) % seqs for step in range(seqs)], dtype=dtype)

    def shard_of(step, flip):
        return (row - step) % team.rows * 2 + (core ^ flip)

    shifts = [(step, flip) for step in range(team.rows) for flip in range(2)]

    w_local = w_qkv.reshape(rows_here, heads * 3 * head_size)
    small = jnp.concatenate([norm1_gain, norm2_gain, b_up, b_down])
    small = jnp.pad(small, (0, wide * 16 - small.shape[0])).reshape(16, wide)

    def columns(first):
        part = lax.dynamic_slice_in_dim(w_local, first * wide, wide, 1)
        return jnp.concatenate([part, small], axis=0)

    parts = [columns(member), columns(member + 1 - 2 * core)]
    far = [
        lax.ppermute(parts[flip], "dp", team.turn_rows(step, flip)) for step, flip in shifts[2:]
    ]
    near = lax.ppermute(parts[1], "dp", team.swap_core())
    x_blocks = spread(after(activations, *parts), near)
    other_ids = lax.ppermute(segment_ids, "dp", team.swap_core())
    w_half, small = join(
        [parts[0], near] + far,
        [shard_of(*s) for s in shifts],
        ends=(rows_here, rows_here + 16),
    )
    w_half = w_half.reshape(width, wide)
    small = small.reshape(team.dp, -1)[:, : 4 * rows_here]
    small = small.reshape(team.dp, 4, rows_here).transpose(1, 0, 2).reshape(4, width).astype(f32)
    gain_in, gain_mid, bias_up, bias_down = (small[i : i + 1] for i in range(4))
    three = after(jnp.concatenate([w_out, w_up, w_down]), *far)
    three = [three] + [
        lax.ppermute(three, "dp", team.turn_rows(step)) for step in range(1, team.rows)
    ]
    cot_own = spread(after(cotangent, *far).astype(bf16))

    ids = lax.dynamic_index_in_dim(
        jnp.where(side == core, segment_ids, other_ids), group, 0, keepdims=False
    )
    starts = jnp.sum((ids[None, :] < ids[:, None]).astype(jnp.int32), axis=1)
    ends = jnp.sum((ids[None, :] <= ids[:, None]).astype(jnp.int32), axis=1) - 1
    count = length // span
    starts = starts.reshape(count, span)
    ends = ends.reshape(count, span)
    index = jnp.arange(count)
    z_of, u_of = index // size, index % size
    at = ((u_of - member) % size) * seqs + (group - z_of) % seqs
    first = starts[:, 0] // span
    last_start = starts[:, -1]
    open_from = jnp.minimum((last_start + span - 1) // span, index)
    open_to = jnp.sum((last_start[None, :] <= index[:, None] * span).astype(jnp.int32), axis=1)
    open_to = jnp.maximum(open_to, index + 1)
    stop = ends[:, -1] // span + 1
    table = jnp.stack([at, first, open_from, open_to, stop]).astype(jnp.int32)

    factor = scale_base / math.sqrt(head_size) * jax.nn.softplus(per_dim_scale)
    unit = jnp.ones((head_size,), f32)
    factor_row = jnp.tile(jnp.concatenate([factor * log2e, unit, unit]), local_heads)[None, :]

    x_own = spread_done(after(x_blocks, w_half, table, starts, factor_row))
    xs = [x_own] + [lax.ppermute(x_own, axes, team.rotate(-j)) for j in range(1, size)]
    qkv, normed_in = project_qkv(
        xs, gain_in, w_half, factor_row, local_heads, head_size, team.dp, span
    )
    early = seqs // 2
    qkv, cot_own[early:] = after((qkv, cot_own[early:]), *cot_own[early:])
    att, lse = attend(table, qkv, starts)
    three = after(three, att)
    swapped = [lax.ppermute(piece, "dp", team.swap_core()) for piece in three]
    w_out_all, w_up_all, w_down_all = (
        w.reshape(-1, width)
        for w in join(
            three + swapped,
            [shard_of(step, 0) for step in range(team.rows)]
            + [shard_of(step, 1) for step in range(team.rows)],
            ends=(rows_here, 2 * rows_here, 3 * rows_here),
        )
    )

    pieces = [(att[:, :own], member)]
    for j in range(1, size):
        got = lax.ppermute(att[:, j * own : (j + 1) * own], axes, team.rotate(j))
        pieces.append((got, (member - j) % size))
    att_own = join([p for p, _ in pieces], [s for _, s in pieces])
    att_own = att_own.reshape(heads * head_size, own)

    x_float = x_own.astype(f32)
    mid = x_float + lax.dot_general(
        att_own, w_out_all, (((0,), (0,)), ((), ())), preferred_element_type=f32
    )
    rms_mid = lax.rsqrt(jnp.mean(mid * mid, axis=-1, keepdims=True) + epsilon)
    normed_mid = (mid * rms_mid * gain_mid).astype(bf16)
    pre_act = mm(normed_mid, w_up_all) + bias_up
    activated = jax.nn.silu(pre_act).astype(bf16)
    result_own = (mid + mm(activated, w_down_all) + bias_down).astype(bf16)
    result = unspread(result_own)
    cot_own = spread_done(after(cot_own, result_own))

    grad_bias_down = jnp.sum(cot_own.astype(f32), axis=0)
    tn = (((0,), (0,)), ((), ()))
    grad_act = mm(cot_own, w_down_all, nt)
    sig = jax.nn.sigmoid(pre_act)
    grad_pre = (grad_act * sig * (1.0 + pre_act * (1.0 - sig))).astype(bf16)
    grad_bias_up = jnp.sum(grad_pre.astype(f32), axis=0)
    grad_normed_mid = mm(grad_pre, w_up_all, nt)
    grad_gain_mid = jnp.sum(grad_normed_mid * mid * rms_mid, axis=0)
    scaled_mid = grad_normed_mid * gain_mid
    grad_mid = cot_own.astype(f32) + rms_mid * (
        scaled_mid - mid * rms_mid * rms_mid * jnp.mean(scaled_mid * mid, axis=-1, keepdims=True)
    )
    grad_attn = grad_mid.astype(bf16)
    grad_att = mm(w_out_all, grad_attn, nt).astype(bf16).reshape(size, -1, own)
    pieces = [(lax.dynamic_index_in_dim(grad_att, member, 0, keepdims=False), 0)]
    for j in range(1, size):
        out = lax.dynamic_index_in_dim(grad_att, (member + j) % size, 0, keepdims=False)
        pieces.append((lax.ppermute(out, axes, team.rotate(j)), (-j) % size))
    pieces.sort(key=lambda item: item[1])
    grad_heads = jnp.concatenate([piece for piece, _ in pieces], axis=1)

    def by_core(grad):
        parts = grad.astype(bf16).reshape(team.rows, 2, rows_here, width)
        keep = lax.dynamic_index_in_dim(parts, core, 1, keepdims=False)
        send = lax.dynamic_index_in_dim(parts, 1 - core, 1, keepdims=False)
        return keep, lax.ppermute(send, "dp", team.swap_core())

    three = [
        by_core(grad)
        for grad in (mm(activated, cot_own, tn), mm(normed_mid, grad_pre, tn), mm(att_own, grad_attn))
    ]

    def both_cores(step):
        at = (row + step) % team.rows
        return jnp.concatenate(
            [
                lax.dynamic_index_in_dim(keep, at, 0, keepdims=False).astype(f32)
                + lax.dynamic_index_in_dim(got, at, 0, keepdims=False).astype(f32)
                for keep, got in three
            ]
        ).astype(bf16)

    three_rows = [both_cores(step) for step in range(team.rows)]
    three_far = [
        lax.ppermute(three_rows[step], "dp", team.turn_rows(step)) for step in range(1, team.rows)
    ]

    def add(first, *more):
        total = first.astype(f32)
        for piece in more:
            total = total + piece.astype(f32)
        return total.astype(bf16)

    pair = math.gcd(local_heads, 4)
    grad_in = after(grad_heads, *three_rows)
    chunks, dots, heads_of = [], 0.0, []
    steps, hold = None, []
    for c in range(local_heads // pair):
        grads, dot = attend_back(
            c, pair, table, qkv, att, grad_in, lse, starts, factor[:, None]
        )
        chunks.append(grads)
        dots = dots + dot
        if c == 0:
            result = after(result, grads)
            grads = after(grads, *result)
        else:
            if steps is None:
                three_far = after(three_far, grads)
                steps = reduce_places(add(three_rows[0], *three_far), team.seq, hold=hold)
            grads = after(grads, next(steps))
        send, keep = head_grad(grads, normed_in, team.rows, row, core)
        near = [lax.ppermute(piece, "dp", team.swap_core()) for piece in send]
        far = [
            [
                lax.ppermute(source, "dp", team.turn_rows(step))
                for source in (keep[step], near[step])
            ]
            for step in range(1, team.rows)
        ]
        heads_of.append((keep[0], near[0], far))
        grad_in = after(grad_in, *send, *keep)
    steps = steps or reduce_places(add(three_rows[0], *three_far), team.seq, hold=hold)
    blocks = own // span
    chunks = after(chunks, *send, *keep)
    partial = [
        input_side(chunks, w_half, span, j * blocks, blocks) for j in range(1, size)
    ]
    chunks = after(chunks, *partial)
    heads_of = after(heads_of, *partial)
    grad_normed_in = sum(
        [
            lax.ppermute(p, axes, team.rotate(j + 1)).astype(f32)
            for j, p in enumerate(partial)
        ],
        input_side(chunks, w_half, span, 0, blocks).astype(f32),
    )
    rms_in = lax.rsqrt(jnp.mean(x_float * x_float, axis=-1, keepdims=True) + epsilon)
    grad_gain_in = jnp.sum(grad_normed_in * x_float * rms_in, axis=0)
    scaled_in = grad_normed_in * gain_in
    input_grad_own = grad_mid + rms_in * (
        scaled_in
        - x_float * rms_in * rms_in * jnp.mean(scaled_in * x_float, axis=-1, keepdims=True)
    )
    input_grad_own = input_grad_own.astype(bf16)
    input_grad = unspread(input_grad_own)
    late = input_grad[seqs // 2 :]
    hold.append(input_grad_own)
    input_grad = unspread_done(input_grad, f32)
    result = unspread_done(result, bf16)

    three = last(steps).astype(f32)
    part_out, part_up, part_down = (
        three[i * rows_here : (i + 1) * rows_here] for i in (2, 1, 0)
    )
    full = []
    for mine, theirs, far in heads_of:
        total = jnp.concatenate(
            [add(mine, *[f[0] for f in far]), add(theirs, *[f[1] for f in far])]
        )
        total = place_in([(total, member // 2)], team.half) if team.half > 1 else total
        total = after(total.reshape(-1, total.shape[-1]), input_grad_own)
        full.append(last(reduce_places(total, team.seq, late)))
    full = unfold(full, team.half, rows_here, core).reshape(heads, 3, head_size, rows_here)
    vectors = sum_everywhere(
        team,
        jnp.concatenate([grad_gain_in, grad_gain_mid, grad_bias_up, grad_bias_down, dots[:, 0]]),
    )
    d = lax.axis_index("dp")

    def slice_of(i):
        return lax.dynamic_slice_in_dim(vectors, i * width + d * rows_here, rows_here, 0)

    grad_scale = vectors[4 * width :] / (factor * log2e) * (
        scale_base / math.sqrt(head_size)
    ) * jax.nn.sigmoid(per_dim_scale)
    return (
        result,
        input_grad,
        slice_of(0),
        full.transpose(3, 0, 1, 2),
        grad_scale,
        part_out,
        slice_of(1),
        part_up,
        slice_of(2),
        part_down,
        slice_of(3),
    )


def solution(mesh):
    in_specs = (
        P("dp", "seq", None),
        P("dp", None),
        P("dp"),
        P("dp", None, None, None),
        P(),
        P("dp", None),
        P("dp"),
        P("dp", None),
        P("dp"),
        P("dp", None),
        P("dp"),
        P("dp", "seq", None),
    )
    out_specs = (
        P("dp", "seq", None),
        P("dp", "seq", None),
        P("dp"),
        P("dp", None, None, None),
        P(),
        P("dp", None),
        P("dp"),
        P("dp", None),
        P("dp"),
        P("dp", None),
        P("dp"),
    )
    return jax.shard_map(
        on_device, mesh=mesh, in_specs=in_specs, out_specs=out_specs, check_vma=False
    )
```

```python
import functools
import math

import jax
import jax.numpy as jnp
from jax import lax
from jax.experimental import pallas as pl
from jax.experimental.pallas import tpu as pltpu
from jax.sharding import PartitionSpec as P

epsilon = 1e-06
scale_base = 1.442695041
log2e = 1.4426950408889634
masked_value = -1e30
score_limit = 100.0
bf16 = jnp.bfloat16
f32 = jnp.float32
axes = ("dp", "seq")
brief = pl.CostEstimate(flops=1, bytes_accessed=1, transcendentals=0)
nt = (((1,), (1,)), ((), ()))
nn = (((1,), (0,)), ((), ()))


def mm(a, b, dims=nn):
    return lax.dot_general(a, b, dims, preferred_element_type=f32)


class Team:
    def __init__(self, dp, seq, seqs):
        self.dp, self.seq, self.seqs = dp, seq, seqs
        self.size = seq // seqs
        assert seq % seqs == 0 and self.size % 2 == 0 and dp % 2 == 0
        self.half = self.size // 2
        self.rows = dp // 2

    def places(self):
        for row in range(self.rows):
            for core in range(2):
                for place in range(self.seq):
                    yield row, core, place

    def rank(self, row, core, place):
        return (row * 2 + core) * self.seq + place

    def here(self):
        d = lax.axis_index("dp")
        p = lax.axis_index("seq")
        row, core = d // 2, d % 2
        group = p // self.size
        side = (p % self.size) // self.half
        member = (p % self.half) * 2 + core
        return row, core, group, side, member

    def spread(self, step):
        pairs = []
        for row, core, place in self.places():
            z, u = place // self.size, place % self.size
            s = (z + step) % self.seqs
            pairs.append(
                (
                    self.rank(row, core, place),
                    self.rank(row, u % 2, s * self.size + core * self.half + u // 2),
                )
            )
        return pairs

    def back(self, step):
        return [(b, a) for a, b in self.spread(step)]

    def rotate(self, step):
        pairs = []
        for row, core, place in self.places():
            base = place - place % self.half
            m = (place % self.half) * 2 + core
            to = (m + step) % self.size
            pairs.append((self.rank(row, core, place), self.rank(row, to % 2, base + to // 2)))
        return pairs

    def swap_core(self):
        return [(d, d ^ 1) for d in range(self.dp)]

    def turn_rows(self, step, flip=0):
        return [(d, ((d + 2 * step) % self.dp) ^ flip) for d in range(self.dp)]


def after(value, *first):
    return lax.optimization_barrier((value, first))[0]


def place_in(pieces, count):
    first = pieces[0][0]
    out = jnp.zeros((count,) + first.shape, first.dtype)
    for piece, index in pieces:
        out = lax.dynamic_update_index_in_dim(out, piece, index, 0)
    return out


def join_kernel(count, ends, slots_ref, *refs):
    outs = refs[count:]
    for k in range(count):
        start = 0
        for out_ref, end in zip(outs, ends):
            out_ref[slots_ref[k]] = refs[k][start:end, :].astype(out_ref.dtype)
            start = end


def join(pieces, slots, ends=None, dtype=None):
    count = len(pieces)
    rows, columns = pieces[0].shape
    dtype = dtype or pieces[0].dtype
    ends = ends or (rows,)
    heights = [b - a for a, b in zip((0,) + tuple(ends[:-1]), ends)]
    wide = columns
    if columns % 128 == 0:
        wide = max(b for b in range(128, min(columns, 640) + 1, 128) if columns % b == 0)
    outs = pl.pallas_call(
        functools.partial(join_kernel, count, ends),
        grid_spec=pltpu.PrefetchScalarGridSpec(
            num_scalar_prefetch=1,
            grid=(columns // wide,),
            in_specs=[pl.BlockSpec((rows, wide), lambda i, s: (0, i)) for _ in pieces],
            out_specs=[pl.BlockSpec((count, h, wide), lambda i, s: (0, 0, i)) for h in heights],
        ),
        out_shape=[jax.ShapeDtypeStruct((count, h, columns), dtype) for h in heights],
        compiler_params=pltpu.CompilerParams(vmem_limit_bytes=56 << 20),
        cost_estimate=brief,
        name="join",
    )(jnp.stack(slots).astype(jnp.int32), *pieces)
    return outs if len(ends) > 1 else outs[0]


def qkv_kernel(count, blocks, parts, head_size, *refs):
    x_refs = refs[:count]
    gain_ref, w_ref, factor_ref, out_ref, normed_ref = refs[count:]
    i = pl.program_id(0)
    x = x_refs[0][...]
    for j in range(1, count):
        x = jnp.where(i >= j * blocks, x_refs[j][...], x)
    x = x.astype(f32)
    rms = lax.rsqrt(jnp.mean(x * x, axis=-1, keepdims=True) + epsilon)
    normed = (x * rms * gain_ref[...]).astype(bf16)
    part = x.shape[1] // parts
    for d in range(parts):
        normed_ref[d % 2, :, d // 2 * part : (d // 2 + 1) * part] = normed[
            :, d * part : (d + 1) * part
        ]
    packed = (mm(normed, w_ref[...]) * factor_ref[...]).astype(bf16)
    for h in range(packed.shape[1] // head_size):
        out_ref[h // 3, h % 3] = packed[:, h * head_size : (h + 1) * head_size]


def project_qkv(xs, gain, w, factor_row, heads, head_size, parts, block):
    own, width = xs[0].shape
    count, blocks = len(xs), own // block
    tokens = own * count
    wide = w.shape[1]

    def x_spec(j):
        return pl.BlockSpec(
            (block, width), lambda i: (jnp.clip(i - j * blocks, 0, blocks - 1), 0)
        )

    return pl.pallas_call(
        functools.partial(qkv_kernel, count, blocks, parts, head_size),
        grid=(tokens // block,),
        in_specs=[x_spec(j) for j in range(count)]
        + [
            pl.BlockSpec((1, width), lambda i: (0, 0)),
            pl.BlockSpec((width, wide), lambda i: (0, 0)),
            pl.BlockSpec((1, wide), lambda i: (0, 0)),
        ],
        out_specs=[
            pl.BlockSpec((heads, 3, block, head_size), lambda i: (0, 0, i, 0)),
            pl.BlockSpec((2, block, width // 2), lambda i: (0, i, 0)),
        ],
        out_shape=[
            jax.ShapeDtypeStruct((heads, 3, tokens, head_size), bf16),
            jax.ShapeDtypeStruct((2, tokens, width // 2), bf16),
        ],
        compiler_params=pltpu.CompilerParams(vmem_limit_bytes=56 << 20),
        cost_estimate=brief,
        name="qkv",
    )(*xs, gain, w, factor_row)


def head_grad_kernel(rows, fold, place_ref, grads_ref, normed_ref, *out_refs):
    result = mm(grads_ref[...], normed_ref[0]).astype(bf16)
    part = result.shape[1] // rows
    lines = result.shape[0] // fold
    for side in range(2):
        for row in range(rows):

            @pl.when((pl.program_id(0) == side) & (place_ref[2] == row))
            def store(side=side, row=row):
                for step in range(rows):
                    at = (row + step) % rows * part
                    for k in range(fold):
                        out_refs[side * rows + step][:, k * part : (k + 1) * part] = result[
                            k * lines : (k + 1) * lines, at : at + part
                        ]


def head_grad(grads, normed, rows, row, core):
    _, tokens, width = normed.shape
    lines = grads.shape[0]
    part = width // rows
    fold = 128 // math.gcd(part, 128)
    shape = (lines // fold, fold * part)
    outs = pl.pallas_call(
        functools.partial(head_grad_kernel, rows, fold),
        grid_spec=pltpu.PrefetchScalarGridSpec(
            num_scalar_prefetch=1,
            grid=(2,),
            in_specs=[
                pl.BlockSpec((lines, tokens), lambda i, o: (0, 0)),
                pl.BlockSpec((1, tokens, width), lambda i, o: (o[i], 0, 0)),
            ],
            out_specs=[pl.BlockSpec(shape, lambda i, o: (0, 0)) for _ in range(2 * rows)],
        ),
        out_shape=[jax.ShapeDtypeStruct(shape, bf16) for _ in range(2 * rows)],
        compiler_params=pltpu.CompilerParams(vmem_limit_bytes=56 << 20),
        cost_estimate=brief,
        name="head_grad",
    )(jnp.stack([1 - core, core, row]).astype(jnp.int32), grads, normed)
    return outs[:rows], outs[rows:]


def unfold_kernel(count, fold, core_ref, *refs):
    out_ref = refs[count]
    part = out_ref.shape[1]
    lines = out_ref.shape[0] // fold
    for c in range(count):

        @pl.when(pl.program_id(0) % count == c)
        def store(c=c):
            for k in range(fold):
                out_ref[k * lines : (k + 1) * lines, :] = refs[c][
                    :, k * part : (k + 1) * part
                ].astype(f32)


def unfold(chunks, groups, part, core):
    count = len(chunks)
    lines = chunks[0].shape[0] // (2 * groups)
    wide = chunks[0].shape[1]
    fold = wide // part

    def source(i, o):
        g = i // count
        return (g // 2 * 2 + (g % 2 + o[0]) % 2, 0)

    return pl.pallas_call(
        functools.partial(unfold_kernel, count, fold),
        grid_spec=pltpu.PrefetchScalarGridSpec(
            num_scalar_prefetch=1,
            grid=(2 * groups * count,),
            in_specs=[pl.BlockSpec((lines, wide), source) for _ in chunks],
            out_specs=pl.BlockSpec((lines * fold, part), lambda i, o: (i, 0)),
        ),
        out_shape=jax.ShapeDtypeStruct((2 * groups * count * lines * fold, part), f32),
        compiler_params=pltpu.CompilerParams(vmem_limit_bytes=56 << 20),
        cost_estimate=brief,
        name="unfold",
    )(core.reshape(1).astype(jnp.int32), *chunks)


def eye_rows(rows, columns):
    a = lax.broadcasted_iota(jnp.int32, (rows, columns), 0)
    b = lax.broadcasted_iota(jnp.int32, (rows, columns), 1)
    return (a == b).astype(bf16)


def attend_kernel(count, block, pair, table, qkv_ref, start_ref, att_ref, lse_ref, vt_ref, acc_ref):
    size = qkv_ref.shape[3]
    rows = vt_ref.shape[1]
    unit = eye_rows(rows, size)
    one_row = (lax.broadcasted_iota(jnp.int32, (rows, block), 0) == size).astype(f32)
    for h in range(pair):
        for b in range(count):
            here = slice(b * block, (b + 1) * block)
            vt_ref[h, :, here] = (mm(unit, qkv_ref[h, 2, here, :], nt) + one_row).astype(bf16)
    key_index = lax.broadcasted_iota(jnp.int32, (block, block), 0)
    lane_index = lax.broadcasted_iota(jnp.int32, (1, block), 1)
    ones = jnp.ones((8, size), bf16)

    def longest(part):
        best = jnp.zeros((8, block), f32)
        for h in range(pair):
            for b in range(count):
                x = qkv_ref[h, part, b * block : (b + 1) * block, :]
                best = jnp.maximum(best, mm(ones, x * x, nt))
        return jnp.max(best)

    small = longest(0) * longest(1) * 1.1 < score_limit * score_limit

    def query_block(raised, i, carry):
        at = pl.multiple_of(table[0, i] * block, block)
        starts = start_ref[pl.ds(i, 1), :]
        places = lane_index + i * block
        queries = [qkv_ref[h, 0, pl.ds(at, block), :] for h in range(pair)]
        acc_ref[...] = jnp.zeros_like(acc_ref)

        def step(masked, j, peaks):
            key_at = pl.multiple_of(table[0, j] * block, block)
            if masked:
                keys_here = key_index + j * block
                seen = (keys_here >= starts) & (keys_here <= places)
            scores = [
                mm(qkv_ref[h, 1, pl.ds(key_at, block), :], queries[h], nt) for h in range(pair)
            ]
            if masked:
                scores = [jnp.where(seen, s, masked_value) for s in scores]
            values = [vt_ref[h, :, pl.ds(key_at, block)] for h in range(pair)]
            if not raised:
                probs = [jnp.exp2(s).astype(bf16) for s in scores]
                sums = [mm(values[h], probs[h]) for h in range(pair)]
                for h in range(pair):
                    acc_ref[h] += sums[h]
                return ()
            out = []
            for h in range(pair):
                peak = jnp.maximum(peaks[h], jnp.max(scores[h], axis=0, keepdims=True))
                p = jnp.exp2(scores[h] - peak).astype(bf16)
                acc_ref[h] = acc_ref[h] * jnp.exp2(peaks[h] - peak) + mm(values[h], p)
                out.append(peak)
            return tuple(out)

        peaks = ()
        if raised:
            peaks = tuple(jnp.full((1, block), masked_value, f32) for _ in range(pair))
        peaks = lax.fori_loop(table[1, i], table[2, i], functools.partial(step, True), peaks)
        peaks = lax.fori_loop(table[2, i], i, functools.partial(step, False), peaks)
        peaks = step(True, i, peaks)
        for h in range(pair):
            total = acc_ref[h, size : size + 1, :]
            att_ref[h * size : (h + 1) * size, pl.ds(at, block)] = (
                acc_ref[h, :size, :] / total
            ).astype(bf16)
            low = jnp.log2(total)
            lse_ref[h, :, pl.ds(at, block)] = peaks[h] + low if raised else low
        return carry

    @pl.when(small)
    def plain():
        lax.fori_loop(0, count, functools.partial(query_block, False), 0)

    @pl.when(jnp.logical_not(small))
    def careful():
        lax.fori_loop(0, count, functools.partial(query_block, True), 0)


def attend(table, qkv, starts):
    heads, _, length, size = qkv.shape
    pair = math.gcd(heads, 8)
    count, block = starts.shape
    rows = (size // 16 + 1) * 16
    return pl.pallas_call(
        functools.partial(attend_kernel, count, block, pair),
        grid_spec=pltpu.PrefetchScalarGridSpec(
            num_scalar_prefetch=1,
            grid=(heads // pair,),
            in_specs=[
                pl.BlockSpec((pair, 3, length, size), lambda g, t: (g, 0, 0, 0)),
                pl.BlockSpec((count, block), lambda g, t: (0, 0)),
            ],
            out_specs=[
                pl.BlockSpec((pair * size, length), lambda g, t: (g, 0)),
                pl.BlockSpec((pair, 1, length), lambda g, t: (g, 0, 0)),
            ],
            scratch_shapes=[
                pltpu.VMEM((pair, rows, length), bf16),
                pltpu.VMEM((pair, rows, block), f32),
            ],
        ),
        out_shape=[
            jax.ShapeDtypeStruct((heads * size, length), bf16),
            jax.ShapeDtypeStruct((heads, 1, length), f32),
        ],
        compiler_params=pltpu.CompilerParams(vmem_limit_bytes=56 << 20),
        cost_estimate=brief,
        name="attend",
    )(table, qkv, starts)


def attend_back_kernel(
    count,
    block,
    pair,
    table,
    qkv_ref,
    att_ref,
    grad_ref,
    lse_ref,
    start_ref,
    factor_ref,
    out_ref,
    dots_ref,
    qt_ref,
    kt_ref,
    delta_ref,
    dq_ref,
    dk_ref,
    dv_ref,
):
    size = qkv_ref.shape[3]
    unit = eye_rows(size, size)
    for h in range(pair):
        for b in range(count):
            here = slice(b * block, (b + 1) * block)
            qt_ref[h, :, here] = mm(unit, qkv_ref[h, 0, here, :], nt).astype(bf16)
            kt_ref[h, :, here] = mm(unit, qkv_ref[h, 1, here, :], nt).astype(bf16)
        rows = slice(h * size, (h + 1) * size)
        delta_ref[h] = jnp.sum(
            att_ref[rows, :].astype(f32) * grad_ref[rows, :].astype(f32), axis=0, keepdims=True
        )
    dq_ref[...] = jnp.zeros_like(dq_ref)
    key_index = lax.broadcasted_iota(jnp.int32, (block, block), 0)
    lane_index = lax.broadcasted_iota(jnp.int32, (1, block), 1)

    def key_block(j, carry):
        key_at = pl.multiple_of(table[0, j] * block, block)
        keys_here = key_index + j * block
        dk_ref[...] = jnp.zeros_like(dk_ref)
        dv_ref[...] = jnp.zeros_like(dv_ref)

        def step(masked, i, inner):
            at = pl.multiple_of(table[0, i] * block, block)
            if masked:
                seen = (keys_here >= start_ref[pl.ds(i, 1), :]) & (
                    keys_here <= lane_index + i * block
                )
            both = range(pair)
            grads = [grad_ref[h * size : (h + 1) * size, pl.ds(at, block)] for h in both]
            queries = [qt_ref[h, :, pl.ds(at, block)] for h in both]
            s = [mm(qkv_ref[h, 1, pl.ds(key_at, block), :], queries[h]) for h in both]
            dp = [mm(qkv_ref[h, 2, pl.ds(key_at, block), :], grads[h]) for h in both]
            p = [jnp.exp2(s[h] - lse_ref[h, :, pl.ds(at, block)]) for h in both]
            if masked:
                p = [jnp.where(seen, x, 0.0) for x in p]
            ds = [
                (p[h] * (dp[h] - delta_ref[h, :, pl.ds(at, block)])).astype(bf16) for h in both
            ]
            dv = [mm(grads[h], p[h].astype(bf16), nt) for h in both]
            dk = [mm(queries[h], ds[h], nt) for h in both]
            dq = [mm(kt_ref[h, :, pl.ds(key_at, block)], ds[h]) for h in both]
            for h in both:
                dv_ref[h] += dv[h]
                dk_ref[h] += dk[h]
                dq_ref[h, :, pl.ds(at, block)] += dq[h]
            return inner

        step(True, j, 0)
        lax.fori_loop(j + 1, table[3, j], functools.partial(step, False), 0)
        lax.fori_loop(table[3, j], table[4, j], functools.partial(step, True), 0)
        for h in range(pair):
            base = h * 3 * size
            out_ref[base + size : base + 2 * size, pl.ds(key_at, block)] = (
                dk_ref[h] * (1.0 / log2e)
            ).astype(bf16)
            out_ref[base + 2 * size : base + 3 * size, pl.ds(key_at, block)] = dv_ref[h].astype(bf16)
        return carry

    lax.fori_loop(0, count, key_block, 0)

    @pl.when(pl.program_id(0) == 0)
    def clear():
        dots_ref[...] = jnp.zeros_like(dots_ref)

    for h in range(pair):
        base = h * 3 * size
        rounded = dq_ref[h].astype(bf16).astype(f32)
        dots_ref[...] += jnp.sum(qt_ref[h].astype(f32) * rounded, axis=1, keepdims=True)
        out_ref[base : base + size, :] = (rounded * factor_ref[...]).astype(bf16)


def attend_back(chunk, pair, table, qkv, att, grad, lse, starts, factor):
    heads, _, length, size = qkv.shape
    count, block = starts.shape
    return pl.pallas_call(
        functools.partial(attend_back_kernel, count, block, pair),
        grid_spec=pltpu.PrefetchScalarGridSpec(
            num_scalar_prefetch=1,
            grid=(1,),
            in_specs=[
                pl.BlockSpec((pair, 3, length, size), lambda g, t: (chunk, 0, 0, 0)),
                pl.BlockSpec((pair * size, length), lambda g, t: (chunk, 0)),
                pl.BlockSpec((pair * size, length), lambda g, t: (chunk, 0)),
                pl.BlockSpec((pair, 1, length), lambda g, t: (chunk, 0, 0)),
                pl.BlockSpec((count, block), lambda g, t: (0, 0)),
                pl.BlockSpec((size, 1), lambda g, t: (0, 0)),
            ],
            out_specs=[
                pl.BlockSpec((pair * 3 * size, length), lambda g, t: (0, 0)),
                pl.BlockSpec((size, 1), lambda g, t: (0, 0)),
            ],
            scratch_shapes=[
                pltpu.VMEM((pair, size, length), bf16),
                pltpu.VMEM((pair, size, length), bf16),
                pltpu.VMEM((pair, 1, length), f32),
                pltpu.VMEM((pair, size, length), f32),
                pltpu.VMEM((pair, size, block), f32),
                pltpu.VMEM((pair, size, block), f32),
            ],
        ),
        out_shape=[
            jax.ShapeDtypeStruct((pair * 3 * size, length), bf16),
            jax.ShapeDtypeStruct((size, 1), f32),
        ],
        compiler_params=pltpu.CompilerParams(vmem_limit_bytes=56 << 20),
        cost_estimate=brief,
        name="attend_back",
    )(table, qkv, att, grad, lse, starts, factor)


def input_side_kernel(count, *refs):
    w_ref, out_ref = refs[count], refs[count + 1]
    grads = jnp.concatenate([ref[...] for ref in refs[:count]], axis=0)
    out_ref[...] = mm(grads.T, w_ref[...], nt).astype(bf16)


def input_side(grads, w, block, first, blocks):
    width, wide = w.shape
    rows = grads[0].shape[0]
    tokens = blocks * block
    return pl.pallas_call(
        functools.partial(input_side_kernel, len(grads)),
        grid=(blocks,),
        in_specs=[pl.BlockSpec((rows, block), lambda i: (0, i + first)) for _ in grads]
        + [pl.BlockSpec((width, wide), lambda i: (0, 0))],
        out_specs=pl.BlockSpec((block, width), lambda i: (i, 0)),
        out_shape=jax.ShapeDtypeStruct((tokens, width), bf16),
        compiler_params=pltpu.CompilerParams(vmem_limit_bytes=56 << 20),
        cost_estimate=pl.CostEstimate(
            flops=4 * tokens * width * wide, bytes_accessed=1, transcendentals=0
        ),
        name="input_side",
    )(*grads, w)


def reduce_places(buf, places):
    place = lax.axis_index("seq")
    lines, wide = buf.shape
    bits = places.bit_length() - 1
    assert places == 1 << bits and lines % places == 0
    for b in range(bits):
        bit = (place >> b) & 1
        halves = buf.reshape(2, -1, wide)
        keep = lax.dynamic_index_in_dim(halves, bit, 0, keepdims=False)
        send = lax.dynamic_index_in_dim(halves, 1 - bit, 0, keepdims=False)
        first = yield send
        got = lax.ppermute(send, "seq", [(i, i ^ (1 << b)) for i in range(places)])
        got = after(got, first) if first is not None else got
        buf = (keep.astype(f32) + got.astype(f32)).astype(bf16)
    for b in reversed(range(bits)):
        bit = (place >> b) & 1
        yield buf
        got = lax.ppermute(buf, "seq", [(i, i ^ (1 << b)) for i in range(places)])
        buf = jnp.where(
            bit == 0, jnp.concatenate([buf, got], axis=0), jnp.concatenate([got, buf], axis=0)
        )
    yield buf


def last(steps):
    for value in steps:
        pass
    return value


def sum_everywhere(team, vector):
    vector = vector + lax.ppermute(vector, "dp", team.swap_core())
    total = vector
    for step in range(1, team.rows):
        total = total + lax.ppermute(vector, "dp", team.turn_rows(step))
    for b in range(team.seq.bit_length() - 1):
        total = total + lax.ppermute(
            total, "seq", [(i, i ^ (1 << b)) for i in range(team.seq)]
        )
    return total


def on_device(
    activations,
    segment_ids,
    norm1_gain,
    w_qkv,
    per_dim_scale,
    w_out,
    norm2_gain,
    w_up,
    b_up,
    w_down,
    b_down,
    cotangent,
):
    seqs, span, width = activations.shape
    rows_here, heads, _, head_size = w_qkv.shape
    length = segment_ids.shape[1]
    team = Team(lax.axis_size("dp"), lax.axis_size("seq"), seqs)
    size = team.size
    row, core, group, side, member = team.here()
    local_heads = heads // size
    wide = local_heads * 3 * head_size
    own = seqs * span

    def spread(array, *near):
        out = []
        for step in range(seqs):
            source = after(array, *near) if near and step < seqs // 2 else array
            block = lax.dynamic_index_in_dim(source, (group + step) % seqs, 0, keepdims=False)
            out.append(lax.ppermute(block, axes, team.spread(step)))
        return out

    def spread_done(pieces):
        return join(pieces, [jnp.int32(k) for k in range(seqs)]).reshape(own, width)

    def unspread(array):
        return [
            lax.ppermute(array[step * span : (step + 1) * span], axes, team.back(step))
            for step in range(seqs)
        ]

    def unspread_done(pieces, dtype):
        return join(pieces, [(group + step) % seqs for step in range(seqs)], dtype=dtype)

    def shard_of(step, flip):
        return (row - step) % team.rows * 2 + (core ^ flip)

    shifts = [(step, flip) for step in range(team.rows) for flip in range(2)]

    w_local = w_qkv.reshape(rows_here, heads * 3 * head_size)
    small = jnp.concatenate([norm1_gain, norm2_gain, b_up, b_down])
    small = jnp.pad(small, (0, wide * 16 - small.shape[0])).reshape(16, wide)

    def columns(first):
        part = lax.dynamic_slice_in_dim(w_local, first * wide, wide, 1)
        return jnp.concatenate([part, small], axis=0)

    parts = [columns(member), columns(member + 1 - 2 * core)]
    far = [
        lax.ppermute(parts[flip], "dp", team.turn_rows(step, flip)) for step, flip in shifts[2:]
    ]
    near = lax.ppermute(parts[1], "dp", team.swap_core())
    x_blocks = spread(after(activations, *parts), near)
    other_ids = lax.ppermute(segment_ids, "dp", team.swap_core())
    w_half, small = join(
        [parts[0], near] + far,
        [shard_of(*s) for s in shifts],
        ends=(rows_here, rows_here + 16),
    )
    w_half = w_half.reshape(width, wide)
    small = small.reshape(team.dp, -1)[:, : 4 * rows_here]
    small = small.reshape(team.dp, 4, rows_here).transpose(1, 0, 2).reshape(4, width).astype(f32)
    gain_in, gain_mid, bias_up, bias_down = (small[i : i + 1] for i in range(4))
    three = after(jnp.concatenate([w_out, w_up, w_down]), *far)
    three = [three] + [
        lax.ppermute(three, "dp", team.turn_rows(step)) for step in range(1, team.rows)
    ]
    cot_own = spread(after(cotangent, *far).astype(bf16))

    ids = lax.dynamic_index_in_dim(
        jnp.where(side == core, segment_ids, other_ids), group, 0, keepdims=False
    )
    starts = jnp.sum((ids[None, :] < ids[:, None]).astype(jnp.int32), axis=1)
    ends = jnp.sum((ids[None, :] <= ids[:, None]).astype(jnp.int32), axis=1) - 1
    count = length // span
    starts = starts.reshape(count, span)
    ends = ends.reshape(count, span)
    index = jnp.arange(count)
    z_of, u_of = index // size, index % size
    at = ((u_of - member) % size) * seqs + (group - z_of) % seqs
    first = starts[:, 0] // span
    last_start = starts[:, -1]
    open_from = jnp.minimum((last_start + span - 1) // span, index)
    open_to = jnp.sum((last_start[None, :] <= index[:, None] * span).astype(jnp.int32), axis=1)
    open_to = jnp.maximum(open_to, index + 1)
    stop = ends[:, -1] // span + 1
    table = jnp.stack([at, first, open_from, open_to, stop]).astype(jnp.int32)

    factor = scale_base / math.sqrt(head_size) * jax.nn.softplus(per_dim_scale)
    unit = jnp.ones((head_size,), f32)
    factor_row = jnp.tile(jnp.concatenate([factor * log2e, unit, unit]), local_heads)[None, :]

    x_own = spread_done(after(x_blocks, w_half, table, starts, factor_row))
    xs = [x_own] + [lax.ppermute(x_own, axes, team.rotate(-j)) for j in range(1, size)]
    qkv, normed_in = project_qkv(
        xs, gain_in, w_half, factor_row, local_heads, head_size, team.dp, span
    )
    qkv, cot_own[1::2] = after((qkv, cot_own[1::2]), *cot_own[1::2])
    att, lse = attend(table, qkv, starts)
    three = after(three, att)
    swapped = [lax.ppermute(piece, "dp", team.swap_core()) for piece in three]
    w_out_all, w_up_all, w_down_all = (
        w.reshape(-1, width)
        for w in join(
            three + swapped,
            [shard_of(step, 0) for step in range(team.rows)]
            + [shard_of(step, 1) for step in range(team.rows)],
            ends=(rows_here, 2 * rows_here, 3 * rows_here),
        )
    )

    pieces = [(att[:, :own], member)]
    for j in range(1, size):
        got = lax.ppermute(att[:, j * own : (j + 1) * own], axes, team.rotate(j))
        pieces.append((got, (member - j) % size))
    att_own = join([p for p, _ in pieces], [s for _, s in pieces])
    att_own = att_own.reshape(heads * head_size, own)

    x_float = x_own.astype(f32)
    mid = x_float + lax.dot_general(
        att_own, w_out_all, (((0,), (0,)), ((), ())), preferred_element_type=f32
    )
    rms_mid = lax.rsqrt(jnp.mean(mid * mid, axis=-1, keepdims=True) + epsilon)
    normed_mid = (mid * rms_mid * gain_mid).astype(bf16)
    pre_act = mm(normed_mid, w_up_all) + bias_up
    activated = jax.nn.silu(pre_act).astype(bf16)
    result_own = (mid + mm(activated, w_down_all) + bias_down).astype(bf16)
    result = unspread(result_own)
    cot_own = spread_done(after(cot_own, result_own))

    grad_bias_down = jnp.sum(cot_own.astype(f32), axis=0)
    tn = (((0,), (0,)), ((), ()))
    grad_act = mm(cot_own, w_down_all, nt)
    sig = jax.nn.sigmoid(pre_act)
    grad_pre = (grad_act * sig * (1.0 + pre_act * (1.0 - sig))).astype(bf16)
    grad_bias_up = jnp.sum(grad_pre.astype(f32), axis=0)
    grad_normed_mid = mm(grad_pre, w_up_all, nt)
    grad_gain_mid = jnp.sum(grad_normed_mid * mid * rms_mid, axis=0)
    scaled_mid = grad_normed_mid * gain_mid
    grad_mid = cot_own.astype(f32) + rms_mid * (
        scaled_mid - mid * rms_mid * rms_mid * jnp.mean(scaled_mid * mid, axis=-1, keepdims=True)
    )
    grad_attn = grad_mid.astype(bf16)
    grad_att = mm(w_out_all, grad_attn, nt).astype(bf16).reshape(size, -1, own)
    pieces = [(lax.dynamic_index_in_dim(grad_att, member, 0, keepdims=False), 0)]
    for j in range(1, size):
        out = lax.dynamic_index_in_dim(grad_att, (member + j) % size, 0, keepdims=False)
        pieces.append((lax.ppermute(out, axes, team.rotate(j)), (-j) % size))
    pieces.sort(key=lambda item: item[1])
    grad_heads = jnp.concatenate([piece for piece, _ in pieces], axis=1)

    def by_core(grad):
        parts = grad.astype(bf16).reshape(team.rows, 2, rows_here, width)
        keep = lax.dynamic_index_in_dim(parts, core, 1, keepdims=False)
        send = lax.dynamic_index_in_dim(parts, 1 - core, 1, keepdims=False)
        return keep, lax.ppermute(send, "dp", team.swap_core())

    three = [
        by_core(grad)
        for grad in (mm(activated, cot_own, tn), mm(normed_mid, grad_pre, tn), mm(att_own, grad_attn))
    ]

    def both_cores(step):
        at = (row + step) % team.rows
        return jnp.concatenate(
            [
                lax.dynamic_index_in_dim(keep, at, 0, keepdims=False).astype(f32)
                + lax.dynamic_index_in_dim(got, at, 0, keepdims=False).astype(f32)
                for keep, got in three
            ]
        ).astype(bf16)

    three_rows = [both_cores(step) for step in range(team.rows)]
    three_far = [
        lax.ppermute(three_rows[step], "dp", team.turn_rows(step)) for step in range(1, team.rows)
    ]

    def add(first, *more):
        total = first.astype(f32)
        for piece in more:
            total = total + piece.astype(f32)
        return total.astype(bf16)

    pair = math.gcd(local_heads, 4)
    grad_in = after(grad_heads, *three_rows)
    chunks, dots, heads_of = [], 0.0, []
    for c in range(local_heads // pair):
        grads, dot = attend_back(
            c, pair, table, qkv, att, grad_in, lse, starts, factor[:, None]
        )
        chunks.append(grads)
        dots = dots + dot
        if c == 0:
            result = after(result, grads)
            grads = after(grads, *result)
        else:
            grads = after(grads, steps.send(grads))
        send, keep = head_grad(grads, normed_in, team.rows, row, core)
        near = [lax.ppermute(piece, "dp", team.swap_core()) for piece in send]
        far = [
            [
                lax.ppermute(source, "dp", team.turn_rows(step))
                for source in (keep[step], near[step])
            ]
            for step in range(1, team.rows)
        ]
        heads_of.append((keep[0], near[0], far))
        if c == 0:
            three_far = after(three_far, *send)
            steps = reduce_places(add(three_rows[0], *three_far), team.seq)
            grad_in = after(grad_in, next(steps))
        grad_in = after(grad_in, *send, *keep)
    blocks = own // span
    chunks = after(chunks, steps.send(send), *send, *keep)
    partial = [
        input_side(chunks, w_half, span, j * blocks, blocks) for j in range(1, size)
    ]
    chunks = after(chunks, *partial)
    heads_of = after(heads_of, *partial)
    grad_normed_in = sum(
        [
            lax.ppermute(p, axes, team.rotate(j + 1)).astype(f32)
            for j, p in enumerate(partial)
        ],
        input_side(chunks, w_half, span, 0, blocks).astype(f32),
    )
    rms_in = lax.rsqrt(jnp.mean(x_float * x_float, axis=-1, keepdims=True) + epsilon)
    grad_gain_in = jnp.sum(grad_normed_in * x_float * rms_in, axis=0)
    scaled_in = grad_normed_in * gain_in
    input_grad_own = grad_mid + rms_in * (
        scaled_in
        - x_float * rms_in * rms_in * jnp.mean(scaled_in * x_float, axis=-1, keepdims=True)
    )
    input_grad = unspread_done(unspread(input_grad_own.astype(bf16)), f32)
    result = unspread_done(result, bf16)

    three = last(steps).astype(f32)
    part_out, part_up, part_down = (
        three[i * rows_here : (i + 1) * rows_here] for i in (2, 1, 0)
    )
    full = []
    for mine, theirs, far in heads_of:
        total = jnp.concatenate(
            [add(mine, *[f[0] for f in far]), add(theirs, *[f[1] for f in far])]
        )
        total = place_in([(total, member // 2)], team.half) if team.half > 1 else total
        full.append(last(reduce_places(total.reshape(-1, total.shape[-1]), team.seq)))
    full = unfold(full, team.half, rows_here, core).reshape(heads, 3, head_size, rows_here)
    vectors = sum_everywhere(
        team,
        jnp.concatenate([grad_gain_in, grad_gain_mid, grad_bias_up, grad_bias_down, dots[:, 0]]),
    )
    d = lax.axis_index("dp")

    def slice_of(i):
        return lax.dynamic_slice_in_dim(vectors, i * width + d * rows_here, rows_here, 0)

    grad_scale = vectors[4 * width :] / (factor * log2e) * (
        scale_base / math.sqrt(head_size)
    ) * jax.nn.sigmoid(per_dim_scale)
    return (
        result,
        input_grad,
        slice_of(0),
        full.transpose(3, 0, 1, 2),
        grad_scale,
        part_out,
        slice_of(1),
        part_up,
        slice_of(2),
        part_down,
        slice_of(3),
    )


def solution(mesh):
    in_specs = (
        P("dp", "seq", None),
        P("dp", None),
        P("dp"),
        P("dp", None, None, None),
        P(),
        P("dp", None),
        P("dp"),
        P("dp", None),
        P("dp"),
        P("dp", None),
        P("dp"),
        P("dp", "seq", None),
    )
    out_specs = (
        P("dp", "seq", None),
        P("dp", "seq", None),
        P("dp"),
        P("dp", None, None, None),
        P(),
        P("dp", None),
        P("dp"),
        P("dp", None),
        P("dp"),
        P("dp", None),
        P("dp"),
    )
    return jax.shard_map(
        on_device, mesh=mesh, in_specs=in_specs, out_specs=out_specs, check_vma=False
    )
```

```python
import functools
import math

import jax
import jax.numpy as jnp
from jax import lax
from jax.experimental import pallas as pl
from jax.experimental.pallas import tpu as pltpu
from jax.sharding import PartitionSpec as P

epsilon = 1e-06
scale_base = 1.442695041
log2e = 1.4426950408889634
masked_value = -1e30
score_limit = 100.0
bf16 = jnp.bfloat16
f32 = jnp.float32
axes = ("dp", "seq")
brief = pl.CostEstimate(flops=1, bytes_accessed=1, transcendentals=0)
nt = (((1,), (1,)), ((), ()))
nn = (((1,), (0,)), ((), ()))


def mm(a, b, dims=nn):
    return lax.dot_general(a, b, dims, preferred_element_type=f32)


class Team:
    def __init__(self, dp, seq, seqs):
        self.dp, self.seq, self.seqs = dp, seq, seqs
        self.size = seq // seqs
        assert seq % seqs == 0 and self.size % 2 == 0 and dp % 2 == 0
        self.half = self.size // 2
        self.rows = dp // 2

    def places(self):
        for row in range(self.rows):
            for core in range(2):
                for place in range(self.seq):
                    yield row, core, place

    def rank(self, row, core, place):
        return (row * 2 + core) * self.seq + place

    def here(self):
        d = lax.axis_index("dp")
        p = lax.axis_index("seq")
        row, core = d // 2, d % 2
        group = p // self.size
        side = (p % self.size) // self.half
        member = (p % self.half) * 2 + core
        return row, core, group, side, member

    def spread(self, step):
        pairs = []
        for row, core, place in self.places():
            z, u = place // self.size, place % self.size
            s = (z + step) % self.seqs
            pairs.append(
                (
                    self.rank(row, core, place),
                    self.rank(row, u % 2, s * self.size + core * self.half + u // 2),
                )
            )
        return pairs

    def back(self, step):
        return [(b, a) for a, b in self.spread(step)]

    def rotate(self, step):
        pairs = []
        for row, core, place in self.places():
            base = place - place % self.half
            m = (place % self.half) * 2 + core
            to = (m + step) % self.size
            pairs.append((self.rank(row, core, place), self.rank(row, to % 2, base + to // 2)))
        return pairs

    def swap_core(self):
        return [(d, d ^ 1) for d in range(self.dp)]

    def turn_rows(self, step, flip=0):
        return [(d, ((d + 2 * step) % self.dp) ^ flip) for d in range(self.dp)]


def after(value, *first):
    return lax.optimization_barrier((value, first))[0]


def place_in(pieces, count):
    first = pieces[0][0]
    out = jnp.zeros((count,) + first.shape, first.dtype)
    for piece, index in pieces:
        out = lax.dynamic_update_index_in_dim(out, piece, index, 0)
    return out


def join_kernel(count, ends, slots_ref, *refs):
    outs = refs[count:]
    for k in range(count):
        start = 0
        for out_ref, end in zip(outs, ends):
            out_ref[slots_ref[k]] = refs[k][start:end, :].astype(out_ref.dtype)
            start = end


def join(pieces, slots, ends=None, dtype=None):
    count = len(pieces)
    rows, columns = pieces[0].shape
    dtype = dtype or pieces[0].dtype
    ends = ends or (rows,)
    heights = [b - a for a, b in zip((0,) + tuple(ends[:-1]), ends)]
    wide = columns
    if columns % 128 == 0:
        wide = max(b for b in range(128, min(columns, 640) + 1, 128) if columns % b == 0)
    outs = pl.pallas_call(
        functools.partial(join_kernel, count, ends),
        grid_spec=pltpu.PrefetchScalarGridSpec(
            num_scalar_prefetch=1,
            grid=(columns // wide,),
            in_specs=[pl.BlockSpec((rows, wide), lambda i, s: (0, i)) for _ in pieces],
            out_specs=[pl.BlockSpec((count, h, wide), lambda i, s: (0, 0, i)) for h in heights],
        ),
        out_shape=[jax.ShapeDtypeStruct((count, h, columns), dtype) for h in heights],
        compiler_params=pltpu.CompilerParams(vmem_limit_bytes=56 << 20),
        cost_estimate=brief,
        name="join",
    )(jnp.stack(slots).astype(jnp.int32), *pieces)
    return outs if len(ends) > 1 else outs[0]


def qkv_kernel(count, blocks, parts, head_size, *refs):
    x_refs = refs[:count]
    gain_ref, w_ref, factor_ref, out_ref, normed_ref = refs[count:]
    i = pl.program_id(0)
    x = x_refs[0][...]
    for j in range(1, count):
        x = jnp.where(i >= j * blocks, x_refs[j][...], x)
    x = x.astype(f32)
    rms = lax.rsqrt(jnp.mean(x * x, axis=-1, keepdims=True) + epsilon)
    normed = (x * rms * gain_ref[...]).astype(bf16)
    part = x.shape[1] // parts
    for d in range(parts):
        normed_ref[d % 2, :, d // 2 * part : (d // 2 + 1) * part] = normed[
            :, d * part : (d + 1) * part
        ]
    packed = (mm(normed, w_ref[...]) * factor_ref[...]).astype(bf16)
    for h in range(packed.shape[1] // head_size):
        out_ref[h // 3, h % 3] = packed[:, h * head_size : (h + 1) * head_size]


def project_qkv(xs, gain, w, factor_row, heads, head_size, parts, block):
    own, width = xs[0].shape
    count, blocks = len(xs), own // block
    tokens = own * count
    wide = w.shape[1]

    def x_spec(j):
        return pl.BlockSpec(
            (block, width), lambda i: (jnp.clip(i - j * blocks, 0, blocks - 1), 0)
        )

    return pl.pallas_call(
        functools.partial(qkv_kernel, count, blocks, parts, head_size),
        grid=(tokens // block,),
        in_specs=[x_spec(j) for j in range(count)]
        + [
            pl.BlockSpec((1, width), lambda i: (0, 0)),
            pl.BlockSpec((width, wide), lambda i: (0, 0)),
            pl.BlockSpec((1, wide), lambda i: (0, 0)),
        ],
        out_specs=[
            pl.BlockSpec((heads, 3, block, head_size), lambda i: (0, 0, i, 0)),
            pl.BlockSpec((2, block, width // 2), lambda i: (0, i, 0)),
        ],
        out_shape=[
            jax.ShapeDtypeStruct((heads, 3, tokens, head_size), bf16),
            jax.ShapeDtypeStruct((2, tokens, width // 2), bf16),
        ],
        compiler_params=pltpu.CompilerParams(vmem_limit_bytes=56 << 20),
        cost_estimate=brief,
        name="qkv",
    )(*xs, gain, w, factor_row)


def head_grad_kernel(rows, fold, place_ref, grads_ref, normed_ref, *out_refs):
    result = mm(grads_ref[...], normed_ref[0]).astype(bf16)
    part = result.shape[1] // rows
    lines = result.shape[0] // fold
    for side in range(2):
        for row in range(rows):

            @pl.when((pl.program_id(0) == side) & (place_ref[2] == row))
            def store(side=side, row=row):
                for step in range(rows):
                    at = (row + step) % rows * part
                    for k in range(fold):
                        out_refs[side * rows + step][:, k * part : (k + 1) * part] = result[
                            k * lines : (k + 1) * lines, at : at + part
                        ]


def head_grad(grads, normed, rows, row, core):
    _, tokens, width = normed.shape
    lines = grads.shape[0]
    part = width // rows
    fold = 128 // math.gcd(part, 128)
    shape = (lines // fold, fold * part)
    outs = pl.pallas_call(
        functools.partial(head_grad_kernel, rows, fold),
        grid_spec=pltpu.PrefetchScalarGridSpec(
            num_scalar_prefetch=1,
            grid=(2,),
            in_specs=[
                pl.BlockSpec((lines, tokens), lambda i, o: (0, 0)),
                pl.BlockSpec((1, tokens, width), lambda i, o: (o[i], 0, 0)),
            ],
            out_specs=[pl.BlockSpec(shape, lambda i, o: (0, 0)) for _ in range(2 * rows)],
        ),
        out_shape=[jax.ShapeDtypeStruct(shape, bf16) for _ in range(2 * rows)],
        compiler_params=pltpu.CompilerParams(vmem_limit_bytes=56 << 20),
        cost_estimate=brief,
        name="head_grad",
    )(jnp.stack([1 - core, core, row]).astype(jnp.int32), grads, normed)
    return outs[:rows], outs[rows:]


def unfold_kernel(count, fold, core_ref, *refs):
    out_ref = refs[count]
    part = out_ref.shape[1]
    lines = out_ref.shape[0] // fold
    for c in range(count):

        @pl.when(pl.program_id(0) % count == c)
        def store(c=c):
            for k in range(fold):
                out_ref[k * lines : (k + 1) * lines, :] = refs[c][
                    :, k * part : (k + 1) * part
                ].astype(f32)


def unfold(chunks, groups, part, core):
    count = len(chunks)
    lines = chunks[0].shape[0] // (2 * groups)
    wide = chunks[0].shape[1]
    fold = wide // part

    def source(i, o):
        g = i // count
        return (g // 2 * 2 + (g % 2 + o[0]) % 2, 0)

    return pl.pallas_call(
        functools.partial(unfold_kernel, count, fold),
        grid_spec=pltpu.PrefetchScalarGridSpec(
            num_scalar_prefetch=1,
            grid=(2 * groups * count,),
            in_specs=[pl.BlockSpec((lines, wide), source) for _ in chunks],
            out_specs=pl.BlockSpec((lines * fold, part), lambda i, o: (i, 0)),
        ),
        out_shape=jax.ShapeDtypeStruct((2 * groups * count * lines * fold, part), f32),
        compiler_params=pltpu.CompilerParams(vmem_limit_bytes=56 << 20),
        cost_estimate=brief,
        name="unfold",
    )(core.reshape(1).astype(jnp.int32), *chunks)


def eye_rows(rows, columns):
    a = lax.broadcasted_iota(jnp.int32, (rows, columns), 0)
    b = lax.broadcasted_iota(jnp.int32, (rows, columns), 1)
    return (a == b).astype(bf16)


def attend_kernel(count, block, pair, table, qkv_ref, start_ref, att_ref, lse_ref, vt_ref, acc_ref):
    size = qkv_ref.shape[3]
    rows = vt_ref.shape[1]
    unit = eye_rows(rows, size)
    one_row = (lax.broadcasted_iota(jnp.int32, (rows, block), 0) == size).astype(f32)
    for h in range(pair):
        for b in range(count):
            here = slice(b * block, (b + 1) * block)
            vt_ref[h, :, here] = (mm(unit, qkv_ref[h, 2, here, :], nt) + one_row).astype(bf16)
    key_index = lax.broadcasted_iota(jnp.int32, (block, block), 0)
    lane_index = lax.broadcasted_iota(jnp.int32, (1, block), 1)
    ones = jnp.ones((8, size), bf16)

    def longest(part):
        best = jnp.zeros((8, block), f32)
        for h in range(pair):
            for b in range(count):
                x = qkv_ref[h, part, b * block : (b + 1) * block, :]
                best = jnp.maximum(best, mm(ones, x * x, nt))
        return jnp.max(best)

    small = longest(0) * longest(1) * 1.1 < score_limit * score_limit

    def query_block(raised, i, carry):
        at = pl.multiple_of(table[0, i] * block, block)
        starts = start_ref[pl.ds(i, 1), :]
        places = lane_index + i * block
        queries = [qkv_ref[h, 0, pl.ds(at, block), :] for h in range(pair)]
        acc_ref[...] = jnp.zeros_like(acc_ref)

        def step(masked, j, peaks):
            key_at = pl.multiple_of(table[0, j] * block, block)
            if masked:
                keys_here = key_index + j * block
                seen = (keys_here >= starts) & (keys_here <= places)
            scores = [
                mm(qkv_ref[h, 1, pl.ds(key_at, block), :], queries[h], nt) for h in range(pair)
            ]
            if masked:
                scores = [jnp.where(seen, s, masked_value) for s in scores]
            values = [vt_ref[h, :, pl.ds(key_at, block)] for h in range(pair)]
            if not raised:
                probs = [jnp.exp2(s).astype(bf16) for s in scores]
                sums = [mm(values[h], probs[h]) for h in range(pair)]
                for h in range(pair):
                    acc_ref[h] += sums[h]
                return ()
            out = []
            for h in range(pair):
                peak = jnp.maximum(peaks[h], jnp.max(scores[h], axis=0, keepdims=True))
                p = jnp.exp2(scores[h] - peak).astype(bf16)
                acc_ref[h] = acc_ref[h] * jnp.exp2(peaks[h] - peak) + mm(values[h], p)
                out.append(peak)
            return tuple(out)

        peaks = ()
        if raised:
            peaks = tuple(jnp.full((1, block), masked_value, f32) for _ in range(pair))
        peaks = lax.fori_loop(table[1, i], table[2, i], functools.partial(step, True), peaks)
        peaks = lax.fori_loop(table[2, i], i, functools.partial(step, False), peaks)
        peaks = step(True, i, peaks)
        for h in range(pair):
            total = acc_ref[h, size : size + 1, :]
            att_ref[h * size : (h + 1) * size, pl.ds(at, block)] = (
                acc_ref[h, :size, :] / total
            ).astype(bf16)
            low = jnp.log2(total)
            lse_ref[h, :, pl.ds(at, block)] = peaks[h] + low if raised else low
        return carry

    @pl.when(small)
    def plain():
        lax.fori_loop(0, count, functools.partial(query_block, False), 0)

    @pl.when(jnp.logical_not(small))
    def careful():
        lax.fori_loop(0, count, functools.partial(query_block, True), 0)


def attend(table, qkv, starts):
    heads, _, length, size = qkv.shape
    pair = math.gcd(heads, 8)
    count, block = starts.shape
    rows = (size // 16 + 1) * 16
    return pl.pallas_call(
        functools.partial(attend_kernel, count, block, pair),
        grid_spec=pltpu.PrefetchScalarGridSpec(
            num_scalar_prefetch=1,
            grid=(heads // pair,),
            in_specs=[
                pl.BlockSpec((pair, 3, length, size), lambda g, t: (g, 0, 0, 0)),
                pl.BlockSpec((count, block), lambda g, t: (0, 0)),
            ],
            out_specs=[
                pl.BlockSpec((pair * size, length), lambda g, t: (g, 0)),
                pl.BlockSpec((pair, 1, length), lambda g, t: (g, 0, 0)),
            ],
            scratch_shapes=[
                pltpu.VMEM((pair, rows, length), bf16),
                pltpu.VMEM((pair, rows, block), f32),
            ],
        ),
        out_shape=[
            jax.ShapeDtypeStruct((heads * size, length), bf16),
            jax.ShapeDtypeStruct((heads, 1, length), f32),
        ],
        compiler_params=pltpu.CompilerParams(vmem_limit_bytes=56 << 20),
        cost_estimate=brief,
        name="attend",
    )(table, qkv, starts)


def attend_back_kernel(
    count,
    block,
    pair,
    table,
    qkv_ref,
    att_ref,
    grad_ref,
    lse_ref,
    start_ref,
    factor_ref,
    out_ref,
    dots_ref,
    qt_ref,
    kt_ref,
    delta_ref,
    dq_ref,
    dk_ref,
    dv_ref,
):
    size = qkv_ref.shape[3]
    unit = eye_rows(size, size)
    for h in range(pair):
        for b in range(count):
            here = slice(b * block, (b + 1) * block)
            qt_ref[h, :, here] = mm(unit, qkv_ref[h, 0, here, :], nt).astype(bf16)
            kt_ref[h, :, here] = mm(unit, qkv_ref[h, 1, here, :], nt).astype(bf16)
        rows = slice(h * size, (h + 1) * size)
        delta_ref[h] = jnp.sum(
            att_ref[rows, :].astype(f32) * grad_ref[rows, :].astype(f32), axis=0, keepdims=True
        )
    dq_ref[...] = jnp.zeros_like(dq_ref)
    key_index = lax.broadcasted_iota(jnp.int32, (block, block), 0)
    lane_index = lax.broadcasted_iota(jnp.int32, (1, block), 1)

    def key_block(j, carry):
        key_at = pl.multiple_of(table[0, j] * block, block)
        keys_here = key_index + j * block
        dk_ref[...] = jnp.zeros_like(dk_ref)
        dv_ref[...] = jnp.zeros_like(dv_ref)

        def step(masked, i, inner):
            at = pl.multiple_of(table[0, i] * block, block)
            if masked:
                seen = (keys_here >= start_ref[pl.ds(i, 1), :]) & (
                    keys_here <= lane_index + i * block
                )
            both = range(pair)
            grads = [grad_ref[h * size : (h + 1) * size, pl.ds(at, block)] for h in both]
            queries = [qt_ref[h, :, pl.ds(at, block)] for h in both]
            s = [mm(qkv_ref[h, 1, pl.ds(key_at, block), :], queries[h]) for h in both]
            dp = [mm(qkv_ref[h, 2, pl.ds(key_at, block), :], grads[h]) for h in both]
            p = [jnp.exp2(s[h] - lse_ref[h, :, pl.ds(at, block)]) for h in both]
            if masked:
                p = [jnp.where(seen, x, 0.0) for x in p]
            ds = [
                (p[h] * (dp[h] - delta_ref[h, :, pl.ds(at, block)])).astype(bf16) for h in both
            ]
            dv = [mm(grads[h], p[h].astype(bf16), nt) for h in both]
            dk = [mm(queries[h], ds[h], nt) for h in both]
            dq = [mm(kt_ref[h, :, pl.ds(key_at, block)], ds[h]) for h in both]
            for h in both:
                dv_ref[h] += dv[h]
                dk_ref[h] += dk[h]
                dq_ref[h, :, pl.ds(at, block)] += dq[h]
            return inner

        step(True, j, 0)
        lax.fori_loop(j + 1, table[3, j], functools.partial(step, False), 0)
        lax.fori_loop(table[3, j], table[4, j], functools.partial(step, True), 0)
        for h in range(pair):
            base = h * 3 * size
            out_ref[base + size : base + 2 * size, pl.ds(key_at, block)] = (
                dk_ref[h] * (1.0 / log2e)
            ).astype(bf16)
            out_ref[base + 2 * size : base + 3 * size, pl.ds(key_at, block)] = dv_ref[h].astype(bf16)
        return carry

    lax.fori_loop(0, count, key_block, 0)

    @pl.when(pl.program_id(0) == 0)
    def clear():
        dots_ref[...] = jnp.zeros_like(dots_ref)

    for h in range(pair):
        base = h * 3 * size
        rounded = dq_ref[h].astype(bf16).astype(f32)
        dots_ref[...] += jnp.sum(qt_ref[h].astype(f32) * rounded, axis=1, keepdims=True)
        out_ref[base : base + size, :] = (rounded * factor_ref[...]).astype(bf16)


def attend_back(chunk, pair, table, qkv, att, grad, lse, starts, factor):
    heads, _, length, size = qkv.shape
    count, block = starts.shape
    return pl.pallas_call(
        functools.partial(attend_back_kernel, count, block, pair),
        grid_spec=pltpu.PrefetchScalarGridSpec(
            num_scalar_prefetch=1,
            grid=(1,),
            in_specs=[
                pl.BlockSpec((pair, 3, length, size), lambda g, t: (chunk, 0, 0, 0)),
                pl.BlockSpec((pair * size, length), lambda g, t: (chunk, 0)),
                pl.BlockSpec((pair * size, length), lambda g, t: (chunk, 0)),
                pl.BlockSpec((pair, 1, length), lambda g, t: (chunk, 0, 0)),
                pl.BlockSpec((count, block), lambda g, t: (0, 0)),
                pl.BlockSpec((size, 1), lambda g, t: (0, 0)),
            ],
            out_specs=[
                pl.BlockSpec((pair * 3 * size, length), lambda g, t: (0, 0)),
                pl.BlockSpec((size, 1), lambda g, t: (0, 0)),
            ],
            scratch_shapes=[
                pltpu.VMEM((pair, size, length), bf16),
                pltpu.VMEM((pair, size, length), bf16),
                pltpu.VMEM((pair, 1, length), f32),
                pltpu.VMEM((pair, size, length), f32),
                pltpu.VMEM((pair, size, block), f32),
                pltpu.VMEM((pair, size, block), f32),
            ],
        ),
        out_shape=[
            jax.ShapeDtypeStruct((pair * 3 * size, length), bf16),
            jax.ShapeDtypeStruct((size, 1), f32),
        ],
        compiler_params=pltpu.CompilerParams(vmem_limit_bytes=56 << 20),
        cost_estimate=brief,
        name="attend_back",
    )(table, qkv, att, grad, lse, starts, factor)


def input_side_kernel(count, *refs):
    w_ref, out_ref = refs[count], refs[count + 1]
    grads = jnp.concatenate([ref[...] for ref in refs[:count]], axis=0)
    out_ref[...] = mm(grads.T, w_ref[...], nt).astype(bf16)


def input_side(grads, w, block, first, blocks):
    width, wide = w.shape
    rows = grads[0].shape[0]
    tokens = blocks * block
    return pl.pallas_call(
        functools.partial(input_side_kernel, len(grads)),
        grid=(blocks,),
        in_specs=[pl.BlockSpec((rows, block), lambda i: (0, i + first)) for _ in grads]
        + [pl.BlockSpec((width, wide), lambda i: (0, 0))],
        out_specs=pl.BlockSpec((block, width), lambda i: (i, 0)),
        out_shape=jax.ShapeDtypeStruct((tokens, width), bf16),
        compiler_params=pltpu.CompilerParams(vmem_limit_bytes=56 << 20),
        cost_estimate=pl.CostEstimate(
            flops=4 * tokens * width * wide, bytes_accessed=1, transcendentals=0
        ),
        name="input_side",
    )(*grads, w)


def reduce_places(buf, places, late=()):
    place = lax.axis_index("seq")
    lines, wide = buf.shape
    bits = places.bit_length() - 1
    assert places == 1 << bits and lines % places == 0
    for b in range(bits):
        bit = (place >> b) & 1
        halves = buf.reshape(2, -1, wide)
        keep = lax.dynamic_index_in_dim(halves, bit, 0, keepdims=False)
        send = lax.dynamic_index_in_dim(halves, 1 - bit, 0, keepdims=False)
        first = yield send
        got = lax.ppermute(send, "seq", [(i, i ^ (1 << b)) for i in range(places)])
        got = after(got, first) if first is not None else got
        buf = (keep.astype(f32) + got.astype(f32)).astype(bf16)
    for b in reversed(range(bits)):
        bit = (place >> b) & 1
        if late and b == 0:
            buf = after(buf, *late)
        yield buf
        got = lax.ppermute(buf, "seq", [(i, i ^ (1 << b)) for i in range(places)])
        buf = jnp.where(
            bit == 0, jnp.concatenate([buf, got], axis=0), jnp.concatenate([got, buf], axis=0)
        )
    yield buf


def last(steps):
    for value in steps:
        pass
    return value


def sum_everywhere(team, vector):
    vector = vector + lax.ppermute(vector, "dp", team.swap_core())
    total = vector
    for step in range(1, team.rows):
        total = total + lax.ppermute(vector, "dp", team.turn_rows(step))
    for b in range(team.seq.bit_length() - 1):
        total = total + lax.ppermute(
            total, "seq", [(i, i ^ (1 << b)) for i in range(team.seq)]
        )
    return total


def on_device(
    activations,
    segment_ids,
    norm1_gain,
    w_qkv,
    per_dim_scale,
    w_out,
    norm2_gain,
    w_up,
    b_up,
    w_down,
    b_down,
    cotangent,
):
    seqs, span, width = activations.shape
    rows_here, heads, _, head_size = w_qkv.shape
    length = segment_ids.shape[1]
    team = Team(lax.axis_size("dp"), lax.axis_size("seq"), seqs)
    size = team.size
    row, core, group, side, member = team.here()
    local_heads = heads // size
    wide = local_heads * 3 * head_size
    own = seqs * span

    def spread(array, *near):
        out = []
        for step in range(seqs):
            source = after(array, *near) if near and step < seqs // 2 else array
            block = lax.dynamic_index_in_dim(source, (group + step) % seqs, 0, keepdims=False)
            out.append(lax.ppermute(block, axes, team.spread(step)))
        return out

    def spread_done(pieces):
        return join(pieces, [jnp.int32(k) for k in range(seqs)]).reshape(own, width)

    def unspread(array):
        return [
            lax.ppermute(array[step * span : (step + 1) * span], axes, team.back(step))
            for step in range(seqs)
        ]

    def unspread_done(pieces, dtype):
        return join(pieces, [(group + step) % seqs for step in range(seqs)], dtype=dtype)

    def shard_of(step, flip):
        return (row - step) % team.rows * 2 + (core ^ flip)

    shifts = [(step, flip) for step in range(team.rows) for flip in range(2)]

    w_local = w_qkv.reshape(rows_here, heads * 3 * head_size)
    small = jnp.concatenate([norm1_gain, norm2_gain, b_up, b_down])
    small = jnp.pad(small, (0, wide * 16 - small.shape[0])).reshape(16, wide)

    def columns(first):
        part = lax.dynamic_slice_in_dim(w_local, first * wide, wide, 1)
        return jnp.concatenate([part, small], axis=0)

    parts = [columns(member), columns(member + 1 - 2 * core)]
    far = [
        lax.ppermute(parts[flip], "dp", team.turn_rows(step, flip)) for step, flip in shifts[2:]
    ]
    near = lax.ppermute(parts[1], "dp", team.swap_core())
    x_blocks = spread(after(activations, *parts), near)
    other_ids = lax.ppermute(segment_ids, "dp", team.swap_core())
    w_half, small = join(
        [parts[0], near] + far,
        [shard_of(*s) for s in shifts],
        ends=(rows_here, rows_here + 16),
    )
    w_half = w_half.reshape(width, wide)
    small = small.reshape(team.dp, -1)[:, : 4 * rows_here]
    small = small.reshape(team.dp, 4, rows_here).transpose(1, 0, 2).reshape(4, width).astype(f32)
    gain_in, gain_mid, bias_up, bias_down = (small[i : i + 1] for i in range(4))
    three = after(jnp.concatenate([w_out, w_up, w_down]), *far)
    three = [three] + [
        lax.ppermute(three, "dp", team.turn_rows(step)) for step in range(1, team.rows)
    ]
    cot_own = spread(after(cotangent, *far).astype(bf16))

    ids = lax.dynamic_index_in_dim(
        jnp.where(side == core, segment_ids, other_ids), group, 0, keepdims=False
    )
    starts = jnp.sum((ids[None, :] < ids[:, None]).astype(jnp.int32), axis=1)
    ends = jnp.sum((ids[None, :] <= ids[:, None]).astype(jnp.int32), axis=1) - 1
    count = length // span
    starts = starts.reshape(count, span)
    ends = ends.reshape(count, span)
    index = jnp.arange(count)
    z_of, u_of = index // size, index % size
    at = ((u_of - member) % size) * seqs + (group - z_of) % seqs
    first = starts[:, 0] // span
    last_start = starts[:, -1]
    open_from = jnp.minimum((last_start + span - 1) // span, index)
    open_to = jnp.sum((last_start[None, :] <= index[:, None] * span).astype(jnp.int32), axis=1)
    open_to = jnp.maximum(open_to, index + 1)
    stop = ends[:, -1] // span + 1
    table = jnp.stack([at, first, open_from, open_to, stop]).astype(jnp.int32)

    factor = scale_base / math.sqrt(head_size) * jax.nn.softplus(per_dim_scale)
    unit = jnp.ones((head_size,), f32)
    factor_row = jnp.tile(jnp.concatenate([factor * log2e, unit, unit]), local_heads)[None, :]

    x_own = spread_done(after(x_blocks, w_half, table, starts, factor_row))
    xs = [x_own] + [lax.ppermute(x_own, axes, team.rotate(-j)) for j in range(1, size)]
    qkv, normed_in = project_qkv(
        xs, gain_in, w_half, factor_row, local_heads, head_size, team.dp, span
    )
    qkv, cot_own[1::2] = after((qkv, cot_own[1::2]), *cot_own[1::2])
    att, lse = attend(table, qkv, starts)
    three = after(three, att)
    swapped = [lax.ppermute(piece, "dp", team.swap_core()) for piece in three]
    w_out_all, w_up_all, w_down_all = (
        w.reshape(-1, width)
        for w in join(
            three + swapped,
            [shard_of(step, 0) for step in range(team.rows)]
            + [shard_of(step, 1) for step in range(team.rows)],
            ends=(rows_here, 2 * rows_here, 3 * rows_here),
        )
    )

    pieces = [(att[:, :own], member)]
    for j in range(1, size):
        got = lax.ppermute(att[:, j * own : (j + 1) * own], axes, team.rotate(j))
        pieces.append((got, (member - j) % size))
    att_own = join([p for p, _ in pieces], [s for _, s in pieces])
    att_own = att_own.reshape(heads * head_size, own)

    x_float = x_own.astype(f32)
    mid = x_float + lax.dot_general(
        att_own, w_out_all, (((0,), (0,)), ((), ())), preferred_element_type=f32
    )
    rms_mid = lax.rsqrt(jnp.mean(mid * mid, axis=-1, keepdims=True) + epsilon)
    normed_mid = (mid * rms_mid * gain_mid).astype(bf16)
    pre_act = mm(normed_mid, w_up_all) + bias_up
    activated = jax.nn.silu(pre_act).astype(bf16)
    result_own = (mid + mm(activated, w_down_all) + bias_down).astype(bf16)
    result = unspread(result_own)
    cot_own = spread_done(after(cot_own, result_own))

    grad_bias_down = jnp.sum(cot_own.astype(f32), axis=0)
    tn = (((0,), (0,)), ((), ()))
    grad_act = mm(cot_own, w_down_all, nt)
    sig = jax.nn.sigmoid(pre_act)
    grad_pre = (grad_act * sig * (1.0 + pre_act * (1.0 - sig))).astype(bf16)
    grad_bias_up = jnp.sum(grad_pre.astype(f32), axis=0)
    grad_normed_mid = mm(grad_pre, w_up_all, nt)
    grad_gain_mid = jnp.sum(grad_normed_mid * mid * rms_mid, axis=0)
    scaled_mid = grad_normed_mid * gain_mid
    grad_mid = cot_own.astype(f32) + rms_mid * (
        scaled_mid - mid * rms_mid * rms_mid * jnp.mean(scaled_mid * mid, axis=-1, keepdims=True)
    )
    grad_attn = grad_mid.astype(bf16)
    grad_att = mm(w_out_all, grad_attn, nt).astype(bf16).reshape(size, -1, own)
    pieces = [(lax.dynamic_index_in_dim(grad_att, member, 0, keepdims=False), 0)]
    for j in range(1, size):
        out = lax.dynamic_index_in_dim(grad_att, (member + j) % size, 0, keepdims=False)
        pieces.append((lax.ppermute(out, axes, team.rotate(j)), (-j) % size))
    pieces.sort(key=lambda item: item[1])
    grad_heads = jnp.concatenate([piece for piece, _ in pieces], axis=1)

    def by_core(grad):
        parts = grad.astype(bf16).reshape(team.rows, 2, rows_here, width)
        keep = lax.dynamic_index_in_dim(parts, core, 1, keepdims=False)
        send = lax.dynamic_index_in_dim(parts, 1 - core, 1, keepdims=False)
        return keep, lax.ppermute(send, "dp", team.swap_core())

    three = [
        by_core(grad)
        for grad in (mm(activated, cot_own, tn), mm(normed_mid, grad_pre, tn), mm(att_own, grad_attn))
    ]

    def both_cores(step):
        at = (row + step) % team.rows
        return jnp.concatenate(
            [
                lax.dynamic_index_in_dim(keep, at, 0, keepdims=False).astype(f32)
                + lax.dynamic_index_in_dim(got, at, 0, keepdims=False).astype(f32)
                for keep, got in three
            ]
        ).astype(bf16)

    three_rows = [both_cores(step) for step in range(team.rows)]
    three_far = [
        lax.ppermute(three_rows[step], "dp", team.turn_rows(step)) for step in range(1, team.rows)
    ]

    def add(first, *more):
        total = first.astype(f32)
        for piece in more:
            total = total + piece.astype(f32)
        return total.astype(bf16)

    pair = math.gcd(local_heads, 4)
    grad_in = after(grad_heads, *three_rows)
    chunks, dots, heads_of = [], 0.0, []
    for c in range(local_heads // pair):
        grads, dot = attend_back(
            c, pair, table, qkv, att, grad_in, lse, starts, factor[:, None]
        )
        chunks.append(grads)
        dots = dots + dot
        if c == 0:
            result = after(result, grads)
            grads = after(grads, *result)
        else:
            grads = after(grads, steps.send(grads))
        send, keep = head_grad(grads, normed_in, team.rows, row, core)
        near = [lax.ppermute(piece, "dp", team.swap_core()) for piece in send]
        far = [
            [
                lax.ppermute(source, "dp", team.turn_rows(step))
                for source in (keep[step], near[step])
            ]
            for step in range(1, team.rows)
        ]
        heads_of.append((keep[0], near[0], far))
        if c == 0:
            three_far = after(three_far, *send)
            steps = reduce_places(add(three_rows[0], *three_far), team.seq)
            grad_in = after(grad_in, next(steps))
        grad_in = after(grad_in, *send, *keep)
    blocks = own // span
    chunks = after(chunks, steps.send(send), *send, *keep)
    partial = [
        input_side(chunks, w_half, span, j * blocks, blocks) for j in range(1, size)
    ]
    chunks = after(chunks, *partial)
    heads_of = after(heads_of, *partial)
    grad_normed_in = sum(
        [
            lax.ppermute(p, axes, team.rotate(j + 1)).astype(f32)
            for j, p in enumerate(partial)
        ],
        input_side(chunks, w_half, span, 0, blocks).astype(f32),
    )
    rms_in = lax.rsqrt(jnp.mean(x_float * x_float, axis=-1, keepdims=True) + epsilon)
    grad_gain_in = jnp.sum(grad_normed_in * x_float * rms_in, axis=0)
    scaled_in = grad_normed_in * gain_in
    input_grad_own = grad_mid + rms_in * (
        scaled_in
        - x_float * rms_in * rms_in * jnp.mean(scaled_in * x_float, axis=-1, keepdims=True)
    )
    input_grad_own = input_grad_own.astype(bf16)
    input_grad = unspread_done(unspread(input_grad_own), f32)
    result = unspread_done(result, bf16)

    three = last(steps).astype(f32)
    part_out, part_up, part_down = (
        three[i * rows_here : (i + 1) * rows_here] for i in (2, 1, 0)
    )
    full = []
    for mine, theirs, far in heads_of:
        total = jnp.concatenate(
            [add(mine, *[f[0] for f in far]), add(theirs, *[f[1] for f in far])]
        )
        total = place_in([(total, member // 2)], team.half) if team.half > 1 else total
        full.append(last(reduce_places(total.reshape(-1, total.shape[-1]), team.seq, (input_grad_own,))))
    full = unfold(full, team.half, rows_here, core).reshape(heads, 3, head_size, rows_here)
    vectors = sum_everywhere(
        team,
        jnp.concatenate([grad_gain_in, grad_gain_mid, grad_bias_up, grad_bias_down, dots[:, 0]]),
    )
    d = lax.axis_index("dp")

    def slice_of(i):
        return lax.dynamic_slice_in_dim(vectors, i * width + d * rows_here, rows_here, 0)

    grad_scale = vectors[4 * width :] / (factor * log2e) * (
        scale_base / math.sqrt(head_size)
    ) * jax.nn.sigmoid(per_dim_scale)
    return (
        result,
        input_grad,
        slice_of(0),
        full.transpose(3, 0, 1, 2),
        grad_scale,
        part_out,
        slice_of(1),
        part_up,
        slice_of(2),
        part_down,
        slice_of(3),
    )


def solution(mesh):
    in_specs = (
        P("dp", "seq", None),
        P("dp", None),
        P("dp"),
        P("dp", None, None, None),
        P(),
        P("dp", None),
        P("dp"),
        P("dp", None),
        P("dp"),
        P("dp", None),
        P("dp"),
        P("dp", "seq", None),
    )
    out_specs = (
        P("dp", "seq", None),
        P("dp", "seq", None),
        P("dp"),
        P("dp", None, None, None),
        P(),
        P("dp", None),
        P("dp"),
        P("dp", None),
        P("dp"),
        P("dp", None),
        P("dp"),
    )
    return jax.shard_map(
        on_device, mesh=mesh, in_specs=in_specs, out_specs=out_specs, check_vma=False
    )
```
